256 devices in a mesh: sec: 4 (over z_lo), row: 8 (over y, core), rad: 8 (over z_hi, x).
Axes of the slice: x: 4, y: 4, z: 8 (z_hi: 2, z_lo: 4; z = z_hi * 4 + z_lo), core: 2. Of those that a mesh axis runs over, the one named last changes fastest.
Arguments:
- state: float32 [5, 4, 16, 64, 1024], P(None, 'sec', None, 'rad', 'row'), may hold values from -6 to 6
- volume: float32 [4, 16, 64, 1024], P('sec', None, 'rad', 'row'), may hold values from 0.5 to 2
- face_axial: float32 [4, 16, 64, 1024], P('sec', None, 'rad', 'row'), may hold values from 0.5 to 1.5
- face_radial: float32 [4, 16, 64, 1024], P('sec', None, 'rad', 'row'), may hold values from 0.5 to 1.5
- face_circum: float32 [4, 16, 64, 1024], P('sec', None, 'rad', 'row'), may hold values from 0.5 to 1.5
- viscosity: float32 [4, 16, 64, 1024], P('sec', None, 'rad', 'row'), may hold values from 0.05 to 0.5
- flux_matrix: float32 [4, 3, 5, 5], P('sec'), may hold values from -2.5 to 2.5
- inflow_plane: float32 [5, 64, 1024], P(None, 'rad', 'row'), may hold values from -6 to 6
- outflow_plane: float32 [5, 64, 1024], P(None, 'rad', 'row'), may hold values from -6 to 6
- down_donors: int32 [4, 512], P('sec', ('row', 'rad')), may hold values from 0 to 511, each once within a row
- up_donors: int32 [4, 512], P('sec', ('row', 'rad')), may hold values from 0 to 511, each once within a row
- pressure_weight: float32 [5], replicated, may hold values from -3 to 3
- boundary_coupling: float32 [5], replicated, may hold values from -4 to 4
Outputs:
- advanced: float32 [5, 4, 16, 64, 1024], P(None, 'sec', None, 'rad', 'row')
The draws below stay inside these ranges and needn't reach their ends.
Inputs may be any that keep to these rules, and one draw needn't show every extreme that they name: `down_donors`: each row names each of the 512 tiles exactly once. `up_donors`: each row names each of the 512 tiles exactly once.
All inputs are finite; a program needn't handle non-finite values.
Results may differ from the reference program's by a relative error of at most 0.0001.
Values sent between devices are 32-bit elements; how exact they have to be, the bound alone decides.
No kernel may reach another device: no remote copies, remote signals or barrier semaphores. Data moves between devices by JAX's collectives and lax.ppermute only.
A program may use at most 64 MiB of HBM per device.

```python
import math
import jax
import jax.numpy as jnp
from jax import lax

NV = 5
STEPS = 4
CX = 16
CR = 8
CC = 128
NT = 512
NR = 64
NC = 1024
N_SEC = 4
N_ROW = 8
N_RAD = 8


def level_of(stream_key, shape, shards, low, high):
    loudness, own = 1.0, jax.random.fold_in(stream_key, 6)
    for dim, blocks in shards:
        steps = jnp.exp(jax.random.uniform(jax.random.fold_in(own, dim), (blocks,), jnp.float32, low / len(shards), high / len(shards)))
        loudness = loudness * jnp.repeat(steps, shape[dim] // blocks).reshape([-1 if axis == dim else 1 for axis in range(len(shape))])
    return loudness


def bell_draw(rng, dims, deviation, reach, split=(), kind=jnp.bfloat16):
    array = deviation * jax.random.normal(rng, dims, jnp.float32)
    if split:
        array = array * level_of(rng, dims, split, -0.22, 0.18)
    return jnp.clip(array, -reach, reach).astype(kind)


def setup_inputs(seed: int = 0) -> dict:
    key_list = jax.random.split(jax.random.key(seed), 14)
    return {
        "state": bell_draw(key_list[0], (NV, N_SEC, CX, NR, NC), 1.0, 6.0, ((1, 4), (3, 8), (4, 8)), jnp.float32),
        "volume": jnp.clip(jnp.exp(math.log(2.0) - 1.3862944 * jax.random.uniform(key_list[1], (N_SEC, CX, NR, NC), jnp.float32) ** level_of(key_list[1], (N_SEC, CX, NR, NC), ((0, 4), (2, 8), (3, 8)), -0.2, 0.2)), 0.5, 2.0),
        "face_axial": jnp.clip(jnp.exp(math.log(1.5) - 1.0986123 * jax.random.uniform(key_list[2], (N_SEC, CX, NR, NC), jnp.float32) ** level_of(key_list[2], (N_SEC, CX, NR, NC), ((0, 4), (2, 8), (3, 8)), -0.2, 0.2)), 0.5, 1.5),
        "face_radial": jnp.clip(jnp.exp(math.log(1.5) - 1.0986123 * jax.random.uniform(key_list[3], (N_SEC, CX, NR, NC), jnp.float32) ** level_of(key_list[3], (N_SEC, CX, NR, NC), ((0, 4), (2, 8), (3, 8)), -0.2, 0.2)), 0.5, 1.5),
        "face_circum": jnp.clip(jnp.exp(math.log(1.5) - 1.0986123 * jax.random.uniform(key_list[4], (N_SEC, CX, NR, NC), jnp.float32) ** level_of(key_list[4], (N_SEC, CX, NR, NC), ((0, 4), (2, 8), (3, 8)), -0.2, 0.2)), 0.5, 1.5),
        "viscosity": jnp.clip(jnp.exp(math.log(0.5) - 2.3025851 * jax.random.uniform(key_list[5], (N_SEC, CX, NR, NC), jnp.float32) ** level_of(key_list[5], (N_SEC, CX, NR, NC), ((0, 4), (2, 8), (3, 8)), -0.2, 0.2)), 0.05, 0.5),
        "flux_matrix": bell_draw(key_list[6], (N_SEC, 3, NV, NV), NV ** -0.5, 2.5, ((0, 4),), jnp.float32),
        "inflow_plane": bell_draw(key_list[7], (NV, NR, NC), 1.0, 6.0, ((1, 8), (2, 8)), jnp.float32),
        "outflow_plane": bell_draw(key_list[8], (NV, NR, NC), 1.0, 6.0, ((1, 8), (2, 8)), jnp.float32),
        "down_donors": jax.vmap(lambda own: jax.random.permutation(own, NT))(jax.random.split(key_list[9], N_SEC)).reshape((N_SEC, NT)).astype(jnp.int32),
        "up_donors": jax.vmap(lambda own: jax.random.permutation(own, NT))(jax.random.split(key_list[10], N_SEC)).reshape((N_SEC, NT)).astype(jnp.int32),
        "pressure_weight": bell_draw(key_list[11], (NV,), 0.5, 3.0, (), jnp.float32),
        "boundary_coupling": bell_draw(key_list[12], (NV,), 1.0, 4.0, (), jnp.float32),
    }


time_step = 0.08


def to_tiles(plane):
    components = plane.shape[0]
    shaped = plane.reshape(components, N_RAD, CR, N_ROW, CC // 128, 128)
    return shaped.transpose(3, 1, 2, 4, 0, 5).reshape(NT, components, 128)


def from_tiles(tiles):
    components = tiles.shape[1]
    shaped = tiles.reshape(N_ROW, N_RAD, CR, CC // 128, components, 128)
    return shaped.transpose(4, 1, 2, 0, 3, 5).reshape(components, NR, NC)


def face_divergence(padded, face_area, viscous, matrix, direction):
    length = padded.shape[direction]
    lower_cells = lax.slice_in_dim(padded, 0, length - 1, axis=direction)
    upper_cells = lax.slice_in_dim(padded, 1, length, axis=direction)
    mixed = jnp.einsum("uv,v...->u...", matrix, lower_cells + upper_cells, precision=lax.Precision.HIGHEST)
    fluxes = face_area * (0.5 * mixed - viscous * (upper_cells - lower_cells))
    return lax.slice_in_dim(fluxes, 1, length - 1, axis=direction) - lax.slice_in_dim(fluxes, 0, length - 2, axis=direction)


def pressure_of(weights, plane):
    return jnp.einsum("v,vjk->jk", weights, plane, precision=lax.Precision.HIGHEST)


def reference(state, volume, face_axial, face_radial, face_circum, viscosity, flux_matrix, inflow_plane, outflow_plane, down_donors, up_donors, pressure_weight, boundary_coupling):
    sections = [state[:, section_id] for section_id in range(N_SEC)]
    for step_index in range(STEPS):
        fresh = []
        for section_id in range(N_SEC):
            field = sections[section_id]
            if section_id == 0:
                donor = inflow_plane
            else:
                donor = sections[section_id - 1][:, -1]
            if section_id == N_SEC - 1:
                beyond = outflow_plane
            else:
                beyond = sections[section_id + 1][:, 0]
            inlet_ghost = from_tiles(jnp.take(to_tiles(donor), down_donors[section_id], axis=0))
            beyond_pressure = pressure_of(pressure_weight, beyond)[None]
            mapped = from_tiles(jnp.take(to_tiles(beyond_pressure), up_donors[section_id], axis=0))[0]
            outlet = field[:, -1]
            outlet_ghost = outlet + boundary_coupling[:, None, None] * (mapped - pressure_of(pressure_weight, outlet))[None]
            axial_padded = jnp.concatenate([inlet_ghost[:, None], field, outlet_ghost[:, None]], axis=1)
            own_face = face_axial[section_id]
            axial_area = jnp.concatenate([own_face[:1], own_face], axis=0)
            own_mu = viscosity[section_id]
            mu_axial = jnp.concatenate([own_mu[:1], own_mu, own_mu[-1:]], axis=0)
            nu_axial = 0.5 * (mu_axial[:-1] + mu_axial[1:])
            radial_face = face_radial[section_id]
            radial_face = jnp.concatenate([radial_face[:, :-1], jnp.zeros_like(radial_face[:, -1:])], axis=1)
            radial_area = jnp.concatenate([radial_face[:, -1:], radial_face], axis=1)
            mu_radial = jnp.pad(own_mu, ((0, 0), (1, 1), (0, 0)), mode="wrap")
            nu_radial = 0.5 * (mu_radial[:, :-1] + mu_radial[:, 1:])
            radial_padded = jnp.pad(field, ((0, 0), (0, 0), (1, 1), (0, 0)), mode="wrap")
            circ_face = face_circum[section_id]
            circ_area = jnp.concatenate([circ_face[:, :, -1:], circ_face], axis=2)
            mu_circ = jnp.pad(own_mu, ((0, 0), (0, 0), (1, 1)), mode="wrap")
            nu_circ = 0.5 * (mu_circ[:, :, :-1] + mu_circ[:, :, 1:])
            circ_padded = jnp.pad(field, ((0, 0), (0, 0), (0, 0), (1, 1)), mode="wrap")
            divergence = face_divergence(axial_padded, axial_area, nu_axial, flux_matrix[section_id, 0], 1)
            divergence = divergence + face_divergence(radial_padded, radial_area, nu_radial, flux_matrix[section_id, 1], 2)
            divergence = divergence + face_divergence(circ_padded, circ_area, nu_circ, flux_matrix[section_id, 2], 3)
            fresh.append(field - (time_step / volume[section_id]) * divergence)
        sections = fresh
    return jnp.stack(sections, axis=1)
```

```python
import functools

import jax
import jax.numpy as jnp
from jax import lax
from jax.experimental import pallas as pl
from jax.experimental.pallas import tpu as pltpu
from jax.sharding import PartitionSpec as P

STEPS = 4
time_step = 0.08
INTERPRET = False

NV = 5
TILE_ROWS = 48
FIELD_ROWS = 80
COEF_ROWS = 32
EDGE_ROWS = 8


def vmem():
    return pl.BlockSpec(memory_space=pltpu.VMEM)


def smem():
    return pl.BlockSpec(memory_space=pltpu.SMEM)


def call(kernel, outs, args, specs, name, flops=0, scratch=()):
    moved = sum(a.size * 4 for a in args) + sum(4 * functools.reduce(lambda x, y: x * y, o) for o in outs)
    return pl.pallas_call(
        kernel,
        out_shape=[jax.ShapeDtypeStruct(o, jnp.float32) for o in outs],
        in_specs=specs,
        out_specs=[vmem() for _ in outs],
        scratch_shapes=list(scratch),
        name=name,
        cost_estimate=pl.CostEstimate(flops=flops, bytes_accessed=moved, transcendentals=0),
        interpret=INTERPRET,
    )(*args)


def lanes_of(shape):
    return lax.broadcasted_iota(jnp.int32, shape, 1)


def rows_of(shape):
    return lax.broadcasted_iota(jnp.int32, shape, 0)


def roll(x, by, axis):
    size = x.shape[axis]
    if not isinstance(by, int):
        return pltpu.roll(x, lax.rem(by + 2 * size, size), axis)
    by %= size
    return x if by == 0 else pltpu.roll(x, by, axis)


def pressure(weight_ref, values):
    total = weight_ref[0] * values[0]
    for v in range(1, NV):
        total = total + weight_ref[v] * values[v]
    return total


def first_kernel(ids, weight, state, outflow, radial, circ, mu, halo, edges, down, up, out_pressure):
    planes = state.shape[1]
    lanes = lanes_of((8, 128))
    rows = rows_of((8, 128))
    casing = ids[2] == ids[3] - 1

    def one(k, carry):
        last, first = carry
        for v in range(NV):
            cell = state[v, k]
            at = v * 16 + k
            halo[0, pl.ds(at, 1), :] = cell[7:8]
            halo[1, pl.ds(at, 1), :] = cell[0:1]
            here = lanes == at
            last = jnp.where(here, roll(cell, at + 1, 1), last)
            first = jnp.where(here, roll(cell, at, 1), first)
        m, c = mu[k], circ[k]
        face = jnp.where(jnp.logical_and(casing, rows == 7), 0.0, radial[k])
        halo[0, pl.ds(80 + k, 1), :] = m[7:8]
        halo[1, pl.ds(80 + k, 1), :] = m[0:1]
        halo[0, pl.ds(96 + k, 1), :] = face[7:8]
        halo[1, pl.ds(96 + k, 1), :] = face[0:1]
        here = lanes == 80 + k
        last = jnp.where(here, roll(m, 81 + k, 1), last)
        first = jnp.where(here, roll(m, 80 + k, 1), first)
        here = lanes == 96 + k
        last = jnp.where(here, roll(c, 97 + k, 1), last)
        return last, first

    zero = jnp.zeros((8, 128), jnp.float32)
    last, first = lax.fori_loop(0, planes, one, (zero, zero))
    edges[0] = last
    edges[1] = first
    for v in range(NV):
        down[v] = state[v, planes - 1]
    up[...] = pressure(weight, [state[v, 0] for v in range(NV)])
    out_pressure[...] = pressure(weight, [outflow[v] for v in range(NV)])


def gather_kernel(ids, down, up, inflow, out_pressure, halo, send):
    section, rad = ids[0], ids[2]
    size = send.shape[0]
    halo_rows = halo.shape[1]
    for v in range(NV):
        value = jnp.where(section == 0, inflow[v], down[v])
        for j in range(size):
            send[j, v * 8 : v * 8 + 8, :] = value
    value = jnp.where(section == ids[4] - 1, out_pressure[...], up[...])
    for j in range(size):
        send[j, 40:48, :] = value

    @pl.when(rad < size - 1)
    def _():
        send[jnp.minimum(rad + 1, size - 1), 48 : 48 + halo_rows, :] = halo[0]

    @pl.when(rad > 0)
    def _():
        send[jnp.maximum(rad - 1, 0), 48 : 48 + halo_rows, :] = halo[1]


def select_kernel(ids, wanted, got, edges, send):
    size = send.shape[0]
    row = ids[1]

    def one(j, carry):
        for a in range(8):
            d = wanted[j, a] & 63
            r, b = d >> 3, d & 7
            for v in range(NV):
                send[j, v * 8 + a : v * 8 + a + 1, :] = got[r, pl.ds(v * 8 + b, 1), :]
            e = wanted[j, 8 + a] & 63
            send[j, 40 + a : 41 + a, :] = got[e >> 3, pl.ds(40 + (e & 7), 1), :]
        return carry

    lax.fori_loop(0, size, one, 0)
    send[lax.rem(row + 1, size), 48:56, :] = edges[0]
    send[lax.rem(row + size - 1, size), 48:56, :] = edges[1]


def coef_kernel(ids, volume, axial, radial, circ, mu, got, across, coef):
    row, rad = ids[1], ids[2]
    row_size, rad_size = ids[5], ids[3]
    planes = volume.shape[0]
    lanes = lanes_of((8, 128))
    rows = rows_of((8, 128))
    below, above = jnp.maximum(rad - 1, 0), jnp.minimum(rad + 1, rad_size - 1)
    left = across[lax.rem(row + row_size - 1, row_size), 48:56, :]
    right = across[lax.rem(row + 1, row_size), 48:56, :]

    def one(k, carry):
        m = mu[k]
        c = time_step / volume[k]
        half = 0.5 * c

        def put(at, area, viscous):
            coef[at, k] = half * area
            coef[at + 1, k] = c * area * viscous

        put(0, axial[jnp.maximum(k - 1, 0)], 0.5 * (m + mu[jnp.maximum(k - 1, 0)]))
        put(2, axial[k], 0.5 * (m + mu[jnp.minimum(k + 1, planes - 1)]))
        face = jnp.where(jnp.logical_and(rad == rad_size - 1, rows == 7), 0.0, radial[k])
        mu_below = jnp.where(rad == 0, m, jnp.broadcast_to(got[below, pl.ds(128 + k, 1), :], (8, 128)))
        mu_above = jnp.where(rad == rad_size - 1, m, jnp.broadcast_to(got[above, pl.ds(128 + k, 1), :], (8, 128)))
        face_below = jnp.where(rad == 0, 0.0, jnp.broadcast_to(got[below, pl.ds(144 + k, 1), :], (8, 128)))
        put(4, jnp.where(rows == 0, face_below, roll(face, 1, 0)), 0.5 * (m + jnp.where(rows == 0, mu_below, roll(m, 1, 0))))
        put(6, face, 0.5 * (m + jnp.where(rows == 7, mu_above, roll(m, 7, 0))))
        around = circ[k]
        at = 80 + k
        mu_left = jnp.where(lanes == 0, roll(left, -at, 1), roll(m, 1, 1))
        mu_right = jnp.where(lanes == 127, roll(right, 127 - at, 1), roll(m, 127, 1))
        circ_left = jnp.where(lanes == 0, roll(left, -(at + 16), 1), roll(around, 1, 1))
        put(8, circ_left, 0.5 * (mu_left + m))
        put(10, around, 0.5 * (m + mu_right))
        return carry

    lax.fori_loop(0, planes, one, 0)


def update_kernel(last_step, ids, donors, weight, coupling, state, coef, matrix, got, across, *outs):
    if last_step:
        new, ghost = outs
    else:
        new, halo, edges, down, up, ghost = outs
    row, rad = ids[1], ids[2]
    row_size, rad_size = ids[5], ids[3]
    planes = state.shape[1]
    lanes = lanes_of((8, 128))
    rows = rows_of((8, 128))
    below, above = jnp.maximum(rad - 1, 0), jnp.minimum(rad + 1, rad_size - 1)
    wall_below, wall_above = rad == 0, rad == rad_size - 1
    left = across[lax.rem(row + row_size - 1, row_size), 48:56, :]
    right = across[lax.rem(row + 1, row_size), 48:56, :]
    for a in range(8):
        d = donors[a] >> 6
        for v in range(NV):
            ghost[v, a : a + 1, :] = across[d, v * 8 + a : v * 8 + a + 1, :]
        e = donors[8 + a] >> 6
        ghost[NV, a : a + 1, :] = across[e, 40 + a : 41 + a, :]
    outlet = [state[v, planes - 1] for v in range(NV)]
    jump = ghost[NV] - pressure(weight, outlet)
    outlet_ghost = [outlet[v] + coupling[v] * jump for v in range(NV)]

    def one(k, carry, after=None):
        before, here, last, first = carry
        if after is None:
            after = [state[v, k + 1] for v in range(NV)]
        total = list(here)
        for d in range(3):
            low_a, low_b = coef[4 * d, k], coef[4 * d + 1, k]
            high_a, high_b = coef[4 * d + 2, k], coef[4 * d + 3, k]
            mixed = []
            for v in range(NV):
                cell = here[v]
                at = v * 16 + k
                if d == 0:
                    lower, upper = before[v], after[v]
                elif d == 1:
                    low = jnp.broadcast_to(got[below, pl.ds(48 + at, 1), :], (8, 128))
                    high = jnp.broadcast_to(got[above, pl.ds(48 + at, 1), :], (8, 128))
                    low = jnp.where(wall_below, cell, low)
                    high = jnp.where(wall_above, cell, high)
                    lower = jnp.where(rows == 0, low, roll(cell, 1, 0))
                    upper = jnp.where(rows == 7, high, roll(cell, 7, 0))
                else:
                    lower = jnp.where(lanes == 0, roll(left, -at, 1), roll(cell, 1, 1))
                    upper = jnp.where(lanes == 127, roll(right, 127 - at, 1), roll(cell, 127, 1))
                mixed.append(high_a * (cell + upper) - low_a * (lower + cell))
                total[v] = total[v] + (high_b * (upper - cell) - low_b * (cell - lower))
            for u in range(NV):
                flow = matrix[25 * d + 5 * u] * mixed[0]
                for v in range(1, NV):
                    flow = flow + matrix[25 * d + 5 * u + v] * mixed[v]
                total[u] = total[u] - flow
        for v in range(NV):
            new[v, k] = total[v]
            if not last_step:
                at = v * 16 + k
                halo[0, pl.ds(at, 1), :] = total[v][7:8]
                halo[1, pl.ds(at, 1), :] = total[v][0:1]
                spot = lanes == at
                last = jnp.where(spot, roll(total[v], at + 1, 1), last)
                first = jnp.where(spot, roll(total[v], at, 1), first)
        return here, after, last, first

    zero = jnp.zeros((8, 128), jnp.float32)
    carry = ([ghost[v] for v in range(NV)], [state[v, 0] for v in range(NV)], zero, zero)
    carry = lax.fori_loop(0, planes - 1, one, carry)
    _, _, last, first = one(planes - 1, carry, outlet_ghost)
    if not last_step:
        edges[0] = last
        edges[1] = first
        for v in range(NV):
            down[v] = new[v, planes - 1]
        up[...] = pressure(weight, [new[v, 0] for v in range(NV)])


def body(
    state,
    volume,
    face_axial,
    face_radial,
    face_circum,
    viscosity,
    flux_matrix,
    inflow_plane,
    outflow_plane,
    down_donors,
    up_donors,
    pressure_weight,
    boundary_coupling,
):
    sections, row_size, rad_size = lax.axis_size("sec"), lax.axis_size("row"), lax.axis_size("rad")
    ids = jnp.stack(
        [
            lax.axis_index("sec"),
            lax.axis_index("row"),
            lax.axis_index("rad"),
            jnp.int32(rad_size),
            jnp.int32(sections),
            jnp.int32(row_size),
        ]
    ).astype(jnp.int32)
    field = state[:, 0]
    planes = field.shape[1]
    volume, axial, radial, circ, mu = volume[0], face_axial[0], face_radial[0], face_circum[0], viscosity[0]
    donors = jnp.concatenate([down_donors[0], up_donors[0]])
    mine = jnp.broadcast_to(jnp.pad(donors, (0, 112))[None, None], (row_size, 8, 128))
    wanted = lax.all_to_all(mine, "row", 0, 0)[:, 0, :16]
    matrix = jnp.broadcast_to(flux_matrix[0].reshape(75)[:, None, None], (75, 8, 128))
    plane = (NV, 8, 128)
    strips = (2, 8, 128)

    halo, edges, down, up, out_pressure = call(
        first_kernel,
        [(2, FIELD_ROWS + COEF_ROWS, 128), strips, plane, (8, 128), (8, 128)],
        [ids, pressure_weight, field, outflow_plane, radial, circ, mu],
        [smem(), smem()] + [vmem()] * 5,
        "first",
    )
    forward = [(i, i + 1) for i in range(sections - 1)]
    backward = [(i + 1, i) for i in range(sections - 1)]
    coef = None
    for step in range(STEPS):
        last_step = step == STEPS - 1
        down = lax.ppermute(down, "sec", forward)
        up = lax.ppermute(up, "sec", backward)
        (send,) = call(
            gather_kernel,
            [(rad_size, TILE_ROWS + halo.shape[1], 128)],
            [ids, down, up, inflow_plane, out_pressure, halo],
            [smem()] + [vmem()] * 5,
            "gather",
        )
        got = lax.all_to_all(send, "rad", 0, 0)
        (send,) = call(
            select_kernel,
            [(row_size, TILE_ROWS + EDGE_ROWS, 128)],
            [ids, wanted, got, edges],
            [smem(), smem()] + [vmem()] * 2,
            "select",
        )
        across = lax.all_to_all(send, "row", 0, 0)
        if step == 0:
            (coef,) = call(
                coef_kernel,
                [(12, planes, 8, 128)],
                [ids, volume, axial, radial, circ, mu, got, across],
                [smem()] + [vmem()] * 7,
                "coef",
            )
        outs = [(NV, planes, 8, 128)]
        if not last_step:
            outs += [(2, FIELD_ROWS, 128), strips, plane, (8, 128)]
        result = call(
            functools.partial(update_kernel, last_step),
            outs,
            [ids, donors, pressure_weight, boundary_coupling, field, coef, matrix, got, across],
            [smem()] * 4 + [vmem()] * 5,
            "update_last" if last_step else "update",
            flops=planes * 1024 * 350,
            scratch=[pltpu.VMEM((NV + 1, 8, 128), jnp.float32)],
        )
        field = result[0]
        if not last_step:
            halo, edges, down, up = result[1:]
    return field[:, None]


def solution(mesh):
    in_specs = (
        P(None, "sec", None, "rad", "row"),
        P("sec", None, "rad", "row"),
        P("sec", None, "rad", "row"),
        P("sec", None, "rad", "row"),
        P("sec", None, "rad", "row"),
        P("sec", None, "rad", "row"),
        P("sec", None, None, None),
        P(None, "rad", "row"),
        P(None, "rad", "row"),
        P("sec", ("row", "rad")),
        P("sec", ("row", "rad")),
        P(),
        P(),
    )
    out_specs = P(None, "sec", None, "rad", "row")
    return jax.shard_map(body, mesh=mesh, in_specs=in_specs, out_specs=out_specs, check_vma=False)
```

```python
import functools

import jax
import jax.numpy as jnp
from jax import lax
from jax.experimental import pallas as pl
from jax.experimental.pallas import tpu as pltpu
from jax.sharding import PartitionSpec as P

STEPS = 4
time_step = 0.08
INTERPRET = False
VMEM_LIMIT = 6 * 1024 * 1024

NV = 5
TILE_ROWS = 48
FIELD_ROWS = 80
COEF_ROWS = 32
EDGE_ROWS = 8


def vmem():
    return pl.BlockSpec(memory_space=pltpu.VMEM)


def smem():
    return pl.BlockSpec(memory_space=pltpu.SMEM)


def call(kernel, outs, args, specs, name, flops=0, scratch=()):
    moved = sum(a.size * 4 for a in args) + sum(4 * functools.reduce(lambda x, y: x * y, o) for o in outs)
    return pl.pallas_call(
        kernel,
        out_shape=[jax.ShapeDtypeStruct(o, jnp.float32) for o in outs],
        in_specs=specs,
        out_specs=[vmem() for _ in outs],
        scratch_shapes=list(scratch),
        name=name,
        compiler_params=pltpu.CompilerParams(vmem_limit_bytes=VMEM_LIMIT),
        cost_estimate=pl.CostEstimate(flops=flops, bytes_accessed=moved, transcendentals=0),
        interpret=INTERPRET,
    )(*args)


def lanes_of(shape):
    return lax.broadcasted_iota(jnp.int32, shape, 1)


def rows_of(shape):
    return lax.broadcasted_iota(jnp.int32, shape, 0)


def roll(x, by, axis):
    size = x.shape[axis]
    if not isinstance(by, int):
        return pltpu.roll(x, lax.rem(by + 2 * size, size), axis)
    by %= size
    return x if by == 0 else pltpu.roll(x, by, axis)


def pressure(weight_ref, values):
    total = weight_ref[0] * values[0]
    for v in range(1, NV):
        total = total + weight_ref[v] * values[v]
    return total


def first_kernel(ids, weight, state, outflow, radial, circ, mu, halo, edges, down, up, out_pressure):
    planes = state.shape[1]
    lanes = lanes_of((8, 128))
    rows = rows_of((8, 128))
    casing = ids[2] == ids[3] - 1

    def one(k, carry):
        last, first = carry
        for v in range(NV):
            cell = state[v, k]
            at = v * 16 + k
            halo[0, pl.ds(at, 1), :] = cell[7:8]
            halo[1, pl.ds(at, 1), :] = cell[0:1]
            here = lanes == at
            last = jnp.where(here, roll(cell, at + 1, 1), last)
            first = jnp.where(here, roll(cell, at, 1), first)
        m, c = mu[k], circ[k]
        face = jnp.where(jnp.logical_and(casing, rows == 7), 0.0, radial[k])
        halo[0, pl.ds(80 + k, 1), :] = m[7:8]
        halo[1, pl.ds(80 + k, 1), :] = m[0:1]
        halo[0, pl.ds(96 + k, 1), :] = face[7:8]
        halo[1, pl.ds(96 + k, 1), :] = face[0:1]
        here = lanes == 80 + k
        last = jnp.where(here, roll(m, 81 + k, 1), last)
        first = jnp.where(here, roll(m, 80 + k, 1), first)
        here = lanes == 96 + k
        last = jnp.where(here, roll(c, 97 + k, 1), last)
        return last, first

    zero = jnp.zeros((8, 128), jnp.float32)
    last, first = lax.fori_loop(0, planes, one, (zero, zero))
    edges[0] = last
    edges[1] = first
    for v in range(NV):
        down[v] = state[v, planes - 1]
    up[...] = pressure(weight, [state[v, 0] for v in range(NV)])
    out_pressure[...] = pressure(weight, [outflow[v] for v in range(NV)])


def gather_kernel(ids, down, up, inflow, out_pressure, halo, send):
    section, rad = ids[0], ids[2]
    size = send.shape[0]
    halo_rows = halo.shape[1]
    for v in range(NV):
        value = jnp.where(section == 0, inflow[v], down[v])
        for j in range(size):
            send[j, v * 8 : v * 8 + 8, :] = value
    value = jnp.where(section == ids[4] - 1, out_pressure[...], up[...])
    for j in range(size):
        send[j, 40:48, :] = value

    @pl.when(rad < size - 1)
    def _():
        send[jnp.minimum(rad + 1, size - 1), 48 : 48 + halo_rows, :] = halo[0]

    @pl.when(rad > 0)
    def _():
        send[jnp.maximum(rad - 1, 0), 48 : 48 + halo_rows, :] = halo[1]


def select_kernel(ids, wanted, got, edges, send):
    size = send.shape[0]
    row = ids[1]

    def one(j, carry):
        for a in range(8):
            d = wanted[j, a] & 63
            r, b = d >> 3, d & 7
            for v in range(NV):
                send[j, v * 8 + a : v * 8 + a + 1, :] = got[r, pl.ds(v * 8 + b, 1), :]
            e = wanted[j, 8 + a] & 63
            send[j, 40 + a : 41 + a, :] = got[e >> 3, pl.ds(40 + (e & 7), 1), :]
        return carry

    lax.fori_loop(0, size, one, 0)
    send[lax.rem(row + 1, size), 48:56, :] = edges[0]
    send[lax.rem(row + size - 1, size), 48:56, :] = edges[1]


def coef_kernel(ids, volume, axial, radial, circ, mu, got, across, coef):
    row, rad = ids[1], ids[2]
    row_size, rad_size = ids[5], ids[3]
    planes = volume.shape[0]
    lanes = lanes_of((8, 128))
    rows = rows_of((8, 128))
    below, above = jnp.maximum(rad - 1, 0), jnp.minimum(rad + 1, rad_size - 1)
    left = across[lax.rem(row + row_size - 1, row_size), 48:56, :]
    right = across[lax.rem(row + 1, row_size), 48:56, :]

    def one(k, carry):
        m = mu[k]
        c = time_step / volume[k]
        half = 0.5 * c

        def put(at, area, viscous):
            coef[at, k] = half * area
            coef[at + 1, k] = c * area * viscous

        put(0, axial[jnp.maximum(k - 1, 0)], 0.5 * (m + mu[jnp.maximum(k - 1, 0)]))
        put(2, axial[k], 0.5 * (m + mu[jnp.minimum(k + 1, planes - 1)]))
        face = jnp.where(jnp.logical_and(rad == rad_size - 1, rows == 7), 0.0, radial[k])
        mu_below = jnp.where(rad == 0, m, jnp.broadcast_to(got[below, pl.ds(128 + k, 1), :], (8, 128)))
        mu_above = jnp.where(rad == rad_size - 1, m, jnp.broadcast_to(got[above, pl.ds(128 + k, 1), :], (8, 128)))
        face_below = jnp.where(rad == 0, 0.0, jnp.broadcast_to(got[below, pl.ds(144 + k, 1), :], (8, 128)))
        put(4, jnp.where(rows == 0, face_below, roll(face, 1, 0)), 0.5 * (m + jnp.where(rows == 0, mu_below, roll(m, 1, 0))))
        put(6, face, 0.5 * (m + jnp.where(rows == 7, mu_above, roll(m, 7, 0))))
        around = circ[k]
        at = 80 + k
        mu_left = jnp.where(lanes == 0, roll(left, -at, 1), roll(m, 1, 1))
        mu_right = jnp.where(lanes == 127, roll(right, 127 - at, 1), roll(m, 127, 1))
        circ_left = jnp.where(lanes == 0, roll(left, -(at + 16), 1), roll(around, 1, 1))
        put(8, circ_left, 0.5 * (mu_left + m))
        put(10, around, 0.5 * (m + mu_right))
        return carry

    lax.fori_loop(0, planes, one, 0)


def update_kernel(last_step, ids, donors, weight, coupling, state, coef, matrix, got, across, *outs):
    if last_step:
        new, ghost = outs
    else:
        new, halo, edges, down, up, ghost = outs
    row, rad = ids[1], ids[2]
    row_size, rad_size = ids[5], ids[3]
    planes = state.shape[1]
    lanes = lanes_of((8, 128))
    rows = rows_of((8, 128))
    below, above = jnp.maximum(rad - 1, 0), jnp.minimum(rad + 1, rad_size - 1)
    wall_below, wall_above = rad == 0, rad == rad_size - 1
    left = across[lax.rem(row + row_size - 1, row_size), 48:56, :]
    right = across[lax.rem(row + 1, row_size), 48:56, :]
    for a in range(8):
        d = donors[a] >> 6
        for v in range(NV):
            ghost[v, a : a + 1, :] = across[d, v * 8 + a : v * 8 + a + 1, :]
        e = donors[8 + a] >> 6
        ghost[NV, a : a + 1, :] = across[e, 40 + a : 41 + a, :]
    outlet = [state[v, planes - 1] for v in range(NV)]
    jump = ghost[NV] - pressure(weight, outlet)
    outlet_ghost = [outlet[v] + coupling[v] * jump for v in range(NV)]

    def one(k, carry, after=None):
        before, here, last, first = carry
        if after is None:
            after = [state[v, k + 1] for v in range(NV)]
        total = list(here)
        for d in range(3):
            low_a, low_b = coef[4 * d, k], coef[4 * d + 1, k]
            high_a, high_b = coef[4 * d + 2, k], coef[4 * d + 3, k]
            mixed = []
            for v in range(NV):
                cell = here[v]
                at = v * 16 + k
                if d == 0:
                    lower, upper = before[v], after[v]
                elif d == 1:
                    low = jnp.broadcast_to(got[below, pl.ds(48 + at, 1), :], (8, 128))
                    high = jnp.broadcast_to(got[above, pl.ds(48 + at, 1), :], (8, 128))
                    low = jnp.where(wall_below, cell, low)
                    high = jnp.where(wall_above, cell, high)
                    lower = jnp.where(rows == 0, low, roll(cell, 1, 0))
                    upper = jnp.where(rows == 7, high, roll(cell, 7, 0))
                else:
                    lower = jnp.where(lanes == 0, roll(left, -at, 1), roll(cell, 1, 1))
                    upper = jnp.where(lanes == 127, roll(right, 127 - at, 1), roll(cell, 127, 1))
                mixed.append(high_a * (cell + upper) - low_a * (lower + cell))
                total[v] = total[v] + (high_b * (upper - cell) - low_b * (cell - lower))
            for u in range(NV):
                flow = matrix[25 * d + 5 * u] * mixed[0]
                for v in range(1, NV):
                    flow = flow + matrix[25 * d + 5 * u + v] * mixed[v]
                total[u] = total[u] - flow
        for v in range(NV):
            new[v, k] = total[v]
            if not last_step:
                at = v * 16 + k
                halo[0, pl.ds(at, 1), :] = total[v][7:8]
                halo[1, pl.ds(at, 1), :] = total[v][0:1]
                spot = lanes == at
                last = jnp.where(spot, roll(total[v], at + 1, 1), last)
                first = jnp.where(spot, roll(total[v], at, 1), first)
        return here, after, last, first

    zero = jnp.zeros((8, 128), jnp.float32)
    carry = ([ghost[v] for v in range(NV)], [state[v, 0] for v in range(NV)], zero, zero)
    carry = lax.fori_loop(0, planes - 1, one, carry)
    _, _, last, first = one(planes - 1, carry, outlet_ghost)
    if not last_step:
        edges[0] = last
        edges[1] = first
        for v in range(NV):
            down[v] = new[v, planes - 1]
        up[...] = pressure(weight, [new[v, 0] for v in range(NV)])


def body(
    state,
    volume,
    face_axial,
    face_radial,
    face_circum,
    viscosity,
    flux_matrix,
    inflow_plane,
    outflow_plane,
    down_donors,
    up_donors,
    pressure_weight,
    boundary_coupling,
):
    sections, row_size, rad_size = lax.axis_size("sec"), lax.axis_size("row"), lax.axis_size("rad")
    ids = jnp.stack(
        [
            lax.axis_index("sec"),
            lax.axis_index("row"),
            lax.axis_index("rad"),
            jnp.int32(rad_size),
            jnp.int32(sections),
            jnp.int32(row_size),
        ]
    ).astype(jnp.int32)
    field = state[:, 0]
    planes = field.shape[1]
    volume, axial, radial, circ, mu = volume[0], face_axial[0], face_radial[0], face_circum[0], viscosity[0]
    donors = jnp.concatenate([down_donors[0], up_donors[0]])
    mine = jnp.broadcast_to(jnp.pad(donors, (0, 112))[None, None], (row_size, 8, 128))
    wanted = lax.all_to_all(mine, "row", 0, 0)[:, 0, :16]
    matrix = jnp.broadcast_to(flux_matrix[0].reshape(75)[:, None, None], (75, 8, 128))
    plane = (NV, 8, 128)
    strips = (2, 8, 128)

    halo, edges, down, up, out_pressure = call(
        first_kernel,
        [(2, FIELD_ROWS + COEF_ROWS, 128), strips, plane, (8, 128), (8, 128)],
        [ids, pressure_weight, field, outflow_plane, radial, circ, mu],
        [smem(), smem()] + [vmem()] * 5,
        "first",
    )
    forward = [(i, i + 1) for i in range(sections - 1)]
    backward = [(i + 1, i) for i in range(sections - 1)]
    coef = None
    for step in range(STEPS):
        last_step = step == STEPS - 1
        down = lax.ppermute(down, "sec", forward)
        up = lax.ppermute(up, "sec", backward)
        (send,) = call(
            gather_kernel,
            [(rad_size, TILE_ROWS + halo.shape[1], 128)],
            [ids, down, up, inflow_plane, out_pressure, halo],
            [smem()] + [vmem()] * 5,
            "gather",
        )
        got = lax.all_to_all(send, "rad", 0, 0)
        (send,) = call(
            select_kernel,
            [(row_size, TILE_ROWS + EDGE_ROWS, 128)],
            [ids, wanted, got, edges],
            [smem(), smem()] + [vmem()] * 2,
            "select",
        )
        across = lax.all_to_all(send, "row", 0, 0)
        if step == 0:
            (coef,) = call(
                coef_kernel,
                [(12, planes, 8, 128)],
                [ids, volume, axial, radial, circ, mu, got, across],
                [smem()] + [vmem()] * 7,
                "coef",
            )
        outs = [(NV, planes, 8, 128)]
        if not last_step:
            outs += [(2, FIELD_ROWS, 128), strips, plane, (8, 128)]
        result = call(
            functools.partial(update_kernel, last_step),
            outs,
            [ids, donors, pressure_weight, boundary_coupling, field, coef, matrix, got, across],
            [smem()] * 4 + [vmem()] * 5,
            "update_last" if last_step else "update",
            flops=planes * 1024 * 350,
            scratch=[pltpu.VMEM((NV + 1, 8, 128), jnp.float32)],
        )
        field = result[0]
        if not last_step:
            halo, edges, down, up = result[1:]
    return field[:, None]


def solution(mesh):
    in_specs = (
        P(None, "sec", None, "rad", "row"),
        P("sec", None, "rad", "row"),
        P("sec", None, "rad", "row"),
        P("sec", None, "rad", "row"),
        P("sec", None, "rad", "row"),
        P("sec", None, "rad", "row"),
        P("sec", None, None, None),
        P(None, "rad", "row"),
        P(None, "rad", "row"),
        P("sec", ("row", "rad")),
        P("sec", ("row", "rad")),
        P(),
        P(),
    )
    out_specs = P(None, "sec", None, "rad", "row")
    return jax.shard_map(body, mesh=mesh, in_specs=in_specs, out_specs=out_specs, check_vma=False)
```

```python
import functools

import jax
import jax.numpy as jnp
from jax import lax
from jax.experimental import pallas as pl
from jax.experimental.pallas import tpu as pltpu
from jax.sharding import PartitionSpec as P

STEPS = 4
time_step = 0.08
INTERPRET = False
VMEM_LIMIT = 8 * 1024 * 1024

NV = 5
WIDE = 4
ROWS = 16
PLANES = 16
TILE_ROWS = 48


def vmem():
    return pl.BlockSpec(memory_space=pltpu.VMEM)


def smem():
    return pl.BlockSpec(memory_space=pltpu.SMEM)


def call(kernel, outs, scalars, arrays, name, flops=0, scratch=()):
    moved = sum(a.size * 4 for a in arrays) + sum(4 * functools.reduce(lambda x, y: x * y, o) for o in outs)
    return pl.pallas_call(
        kernel,
        out_shape=[jax.ShapeDtypeStruct(o, jnp.float32) for o in outs],
        in_specs=[smem() for _ in scalars] + [vmem() for _ in arrays],
        out_specs=[vmem() for _ in outs],
        scratch_shapes=list(scratch),
        name=name,
        compiler_params=pltpu.CompilerParams(vmem_limit_bytes=VMEM_LIMIT),
        cost_estimate=pl.CostEstimate(flops=flops, bytes_accessed=moved, transcendentals=0),
        interpret=INTERPRET,
    )(*scalars, *arrays)


def lanes_of(shape):
    return lax.broadcasted_iota(jnp.int32, shape, 1)


def rows_of(shape):
    return lax.broadcasted_iota(jnp.int32, shape, 0)


def roll(x, by, axis):
    size = x.shape[axis]
    if not isinstance(by, int):
        return pltpu.roll(x, lax.rem(by + 2 * size, size), axis)
    by %= size
    return x if by == 0 else pltpu.roll(x, by, axis)


def pressure(weight_ref, values):
    total = weight_ref[0] * values[0]
    for v in range(1, NV):
        total = total + weight_ref[v] * values[v]
    return total


def picked(step):
    count = 2 * (WIDE - 1 - step) + 8
    return range(step + 1, step + 1 + count), -(-6 * count // 8) * 8


def first_kernel(weight, state, volume, axial, radial, circ, mu, outflow, to_above, to_below, down, up, out_pressure):
    def put(at, half, cell):
        to_above[at, half : half + 4, :] = cell[4:8]
        to_below[at, half : half + 4, :] = cell[0:4]

    def one(k, carry):
        for half in (0, 1):
            plane = 2 * k + half
            for v in range(NV):
                put(v * 8 + k, 4 * half, state[v, plane])
            for at, array in enumerate((volume, axial, radial, circ, mu)):
                put((NV + at) * 8 + k, 4 * half, array[plane])
        return carry

    for v in range(NV):
        down[v] = state[v, PLANES - 1]
    up[...] = pressure(weight, [state[v, 0] for v in range(NV)])
    out_pressure[...] = pressure(weight, [outflow[v] for v in range(NV)])
    lax.fori_loop(0, PLANES // 2, one, 0)


def gather_kernel(first_step, ids, down, up, inflow, out_pressure, *refs):
    if first_step:
        donors, send = refs
    else:
        (send,) = refs
    section = ids[0]
    size = send.shape[0]
    for v in range(NV):
        value = jnp.where(section == 0, inflow[v], down[v])
        for j in range(size):
            send[j, v * 8 : v * 8 + 8, :] = value
    value = jnp.where(section == ids[4] - 1, out_pressure[...], up[...])
    for j in range(size):
        send[j, 40:48, :] = value
        if first_step:
            send[j, 48:56, :] = donors[...]


def wanted_kernel(ids, got, send, mine):
    rad, rad_size = ids[2], ids[3]
    lanes = lanes_of((8, 128))
    below = got[jnp.maximum(rad - 1, 0), 48:56, :]
    above = got[jnp.minimum(rad + 1, rad_size - 1), 48:56, :]
    own = got[rad, 48:56, :]
    down = jnp.where(lanes < 4, roll(below, -4, 1), jnp.where(lanes < 12, roll(own, 4, 1), roll(above, 12, 1)))
    up = jnp.where(lanes < 20, roll(below, 4, 1), jnp.where(lanes < 28, roll(own, 12, 1), roll(above, 20, 1)))
    both = jnp.where(lanes < 16, down, up)
    mine[...] = both
    for j in range(send.shape[0]):
        send[j] = both


def extend_kernel(state, volume, axial, radial, circ, mu, from_below, from_above, field, raw, edges):
    lanes = lanes_of((ROWS, 128))

    def one(k, carry):
        last, first = carry
        for half in (0, 1):
            plane = 2 * k + half
            rows = slice(4 * half, 4 * half + 4)

            def put(at, target, index, cell):
                target[index, plane, 0:4, :] = from_below[at, rows, :]
                target[index, plane, 4:12, :] = cell
                target[index, plane, 12:16, :] = from_above[at, rows, :]
                return target[index, plane]

            for v in range(NV):
                cell = put(v * 8 + k, field, v, state[v, plane])
                at = v * 16 + plane
                last = jnp.where(lanes == at, roll(cell, at + 1, 1), last)
                first = jnp.where(lanes == at, roll(cell, at, 1), first)
            for at, array in enumerate((volume, axial, radial, circ, mu)):
                cell = put((NV + at) * 8 + k, raw, at, array[plane])
                if at == 3:
                    last = jnp.where(lanes == 96 + plane, roll(cell, 97 + plane, 1), last)
                if at == 4:
                    last = jnp.where(lanes == 80 + plane, roll(cell, 81 + plane, 1), last)
                    first = jnp.where(lanes == 80 + plane, roll(cell, 80 + plane, 1), first)
        return last, first

    zero = jnp.zeros((ROWS, 128), jnp.float32)
    last, first = lax.fori_loop(0, PLANES // 2, one, (zero, zero))
    edges[0] = last
    edges[1] = first


def select_kernel(step, ids, wanted, got, edges, send):
    size = send.shape[0]
    row = ids[1]
    rows, base = picked(step)
    count = len(rows)

    def one(j, carry):
        for n, i in enumerate(rows):
            d = wanted[j, i] & 63
            r, b = d >> 3, d & 7
            for v in range(NV):
                send[j, v * count + n : v * count + n + 1, :] = got[r, pl.ds(v * 8 + b, 1), :]
            e = wanted[j, 16 + i] & 63
            send[j, NV * count + n : NV * count + n + 1, :] = got[e >> 3, pl.ds(40 + (e & 7), 1), :]
        return carry

    lax.fori_loop(0, size, one, 0)
    send[lax.rem(row + 1, size), base : base + ROWS, :] = edges[0]
    send[lax.rem(row + size - 1, size), base : base + ROWS, :] = edges[1]


def sides(ids, across, base):
    row, row_size = ids[1], ids[5]
    left = across[lax.rem(row + row_size - 1, row_size), base : base + ROWS, :]
    right = across[lax.rem(row + 1, row_size), base : base + ROWS, :]
    return left, right


def coef_kernel(ids, raw, across, coef):
    rad, rad_size = ids[2], ids[3]
    lanes = lanes_of((ROWS, 128))
    rows = rows_of((ROWS, 128))
    outside = jnp.logical_or(
        jnp.logical_and(rad == 0, rows < WIDE), jnp.logical_and(rad == rad_size - 1, rows >= WIDE + 8)
    )
    casing = jnp.logical_and(rad == rad_size - 1, rows >= WIDE + 7)
    left, right = sides(ids, across, picked(0)[1])

    def one(k, carry):
        m = raw[4, k]
        c = jnp.where(outside, 0.0, time_step / jnp.where(outside, 1.0, raw[0, k]))
        half = 0.5 * c
        diffused = []

        def put(at, area, viscous):
            coef[at, k] = half * area
            b = c * area * viscous
            coef[at + 1, k] = b
            diffused.append(b)

        lower, upper = jnp.maximum(k - 1, 0), jnp.minimum(k + 1, PLANES - 1)
        put(0, raw[1, lower], 0.5 * (m + raw[4, lower]))
        put(2, raw[1, k], 0.5 * (m + raw[4, upper]))
        face = jnp.where(casing, 0.0, raw[2, k])
        put(4, roll(face, 1, 0), 0.5 * (m + roll(m, 1, 0)))
        put(6, face, 0.5 * (m + roll(m, ROWS - 1, 0)))
        around = raw[3, k]
        at = 80 + k
        mu_left = jnp.where(lanes == 0, roll(left, -at, 1), roll(m, 1, 1))
        mu_right = jnp.where(lanes == 127, roll(right, 127 - at, 1), roll(m, 127, 1))
        circ_left = jnp.where(lanes == 0, roll(left, -(at + 16), 1), roll(around, 1, 1))
        put(8, circ_left, 0.5 * (mu_left + m))
        put(10, around, 0.5 * (m + mu_right))
        total = diffused[0]
        for b in diffused[1:]:
            total = total + b
        coef[12, k] = 1.0 - total
        return carry

    lax.fori_loop(0, PLANES, one, 0)


def advance(k, before, here, after, coef, matrix, left, right, lanes):
    rest = coef[12, k]
    total = [rest * here[v] for v in range(NV)]
    for d in range(3):
        low_a, low_b = coef[4 * d, k], coef[4 * d + 1, k]
        high_a, high_b = coef[4 * d + 2, k], coef[4 * d + 3, k]
        own_a = high_a - low_a
        mixed = []
        for v in range(NV):
            cell = here[v]
            if d == 0:
                lower, upper = before[v], after[v]
            elif d == 1:
                lower, upper = roll(cell, 1, 0), roll(cell, ROWS - 1, 0)
            else:
                at = v * 16 + k
                lower = jnp.where(lanes == 0, roll(left, -at, 1), roll(cell, 1, 1))
                upper = jnp.where(lanes == 127, roll(right, 127 - at, 1), roll(cell, 127, 1))
            mixed.append(high_a * upper - low_a * lower + own_a * cell)
            total[v] = total[v] + (high_b * upper + low_b * lower)
        for u in range(NV):
            for v in range(NV):
                at = 25 * d + 5 * u + v
                total[u] = total[u] - jnp.broadcast_to(matrix[at : at + 1, :], (ROWS, 128)) * mixed[v]
    return total


def ghosts_of(step, donors, weight, coupling, field, across, ghost):
    rows, _ = picked(step)
    count = len(rows)
    ghost[...] = jnp.zeros(ghost.shape, jnp.float32)
    for n, i in enumerate(rows):
        d = donors[i] >> 6
        for v in range(NV):
            ghost[v, i : i + 1, :] = across[d, v * count + n : v * count + n + 1, :]
        e = donors[16 + i] >> 6
        ghost[NV, i : i + 1, :] = across[e, NV * count + n : NV * count + n + 1, :]
    outlet = [field[v, PLANES - 1] for v in range(NV)]
    jump = ghost[NV] - pressure(weight, outlet)
    return [ghost[v] for v in range(NV)], [outlet[v] + coupling[v] * jump for v in range(NV)]


def ends_of(step, ids, donors, weight, coupling, field, coef, matrix, across, ghost):
    lanes = lanes_of((ROWS, 128))
    left, right = sides(ids, across, picked(step)[1])
    inlet_ghost, outlet_ghost = ghosts_of(step, donors, weight, coupling, field, across, ghost)
    plane = lambda k: [field[v, k] for v in range(NV)]
    new_inlet = advance(0, inlet_ghost, plane(0), plane(1), coef, matrix, left, right, lanes)
    last = PLANES - 1
    new_outlet = advance(last, plane(last - 1), plane(last), outlet_ghost, coef, matrix, left, right, lanes)
    return new_inlet, new_outlet


def ends_kernel(step, ids, donors, weight, coupling, field, coef, matrix, across, ends, down, up, ghost):
    new_inlet, new_outlet = ends_of(step, ids, donors, weight, coupling, field, coef, matrix, across, ghost)
    for v in range(NV):
        ends[0, v] = new_inlet[v]
        ends[1, v] = new_outlet[v]
        down[v] = new_outlet[v][WIDE : WIDE + 8]
    up[...] = pressure(weight, new_inlet)[WIDE : WIDE + 8]


def bulk_kernel(step, ids, field, coef, matrix, across, ends, new, edges):
    lanes = lanes_of((ROWS, 128))
    left, right = sides(ids, across, picked(step)[1])

    def note(k, total, last, first):
        for v in range(NV):
            new[v, k] = total[v]
            at = v * 16 + k
            spot = lanes == at
            last = jnp.where(spot, roll(total[v], at + 1, 1), last)
            first = jnp.where(spot, roll(total[v], at, 1), first)
        return last, first

    def one(k, carry):
        before, here, last, first = carry
        after = [field[v, k + 1] for v in range(NV)]
        total = advance(k, before, here, after, coef, matrix, left, right, lanes)
        last, first = note(k, total, last, first)
        return here, after, last, first

    zero = jnp.zeros((ROWS, 128), jnp.float32)
    last, first = note(0, [ends[0, v] for v in range(NV)], zero, zero)
    last, first = note(PLANES - 1, [ends[1, v] for v in range(NV)], last, first)
    carry = ([field[v, 0] for v in range(NV)], [field[v, 1] for v in range(NV)], last, first)
    _, _, last, first = lax.fori_loop(1, PLANES - 1, one, carry)
    edges[0] = last
    edges[1] = first


def last_kernel(step, ids, donors, weight, coupling, field, coef, matrix, across, new, ghost):
    lanes = lanes_of((ROWS, 128))
    left, right = sides(ids, across, picked(step)[1])
    new_inlet, new_outlet = ends_of(step, ids, donors, weight, coupling, field, coef, matrix, across, ghost)
    for v in range(NV):
        new[v, 0] = new_inlet[v][WIDE : WIDE + 8]
        new[v, PLANES - 1] = new_outlet[v][WIDE : WIDE + 8]

    def one(k, carry):
        before, here = carry
        after = [field[v, k + 1] for v in range(NV)]
        total = advance(k, before, here, after, coef, matrix, left, right, lanes)
        for v in range(NV):
            new[v, k] = total[v][WIDE : WIDE + 8]
        return here, after

    carry = ([field[v, 0] for v in range(NV)], [field[v, 1] for v in range(NV)])
    lax.fori_loop(1, PLANES - 1, one, carry)


def body(
    state,
    volume,
    face_axial,
    face_radial,
    face_circum,
    viscosity,
    flux_matrix,
    inflow_plane,
    outflow_plane,
    down_donors,
    up_donors,
    pressure_weight,
    boundary_coupling,
):
    sections, row_size, rad_size = lax.axis_size("sec"), lax.axis_size("row"), lax.axis_size("rad")
    ids = jnp.stack(
        [
            lax.axis_index("sec"),
            lax.axis_index("row"),
            lax.axis_index("rad"),
            jnp.int32(rad_size),
            jnp.int32(sections),
            jnp.int32(row_size),
        ]
    ).astype(jnp.int32)
    own = [state[:, 0], volume[0], face_axial[0], face_radial[0], face_circum[0], viscosity[0]]
    donors = jnp.concatenate([down_donors[0], up_donors[0]]).astype(jnp.float32)
    donors = jnp.broadcast_to(jnp.pad(donors, (0, 112))[None], (8, 128))
    matrix = jnp.broadcast_to(jnp.pad(flux_matrix[0].reshape(75), (0, 5))[:, None], (80, 128))
    extended = (NV, PLANES, ROWS, 128)
    strips = (2, ROWS, 128)
    sent = (2 * NV * PLANES // 2, 8, 128)
    scalars = [pressure_weight, boundary_coupling]

    to_above, to_below, down, up, out_pressure = call(
        first_kernel,
        [sent, sent, (NV, 8, 128), (8, 128), (8, 128)],
        [pressure_weight],
        own + [outflow_plane],
        "first",
    )
    forward = [(i, i + 1) for i in range(sections - 1)]
    backward = [(i + 1, i) for i in range(sections - 1)]
    outward = [(i, i + 1) for i in range(rad_size - 1)]
    inward = [(i + 1, i) for i in range(rad_size - 1)]
    field = coef = edges = wanted = mine = None
    for step in range(STEPS):
        last_step = step == STEPS - 1
        rows, base = picked(step)
        down = lax.ppermute(down, "sec", forward)
        up = lax.ppermute(up, "sec", backward)
        if step == 0:
            from_below = lax.ppermute(to_above, "rad", outward)
            from_above = lax.ppermute(to_below, "rad", inward)
        (send,) = call(
            functools.partial(gather_kernel, step == 0),
            [(rad_size, TILE_ROWS + (8 if step == 0 else 0), 128)],
            [ids],
            [down, up, inflow_plane, out_pressure] + ([donors] if step == 0 else []),
            "gather",
        )
        got = lax.all_to_all(send, "rad", 0, 0)
        if step == 0:
            lists, mine = call(wanted_kernel, [(row_size, 8, 128), (8, 128)], [ids], [got], "wanted")
            wanted = lax.all_to_all(lists, "row", 0, 0)[:, 0, :32].astype(jnp.int32)
            mine = mine[0, :32].astype(jnp.int32)
            field, raw, edges = call(
                extend_kernel, [extended, extended, strips], [], own + [from_below, from_above], "extend"
            )
        (send,) = call(
            functools.partial(select_kernel, step),
            [(row_size, base + ROWS, 128)],
            [ids, wanted],
            [got, edges],
            "select",
        )
        across = lax.all_to_all(send, "row", 0, 0)
        if step == 0:
            (coef,) = call(coef_kernel, [(13, PLANES, ROWS, 128)], [ids], [raw, across], "coef")
        ghost = [pltpu.VMEM((NV + 1, ROWS, 128), jnp.float32)]
        if last_step:
            (field,) = call(
                functools.partial(last_kernel, step),
                [(NV, PLANES, 8, 128)],
                [ids, mine] + scalars,
                [field, coef, matrix, across],
                "last",
                flops=PLANES * ROWS * 128 * 300,
                scratch=ghost,
            )
        else:
            ends, down, up = call(
                functools.partial(ends_kernel, step),
                [(2, NV, ROWS, 128), (NV, 8, 128), (8, 128)],
                [ids, mine] + scalars,
                [field, coef, matrix, across],
                "ends",
                flops=2 * ROWS * 128 * 300,
                scratch=ghost,
            )
            field, edges = call(
                functools.partial(bulk_kernel, step),
                [extended, strips],
                [ids],
                [field, coef, matrix, across, ends],
                "bulk",
                flops=PLANES * ROWS * 128 * 300,
            )
    return field[:, None]


def solution(mesh):
    in_specs = (
        P(None, "sec", None, "rad", "row"),
        P("sec", None, "rad", "row"),
        P("sec", None, "rad", "row"),
        P("sec", None, "rad", "row"),
        P("sec", None, "rad", "row"),
        P("sec", None, "rad", "row"),
        P("sec", None, None, None),
        P(None, "rad", "row"),
        P(None, "rad", "row"),
        P("sec", ("row", "rad")),
        P("sec", ("row", "rad")),
        P(),
        P(),
    )
    out_specs = P(None, "sec", None, "rad", "row")
    return jax.shard_map(body, mesh=mesh, in_specs=in_specs, out_specs=out_specs, check_vma=False)
```

```python
import functools

import jax
import jax.numpy as jnp
from jax import lax
from jax.experimental import pallas as pl
from jax.experimental.pallas import tpu as pltpu
from jax.sharding import PartitionSpec as P


STEPS = 4
time_step = 0.08
INTERPRET = False
VMEM_LIMIT = 8 * 1024 * 1024

NV = 5
WIDE = 4
ROWS = 16
PLANES = 16
TILE_ROWS = 48


def vmem():
    return pl.BlockSpec(memory_space=pltpu.VMEM)


def smem():
    return pl.BlockSpec(memory_space=pltpu.SMEM)


def call(kernel, outs, scalars, arrays, flops=0, scratch=(), limit=VMEM_LIMIT):
    moved = sum(a.size * 4 for a in arrays) + sum(4 * functools.reduce(lambda x, y: x * y, o) for o in outs)
    return pl.pallas_call(
        kernel,
        out_shape=[jax.ShapeDtypeStruct(o, jnp.float32) for o in outs],
        in_specs=[smem() for _ in scalars] + [vmem() for _ in arrays],
        out_specs=[vmem() for _ in outs],
        scratch_shapes=list(scratch),
        compiler_params=pltpu.CompilerParams(vmem_limit_bytes=limit),
        cost_estimate=pl.CostEstimate(flops=flops, bytes_accessed=moved, transcendentals=0),
        interpret=INTERPRET,
    )(*scalars, *arrays)


def lanes_of(shape):
    return lax.broadcasted_iota(jnp.int32, shape, 1)


def rows_of(shape):
    return lax.broadcasted_iota(jnp.int32, shape, 0)


def roll(x, by, axis):
    size = x.shape[axis]
    if not isinstance(by, int):
        return pltpu.roll(x, lax.rem(by + 2 * size, size), axis)
    by %= size
    return x if by == 0 else pltpu.roll(x, by, axis)


def pressure(weight_ref, values):
    total = weight_ref[0] * values[0]
    for v in range(1, NV):
        total = total + weight_ref[v] * values[v]
    return total


def picked(step):
    count = 2 * (WIDE - 1 - step) + 8
    return range(step + 1, step + 1 + count), -(-6 * count // 8) * 8


def first_kernel(weight, state, volume, axial, radial, circ, mu, outflow, to_above, to_below, down, up, out_pressure):
    def put(at, half, cell):
        to_above[at, half : half + 4, :] = cell[4:8]
        to_below[at, half : half + 4, :] = cell[0:4]

    def one(k, carry):
        for half in (0, 1):
            plane = 2 * k + half
            for v in range(NV):
                put(v * 8 + k, 4 * half, state[v, plane])
            for at, array in enumerate((volume, axial, radial, circ, mu)):
                put((NV + at) * 8 + k, 4 * half, array[plane])
        return carry

    for v in range(NV):
        down[v] = state[v, PLANES - 1]
    up[...] = pressure(weight, [state[v, 0] for v in range(NV)])
    out_pressure[...] = pressure(weight, [outflow[v] for v in range(NV)])
    lax.fori_loop(0, PLANES // 2, one, 0)


def gather_kernel(first_step, ids, down, up, inflow, out_pressure, *refs):
    others, send = refs
    section = ids[0]
    size = send.shape[0]
    for v in range(NV):
        value = jnp.where(section == 0, inflow[v], down[v])
        for j in range(size):
            send[j, v * 8 : v * 8 + 8, :] = value
    value = jnp.where(section == ids[4] - 1, out_pressure[...], up[...])
    for j in range(size):
        send[j, 40:48, :] = value
        if first_step:
            for w in range(others.shape[0]):
                send[j, 48 + w : 49 + w, :] = others[w, 0:1, :]


def wanted_kernel(ids, got, lists):
    rad, rad_size = ids[2], ids[3]
    lanes = lanes_of((8, 128))
    below = got[jnp.maximum(rad - 1, 0), 48:56, :]
    above = got[jnp.minimum(rad + 1, rad_size - 1), 48:56, :]
    own = got[rad, 48:56, :]
    down = jnp.where(lanes < 4, roll(below, -4, 1), jnp.where(lanes < 12, roll(own, 4, 1), roll(above, 12, 1)))
    up = jnp.where(lanes < 20, roll(below, 4, 1), jnp.where(lanes < 28, roll(own, 12, 1), roll(above, 20, 1)))
    lists[...] = jnp.where(lanes < 16, down, up)


def extend_kernel(state, volume, axial, radial, circ, mu, from_below, from_above, field, raw, edges):
    lanes = lanes_of((ROWS, 128))

    def one(k, carry):
        last, first = carry
        for half in (0, 1):
            plane = 2 * k + half
            rows = slice(4 * half, 4 * half + 4)

            def put(at, target, index, cell):
                target[index, plane, 0:4, :] = from_below[at, rows, :]
                target[index, plane, 4:12, :] = cell
                target[index, plane, 12:16, :] = from_above[at, rows, :]
                return target[index, plane]

            for v in range(NV):
                cell = put(v * 8 + k, field, v, state[v, plane])
                at = v * 16 + plane
                last = jnp.where(lanes == at, roll(cell, at + 1, 1), last)
                first = jnp.where(lanes == at, roll(cell, at, 1), first)
            for at, array in enumerate((volume, axial, radial, circ, mu)):
                cell = put((NV + at) * 8 + k, raw, at, array[plane])
                if at == 3:
                    last = jnp.where(lanes == 96 + plane, roll(cell, 97 + plane, 1), last)
                if at == 4:
                    last = jnp.where(lanes == 80 + plane, roll(cell, 81 + plane, 1), last)
                    first = jnp.where(lanes == 80 + plane, roll(cell, 80 + plane, 1), first)
        return last, first

    zero = jnp.zeros((ROWS, 128), jnp.float32)
    last, first = lax.fori_loop(0, PLANES // 2, one, (zero, zero))
    edges[0] = last
    edges[1] = first


def select_kernel(step, ids, wanted, got, edges, send):
    size = send.shape[0]
    row = ids[1]
    rows, base = picked(step)
    count = len(rows)

    def one(j, carry):
        for n, i in enumerate(rows):
            d = wanted[j, i] & 63
            r, b = d >> 3, d & 7
            for v in range(NV):
                send[j, v * count + n : v * count + n + 1, :] = got[r, pl.ds(v * 8 + b, 1), :]
            e = wanted[j, 16 + i] & 63
            send[j, NV * count + n : NV * count + n + 1, :] = got[e >> 3, pl.ds(40 + (e & 7), 1), :]
        return carry

    lax.fori_loop(0, size, one, 0)
    send[lax.rem(row + 1, size), base : base + ROWS, :] = edges[0]
    send[lax.rem(row + size - 1, size), base : base + ROWS, :] = edges[1]


def sides(ids, across, base):
    row, row_size = ids[1], ids[5]
    left = across[lax.rem(row + row_size - 1, row_size), base : base + ROWS, :]
    right = across[lax.rem(row + 1, row_size), base : base + ROWS, :]
    return left, right


def coef_kernel(ids, raw, across, coef):
    rad, rad_size = ids[2], ids[3]
    lanes = lanes_of((ROWS, 128))
    rows = rows_of((ROWS, 128))
    outside = jnp.logical_or(
        jnp.logical_and(rad == 0, rows < WIDE), jnp.logical_and(rad == rad_size - 1, rows >= WIDE + 8)
    )
    casing = jnp.logical_and(rad == rad_size - 1, rows >= WIDE + 7)
    left, right = sides(ids, across, picked(0)[1])

    def one(k, carry):
        m = raw[4, k]
        c = jnp.where(outside, 0.0, time_step / jnp.where(outside, 1.0, raw[0, k]))
        half = 0.5 * c
        diffused = []

        def put(at, area, viscous):
            coef[at, k] = half * area
            b = c * area * viscous
            coef[at + 1, k] = b
            diffused.append(b)

        lower, upper = jnp.maximum(k - 1, 0), jnp.minimum(k + 1, PLANES - 1)
        put(0, raw[1, lower], 0.5 * (m + raw[4, lower]))
        put(2, raw[1, k], 0.5 * (m + raw[4, upper]))
        face = jnp.where(casing, 0.0, raw[2, k])
        put(4, roll(face, 1, 0), 0.5 * (m + roll(m, 1, 0)))
        put(6, face, 0.5 * (m + roll(m, ROWS - 1, 0)))
        around = raw[3, k]
        at = 80 + k
        mu_left = jnp.where(lanes == 0, roll(left, -at, 1), roll(m, 1, 1))
        mu_right = jnp.where(lanes == 127, roll(right, 127 - at, 1), roll(m, 127, 1))
        circ_left = jnp.where(lanes == 0, roll(left, -(at + 16), 1), roll(around, 1, 1))
        put(8, circ_left, 0.5 * (mu_left + m))
        put(10, around, 0.5 * (m + mu_right))
        total = diffused[0]
        for b in diffused[1:]:
            total = total + b
        coef[12, k] = 1.0 - total
        return carry

    lax.fori_loop(0, PLANES, one, 0)


def advance(k, before, here, after, coef, matrix, left, right, lanes):
    rest = coef[12, k]
    total = [rest * here[v] for v in range(NV)]
    for d in range(3):
        low_a, low_b = coef[4 * d, k], coef[4 * d + 1, k]
        high_a, high_b = coef[4 * d + 2, k], coef[4 * d + 3, k]
        own_a = high_a - low_a
        mixed = []
        for v in range(NV):
            cell = here[v]
            if d == 0:
                lower, upper = before[v], after[v]
            elif d == 1:
                lower, upper = roll(cell, 1, 0), roll(cell, ROWS - 1, 0)
            else:
                at = v * 16 + k
                lower = jnp.where(lanes == 0, roll(left, -at, 1), roll(cell, 1, 1))
                upper = jnp.where(lanes == 127, roll(right, 127 - at, 1), roll(cell, 127, 1))
            mixed.append(high_a * upper - low_a * lower + own_a * cell)
            total[v] = total[v] + (high_b * upper + low_b * lower)
        for u in range(NV):
            for v in range(NV):
                at = 25 * d + 5 * u + v
                total[u] = total[u] - jnp.broadcast_to(matrix[at : at + 1, :], (ROWS, 128)) * mixed[v]
    return total


def ghosts_of(step, ids, wanted, weight, coupling, field, across, ghost):
    rows, _ = picked(step)
    count = len(rows)
    ghost[...] = jnp.zeros(ghost.shape, jnp.float32)
    for n, i in enumerate(rows):
        d = wanted[ids[1], i] >> 6
        for v in range(NV):
            ghost[v, i : i + 1, :] = across[d, v * count + n : v * count + n + 1, :]
        e = wanted[ids[1], 16 + i] >> 6
        ghost[NV, i : i + 1, :] = across[e, NV * count + n : NV * count + n + 1, :]
    outlet = [field[v, PLANES - 1] for v in range(NV)]
    jump = ghost[NV] - pressure(weight, outlet)
    return [ghost[v] for v in range(NV)], [outlet[v] + coupling[v] * jump for v in range(NV)]


def ends_of(step, ids, wanted, weight, coupling, field, coef, matrix, across, ghost):
    lanes = lanes_of((ROWS, 128))
    left, right = sides(ids, across, picked(step)[1])
    inlet_ghost, outlet_ghost = ghosts_of(step, ids, wanted, weight, coupling, field, across, ghost)
    plane = lambda k: [field[v, k] for v in range(NV)]
    new_inlet = advance(0, inlet_ghost, plane(0), plane(1), coef, matrix, left, right, lanes)
    last = PLANES - 1
    new_outlet = advance(last, plane(last - 1), plane(last), outlet_ghost, coef, matrix, left, right, lanes)
    return new_inlet, new_outlet


def ends_kernel(step, ids, wanted, weight, coupling, field, coef, matrix, across, ends, down, up, ghost):
    new_inlet, new_outlet = ends_of(step, ids, wanted, weight, coupling, field, coef, matrix, across, ghost)
    for v in range(NV):
        ends[0, v] = new_inlet[v]
        ends[1, v] = new_outlet[v]
        down[v] = new_outlet[v][WIDE : WIDE + 8]
    up[...] = pressure(weight, new_inlet)[WIDE : WIDE + 8]


def bulk_kernel(step, ids, field, coef, matrix, across, ends, new, edges):
    lanes = lanes_of((ROWS, 128))
    left, right = sides(ids, across, picked(step)[1])

    def note(k, total, last, first):
        for v in range(NV):
            new[v, k] = total[v]
            at = v * 16 + k
            spot = lanes == at
            last = jnp.where(spot, roll(total[v], at + 1, 1), last)
            first = jnp.where(spot, roll(total[v], at, 1), first)
        return last, first

    def one(k, carry):
        before, here, last, first = carry
        after = [field[v, k + 1] for v in range(NV)]
        total = advance(k, before, here, after, coef, matrix, left, right, lanes)
        last, first = note(k, total, last, first)
        return here, after, last, first

    zero = jnp.zeros((ROWS, 128), jnp.float32)
    last, first = note(0, [ends[0, v] for v in range(NV)], zero, zero)
    last, first = note(PLANES - 1, [ends[1, v] for v in range(NV)], last, first)
    carry = ([field[v, 0] for v in range(NV)], [field[v, 1] for v in range(NV)], last, first)
    _, _, last, first = lax.fori_loop(1, PLANES - 1, one, carry)
    edges[0] = last
    edges[1] = first


def last_kernel(step, ids, wanted, weight, coupling, field, coef, matrix, across, new, ghost):
    lanes = lanes_of((ROWS, 128))
    left, right = sides(ids, across, picked(step)[1])
    new_inlet, new_outlet = ends_of(step, ids, wanted, weight, coupling, field, coef, matrix, across, ghost)
    for v in range(NV):
        new[v, 0] = new_inlet[v][WIDE : WIDE + 8]
        new[v, PLANES - 1] = new_outlet[v][WIDE : WIDE + 8]

    def one(k, carry):
        before, here = carry
        after = [field[v, k + 1] for v in range(NV)]
        total = advance(k, before, here, after, coef, matrix, left, right, lanes)
        for v in range(NV):
            new[v, k] = total[v][WIDE : WIDE + 8]
        return here, after

    carry = ([field[v, 0] for v in range(NV)], [field[v, 1] for v in range(NV)])
    lax.fori_loop(1, PLANES - 1, one, carry)


def body(
    state,
    volume,
    face_axial,
    face_radial,
    face_circum,
    viscosity,
    flux_matrix,
    inflow_plane,
    outflow_plane,
    down_donors,
    up_donors,
    pressure_weight,
    boundary_coupling,
):
    sections, row_size, rad_size = lax.axis_size("sec"), lax.axis_size("row"), lax.axis_size("rad")
    ids = jnp.stack(
        [
            lax.axis_index("sec"),
            lax.axis_index("row"),
            lax.axis_index("rad"),
            jnp.int32(rad_size),
            jnp.int32(sections),
            jnp.int32(row_size),
        ]
    ).astype(jnp.int32)
    own = [state[:, 0], volume[0], face_axial[0], face_radial[0], face_circum[0], viscosity[0]]
    donors = jnp.concatenate([down_donors[0], up_donors[0]]).astype(jnp.float32)
    donors = jnp.broadcast_to(jnp.pad(donors, (0, 112))[None, None], (row_size, 8, 128))
    matrix = jnp.broadcast_to(jnp.pad(flux_matrix[0].reshape(75), (0, 5))[:, None], (80, 128))
    extended = (NV, PLANES, ROWS, 128)
    strips = (2, ROWS, 128)
    sent = (2 * NV * PLANES // 2, 8, 128)
    scalars = [pressure_weight, boundary_coupling]

    to_above, to_below, down, up, out_pressure = call(
        first_kernel,
        [sent, sent, (NV, 8, 128), (8, 128), (8, 128)],
        [pressure_weight],
        own + [outflow_plane],
        limit=60 * 1024 * 1024,
    )
    forward = [(i, i + 1) for i in range(sections - 1)]
    backward = [(i + 1, i) for i in range(sections - 1)]
    outward = [(i, i + 1) for i in range(rad_size - 1)]
    inward = [(i + 1, i) for i in range(rad_size - 1)]
    from_below = lax.ppermute(to_above, "rad", outward)
    from_above = lax.ppermute(to_below, "rad", inward)
    table = lax.all_to_all(donors, "row", 0, 0)
    field = coef = edges = wanted = None
    for step in range(STEPS):
        last_step = step == STEPS - 1
        _, base = picked(step)
        down = lax.ppermute(down, "sec", forward)
        up = lax.ppermute(up, "sec", backward)
        (send,) = call(
            functools.partial(gather_kernel, step == 0),
            [(rad_size, TILE_ROWS + (8 if step == 0 else 0), 128)],
            [ids],
            [down, up, inflow_plane, out_pressure, table if step == 0 else edges],
        )
        got = lax.all_to_all(send, "rad", 0, 0)
        if step == 0:
            (lists,) = call(wanted_kernel, [(8, 128)], [ids], [got])
            wanted = lists[:, :32].astype(jnp.int32)
            field, raw, edges = call(extend_kernel, [extended, extended, strips], [], own + [from_below, from_above])
        (send,) = call(
            functools.partial(select_kernel, step), [(row_size, base + ROWS, 128)], [ids, wanted], [got, edges]
        )
        across = lax.all_to_all(send, "row", 0, 0)
        if step == 0:
            (coef,) = call(coef_kernel, [(13, PLANES, ROWS, 128)], [ids], [raw, across])
        ghost = [pltpu.VMEM((NV + 1, ROWS, 128), jnp.float32)]
        if last_step:
            (field,) = call(
                functools.partial(last_kernel, step),
                [(NV, PLANES, 8, 128)],
                [ids, wanted] + scalars,
                [field, coef, matrix, across],
                flops=PLANES * ROWS * 128 * 300,
                scratch=ghost,
            )
        else:
            ends, down, up = call(
                functools.partial(ends_kernel, step),
                [(2, NV, ROWS, 128), (NV, 8, 128), (8, 128)],
                [ids, wanted] + scalars,
                [field, coef, matrix, across],
                flops=2 * ROWS * 128 * 300,
                scratch=ghost,
            )
            field, edges = call(
                functools.partial(bulk_kernel, step),
                [extended, strips],
                [ids],
                [field, coef, matrix, across, ends],
                flops=PLANES * ROWS * 128 * 300,
            )
    return field[:, None]


def solution(mesh):
    in_specs = (
        P(None, "sec", None, "rad", "row"),
        P("sec", None, "rad", "row"),
        P("sec", None, "rad", "row"),
        P("sec", None, "rad", "row"),
        P("sec", None, "rad", "row"),
        P("sec", None, "rad", "row"),
        P("sec", None, None, None),
        P(None, "rad", "row"),
        P(None, "rad", "row"),
        P("sec", ("row", "rad")),
        P("sec", ("row", "rad")),
        P(),
        P(),
    )
    out_specs = P(None, "sec", None, "rad", "row")

    return jax.shard_map(body, mesh=mesh, in_specs=in_specs, out_specs=out_specs, check_vma=False)
```

```python
import functools

import jax
import jax.numpy as jnp
from jax import lax
from jax.experimental import pallas as pl
from jax.experimental.pallas import tpu as pltpu
from jax.sharding import PartitionSpec as P


STEPS = 4
time_step = 0.08
INTERPRET = False
VMEM_LIMIT = 8 * 1024 * 1024
FAR_LIMIT = 60 * 1024 * 1024

NV = 5
WIDE = 4
ROWS = 16
PLANES = 16
TILE_ROWS = 48


def vmem():
    return pl.BlockSpec(memory_space=pltpu.VMEM)


def smem():
    return pl.BlockSpec(memory_space=pltpu.SMEM)


def hbm():
    return pl.BlockSpec(memory_space=pltpu.HBM)


def call(kernel, outs, scalars, arrays, flops=0, scratch=(), far=()):
    moved = sum(a.size * 4 for a in arrays) + sum(4 * functools.reduce(lambda x, y: x * y, o) for o in outs)
    scratch = list(scratch)
    if far:
        scratch += [pltpu.VMEM(a.shape, jnp.float32) for a in far] + [pltpu.SemaphoreType.DMA((len(far),))]
    return pl.pallas_call(
        kernel,
        out_shape=[jax.ShapeDtypeStruct(o, jnp.float32) for o in outs],
        in_specs=[smem() for _ in scalars] + [vmem() for _ in arrays] + [hbm() for _ in far],
        out_specs=[vmem() for _ in outs],
        scratch_shapes=scratch,
        compiler_params=pltpu.CompilerParams(vmem_limit_bytes=FAR_LIMIT if far else VMEM_LIMIT),
        cost_estimate=pl.CostEstimate(flops=flops, bytes_accessed=moved, transcendentals=0),
        interpret=INTERPRET,
    )(*scalars, *arrays, *far)


def lanes_of(shape):
    return lax.broadcasted_iota(jnp.int32, shape, 1)


def rows_of(shape):
    return lax.broadcasted_iota(jnp.int32, shape, 0)


def roll(x, by, axis):
    size = x.shape[axis]
    if not isinstance(by, int):
        return pltpu.roll(x, lax.rem(by + 2 * size, size), axis)
    by %= size
    return x if by == 0 else pltpu.roll(x, by, axis)


def pressure(weight_ref, values):
    total = weight_ref[0] * values[0]
    for v in range(1, NV):
        total = total + weight_ref[v] * values[v]
    return total


def picked(step):
    count = 2 * (WIDE - 1 - step) + 8
    return range(step + 1, step + 1 + count), -(-6 * count // 8) * 8


def fetch(sources, targets, sems):
    copies = [pltpu.make_async_copy(a, b, sems.at[i]) for i, (a, b) in enumerate(zip(sources, targets))]
    for copy in copies:
        copy.start()
    for copy in copies:
        copy.wait()


def first_kernel(ids, weight, down_donors, up_donors, state_hbm, circ_hbm, mu_hbm, outflow_hbm, down, up, out_pressure, send, state, circ, mu, outflow, sems):
    fetch((state_hbm, circ_hbm, mu_hbm, outflow_hbm), (state, circ, mu, outflow), sems)
    lanes = lanes_of((8, 128))
    row, size = ids[1], send.shape[0]
    for v in range(NV):
        down[v] = state[v, PLANES - 1]
    up[...] = pressure(weight, [state[v, 0] for v in range(NV)])
    out_pressure[...] = pressure(weight, [outflow[v] for v in range(NV)])
    listed = jnp.zeros((8, 128), jnp.int32)
    for a in range(8):
        listed = jnp.where(lanes == a, down_donors[a], listed)
        listed = jnp.where(lanes == 8 + a, up_donors[a], listed)
    listed = listed.astype(jnp.float32)
    for j in range(size):
        send[j, 0:8, :] = listed

    def one(k, carry):
        last, first = carry
        for v in range(NV):
            cell = state[v, k]
            at = v * 16 + k
            here = lanes == at
            last = jnp.where(here, roll(cell, at + 1, 1), last)
            first = jnp.where(here, roll(cell, at, 1), first)
        here = lanes == 80 + k
        last = jnp.where(here, roll(mu[k], 81 + k, 1), last)
        first = jnp.where(here, roll(mu[k], 80 + k, 1), first)
        last = jnp.where(lanes == 96 + k, roll(circ[k], 97 + k, 1), last)
        return last, first

    zero = jnp.zeros((8, 128), jnp.float32)
    last, first = lax.fori_loop(0, PLANES, one, (zero, zero))
    send[lax.rem(row + 1, size), 8:16, :] = last
    send[lax.rem(row + size - 1, size), 8:16, :] = first


def pack_kernel(ids, table, *refs):
    sources, (to_above, to_below, field, raw), targets, sems = refs[:6], refs[6:10], refs[10:16], refs[16]
    fetch(sources, targets, sems)
    state, arrays = targets[0], targets[1:]
    row, size = ids[1], table.shape[0]

    def put(at, half, cell):
        to_above[at, half : half + 4, :] = cell[4:8]
        to_below[at, half : half + 4, :] = cell[0:4]

    def one(k, carry):
        for half in (0, 1):
            plane = 2 * k + half
            for v in range(NV):
                cell = state[v, plane]
                put(v * 8 + k, 4 * half, cell)
                field[v, plane, 4:12, :] = cell
            for at, array in enumerate(arrays):
                cell = array[plane]
                put((NV + at) * 8 + k, 4 * half, cell)
                raw[at, plane, 4:12, :] = cell
        return carry

    lax.fori_loop(0, PLANES // 2, one, 0)
    put(2 * NV * 8, 0, table[lax.rem(row + size - 1, size), 8:16, :])
    put(2 * NV * 8, 4, table[lax.rem(row + 1, size), 8:16, :])


def gather_kernel(first_step, ids, down, up, inflow, out_pressure, *refs):
    others, send = refs
    section = ids[0]
    size = send.shape[0]
    for v in range(NV):
        value = jnp.where(section == 0, inflow[v], down[v])
        for j in range(size):
            send[j, v * 8 : v * 8 + 8, :] = value
    value = jnp.where(section == ids[4] - 1, out_pressure[...], up[...])
    for j in range(size):
        send[j, 40:48, :] = value
        if first_step:
            for w in range(others.shape[0]):
                send[j, 48 + w : 49 + w, :] = others[w, 0:1, :]


def wanted_kernel(ids, got, lists):
    rad, rad_size = ids[2], ids[3]
    lanes = lanes_of((8, 128))
    below = got[jnp.maximum(rad - 1, 0), 48:56, :]
    above = got[jnp.minimum(rad + 1, rad_size - 1), 48:56, :]
    own = got[rad, 48:56, :]
    down = jnp.where(lanes < 4, roll(below, -4, 1), jnp.where(lanes < 12, roll(own, 4, 1), roll(above, 12, 1)))
    up = jnp.where(lanes < 20, roll(below, 4, 1), jnp.where(lanes < 28, roll(own, 12, 1), roll(above, 20, 1)))
    lists[...] = jnp.where(lanes < 16, down, up)


def extend_kernel(ids, field_in, raw_in, table, from_below, from_above, field, raw, around):
    row, size = ids[1], table.shape[0]

    def one(k, carry):
        for half in (0, 1):
            plane = 2 * k + half
            rows = slice(4 * half, 4 * half + 4)
            for target, base in ((field, 0), (raw, NV)):
                for v in range(NV):
                    at = (base + v) * 8 + k
                    target[v, plane, 0:4, :] = from_below[at, rows, :]
                    target[v, plane, 12:16, :] = from_above[at, rows, :]
                    target[v, plane, 4:12, :] = (field_in, raw_in)[base // NV][v, plane, 4:12, :]
        return carry

    lax.fori_loop(0, PLANES // 2, one, 0)
    for side, source in enumerate((lax.rem(row + size - 1, size), lax.rem(row + 1, size))):
        rows = slice(4 * side, 4 * side + 4)
        around[side, 0:4, :] = from_below[2 * NV * 8, rows, :]
        around[side, 4:12, :] = table[source, 8:16, :]
        around[side, 12:16, :] = from_above[2 * NV * 8, rows, :]


def select_kernel(step, ids, wanted, got, *refs):
    send = refs[-1]
    size = send.shape[0]
    row = ids[1]
    rows, base = picked(step)
    count = len(rows)

    def one(j, carry):
        for n, i in enumerate(rows):
            d = wanted[j, i] & 63
            r, b = d >> 3, d & 7
            for v in range(NV):
                send[j, v * count + n : v * count + n + 1, :] = got[r, pl.ds(v * 8 + b, 1), :]
            e = wanted[j, 16 + i] & 63
            send[j, NV * count + n : NV * count + n + 1, :] = got[e >> 3, pl.ds(40 + (e & 7), 1), :]
        return carry

    lax.fori_loop(0, size, one, 0)
    if step:
        edges = refs[0]
        send[lax.rem(row + 1, size), base : base + ROWS, :] = edges[0]
        send[lax.rem(row + size - 1, size), base : base + ROWS, :] = edges[1]


def sides(step, ids, around):
    if step == 0:
        return around[0], around[1]
    base = picked(step)[1]
    row, row_size = ids[1], ids[5]
    left = around[lax.rem(row + row_size - 1, row_size), base : base + ROWS, :]
    right = around[lax.rem(row + 1, row_size), base : base + ROWS, :]
    return left, right


def coef_kernel(ids, raw, around_ref, coef):
    rad, rad_size = ids[2], ids[3]
    lanes = lanes_of((ROWS, 128))
    rows = rows_of((ROWS, 128))
    outside = jnp.logical_or(
        jnp.logical_and(rad == 0, rows < WIDE), jnp.logical_and(rad == rad_size - 1, rows >= WIDE + 8)
    )
    casing = jnp.logical_and(rad == rad_size - 1, rows >= WIDE + 7)
    left, right = sides(0, ids, around_ref)

    def one(k, carry):
        m = raw[4, k]
        c = jnp.where(outside, 0.0, time_step / jnp.where(outside, 1.0, raw[0, k]))
        half = 0.5 * c
        diffused = []

        def put(at, area, viscous):
            coef[at, k] = half * area
            b = c * area * viscous
            coef[at + 1, k] = b
            diffused.append(b)

        lower, upper = jnp.maximum(k - 1, 0), jnp.minimum(k + 1, PLANES - 1)
        put(0, raw[1, lower], 0.5 * (m + raw[4, lower]))
        put(2, raw[1, k], 0.5 * (m + raw[4, upper]))
        face = jnp.where(casing, 0.0, raw[2, k])
        put(4, roll(face, 1, 0), 0.5 * (m + roll(m, 1, 0)))
        put(6, face, 0.5 * (m + roll(m, ROWS - 1, 0)))
        around = raw[3, k]
        at = 80 + k
        mu_left = jnp.where(lanes == 0, roll(left, -at, 1), roll(m, 1, 1))
        mu_right = jnp.where(lanes == 127, roll(right, 127 - at, 1), roll(m, 127, 1))
        circ_left = jnp.where(lanes == 0, roll(left, -(at + 16), 1), roll(around, 1, 1))
        put(8, circ_left, 0.5 * (mu_left + m))
        put(10, around, 0.5 * (m + mu_right))
        total = diffused[0]
        for b in diffused[1:]:
            total = total + b
        coef[12, k] = 1.0 - total
        return carry

    lax.fori_loop(0, PLANES, one, 0)


def advance(k, before, here, after, coef, matrix, left, right, lanes):
    rest = coef[12, k]
    total = [rest * here[v] for v in range(NV)]
    for d in range(3):
        low_a, low_b = coef[4 * d, k], coef[4 * d + 1, k]
        high_a, high_b = coef[4 * d + 2, k], coef[4 * d + 3, k]
        own_a = high_a - low_a
        mixed = []
        for v in range(NV):
            cell = here[v]
            if d == 0:
                lower, upper = before[v], after[v]
            elif d == 1:
                lower, upper = roll(cell, 1, 0), roll(cell, ROWS - 1, 0)
            else:
                at = v * 16 + k
                lower = jnp.where(lanes == 0, roll(left, -at, 1), roll(cell, 1, 1))
                upper = jnp.where(lanes == 127, roll(right, 127 - at, 1), roll(cell, 127, 1))
            mixed.append(high_a * upper - low_a * lower + own_a * cell)
            total[v] = total[v] + (high_b * upper + low_b * lower)
        for u in range(NV):
            for v in range(NV):
                at = 25 * d + 5 * u + v
                total[u] = total[u] - jnp.broadcast_to(matrix[at : at + 1, :], (ROWS, 128)) * mixed[v]
    return total


def ghosts_of(step, ids, wanted, weight, coupling, field, across, ghost):
    rows, _ = picked(step)
    count = len(rows)
    ghost[...] = jnp.zeros(ghost.shape, jnp.float32)
    for n, i in enumerate(rows):
        d = wanted[ids[1], i] >> 6
        for v in range(NV):
            ghost[v, i : i + 1, :] = across[d, v * count + n : v * count + n + 1, :]
        e = wanted[ids[1], 16 + i] >> 6
        ghost[NV, i : i + 1, :] = across[e, NV * count + n : NV * count + n + 1, :]
    outlet = [field[v, PLANES - 1] for v in range(NV)]
    jump = ghost[NV] - pressure(weight, outlet)
    return [ghost[v] for v in range(NV)], [outlet[v] + coupling[v] * jump for v in range(NV)]


def ends_of(step, ids, wanted, weight, coupling, field, coef, matrix, across, around, ghost):
    lanes = lanes_of((ROWS, 128))
    left, right = sides(step, ids, around)
    inlet_ghost, outlet_ghost = ghosts_of(step, ids, wanted, weight, coupling, field, across, ghost)
    plane = lambda k: [field[v, k] for v in range(NV)]
    new_inlet = advance(0, inlet_ghost, plane(0), plane(1), coef, matrix, left, right, lanes)
    last = PLANES - 1
    new_outlet = advance(last, plane(last - 1), plane(last), outlet_ghost, coef, matrix, left, right, lanes)
    return new_inlet, new_outlet


def ends_kernel(step, ids, wanted, weight, coupling, field, coef, matrix, across, around, ends, down, up, ghost):
    new_inlet, new_outlet = ends_of(step, ids, wanted, weight, coupling, field, coef, matrix, across, around, ghost)
    for v in range(NV):
        ends[0, v] = new_inlet[v]
        ends[1, v] = new_outlet[v]
        down[v] = new_outlet[v][WIDE : WIDE + 8]
    up[...] = pressure(weight, new_inlet)[WIDE : WIDE + 8]


def bulk_kernel(step, ids, field, coef, matrix, around, ends, new, edges):
    lanes = lanes_of((ROWS, 128))
    left, right = sides(step, ids, around)

    def note(k, total, last, first):
        for v in range(NV):
            new[v, k] = total[v]
            at = v * 16 + k
            spot = lanes == at
            last = jnp.where(spot, roll(total[v], at + 1, 1), last)
            first = jnp.where(spot, roll(total[v], at, 1), first)
        return last, first

    def one(k, carry):
        before, here, last, first = carry
        after = [field[v, k + 1] for v in range(NV)]
        total = advance(k, before, here, after, coef, matrix, left, right, lanes)
        last, first = note(k, total, last, first)
        return here, after, last, first

    zero = jnp.zeros((ROWS, 128), jnp.float32)
    last, first = note(0, [ends[0, v] for v in range(NV)], zero, zero)
    last, first = note(PLANES - 1, [ends[1, v] for v in range(NV)], last, first)
    carry = ([field[v, 0] for v in range(NV)], [field[v, 1] for v in range(NV)], last, first)
    _, _, last, first = lax.fori_loop(1, PLANES - 1, one, carry)
    edges[0] = last
    edges[1] = first


def last_kernel(step, ids, wanted, weight, coupling, field, coef, matrix, across, around, new, ghost):
    lanes = lanes_of((ROWS, 128))
    left, right = sides(step, ids, around)
    new_inlet, new_outlet = ends_of(step, ids, wanted, weight, coupling, field, coef, matrix, across, around, ghost)
    for v in range(NV):
        new[v, 0] = new_inlet[v][WIDE : WIDE + 8]
        new[v, PLANES - 1] = new_outlet[v][WIDE : WIDE + 8]

    def one(k, carry):
        before, here = carry
        after = [field[v, k + 1] for v in range(NV)]
        total = advance(k, before, here, after, coef, matrix, left, right, lanes)
        for v in range(NV):
            new[v, k] = total[v][WIDE : WIDE + 8]
        return here, after

    carry = ([field[v, 0] for v in range(NV)], [field[v, 1] for v in range(NV)])
    lax.fori_loop(1, PLANES - 1, one, carry)


def body(
    state,
    volume,
    face_axial,
    face_radial,
    face_circum,
    viscosity,
    flux_matrix,
    inflow_plane,
    outflow_plane,
    down_donors,
    up_donors,
    pressure_weight,
    boundary_coupling,
):
    sections, row_size, rad_size = lax.axis_size("sec"), lax.axis_size("row"), lax.axis_size("rad")
    ids = jnp.stack(
        [
            lax.axis_index("sec"),
            lax.axis_index("row"),
            lax.axis_index("rad"),
            jnp.int32(rad_size),
            jnp.int32(sections),
            jnp.int32(row_size),
        ]
    ).astype(jnp.int32)
    own = [state[:, 0], volume[0], face_axial[0], face_radial[0], face_circum[0], viscosity[0]]
    matrix = jnp.broadcast_to(jnp.pad(flux_matrix[0].reshape(75), (0, 5))[:, None], (80, 128))
    extended = (NV, PLANES, ROWS, 128)
    strips = (2, ROWS, 128)
    sent = (2 * NV * PLANES // 2 + 1, 8, 128)
    scalars = [pressure_weight, boundary_coupling]

    down, up, out_pressure, lists = call(
        first_kernel,
        [(NV, 8, 128), (8, 128), (8, 128), (row_size, 16, 128)],
        [ids, pressure_weight, down_donors[0], up_donors[0]],
        [],
        far=[own[0], own[4], own[5], outflow_plane],
    )
    forward = [(i, i + 1) for i in range(sections - 1)]
    backward = [(i + 1, i) for i in range(sections - 1)]
    outward = [(i, i + 1) for i in range(rad_size - 1)]
    inward = [(i + 1, i) for i in range(rad_size - 1)]
    table = lax.all_to_all(lists, "row", 0, 0)
    to_above, to_below, field, raw = call(pack_kernel, [sent, sent, extended, extended], [ids], [table], far=own)
    from_below = lax.ppermute(to_above, "rad", outward)
    from_above = lax.ppermute(to_below, "rad", inward)
    coef = edges = wanted = None
    for step in range(STEPS):
        last_step = step == STEPS - 1
        _, base = picked(step)
        down = lax.ppermute(down, "sec", forward)
        up = lax.ppermute(up, "sec", backward)
        (send,) = call(
            functools.partial(gather_kernel, step == 0),
            [(rad_size, TILE_ROWS + (8 if step == 0 else 0), 128)],
            [ids],
            [down, up, inflow_plane, out_pressure, table if step == 0 else edges],
        )
        got = lax.all_to_all(send, "rad", 0, 0)
        if step == 0:
            (lists,) = call(wanted_kernel, [(8, 128)], [ids], [got])
            wanted = lists[:, :32].astype(jnp.int32)
            field, raw, around = call(
                extend_kernel, [extended, extended, strips], [ids], [field, raw, table, from_below, from_above]
            )
            (coef,) = call(coef_kernel, [(13, PLANES, ROWS, 128)], [ids], [raw, around])
        (send,) = call(
            functools.partial(select_kernel, step),
            [(row_size, base + (ROWS if step else 0), 128)],
            [ids, wanted],
            [got, edges] if step else [got],
        )
        across = lax.all_to_all(send, "row", 0, 0)
        if step:
            around = across
        ghost = [pltpu.VMEM((NV + 1, ROWS, 128), jnp.float32)]
        if last_step:
            (field,) = call(
                functools.partial(last_kernel, step),
                [(NV, PLANES, 8, 128)],
                [ids, wanted] + scalars,
                [field, coef, matrix, across, around],
                flops=PLANES * ROWS * 128 * 300,
                scratch=ghost,
            )
        else:
            ends, down, up = call(
                functools.partial(ends_kernel, step),
                [(2, NV, ROWS, 128), (NV, 8, 128), (8, 128)],
                [ids, wanted] + scalars,
                [field, coef, matrix, across, around],
                flops=2 * ROWS * 128 * 300,
                scratch=ghost,
            )
            field, edges = call(
                functools.partial(bulk_kernel, step),
                [extended, strips],
                [ids],
                [field, coef, matrix, around, ends],
                flops=PLANES * ROWS * 128 * 300,
            )
    return field[:, None]


def solution(mesh):
    in_specs = (
        P(None, "sec", None, "rad", "row"),
        P("sec", None, "rad", "row"),
        P("sec", None, "rad", "row"),
        P("sec", None, "rad", "row"),
        P("sec", None, "rad", "row"),
        P("sec", None, "rad", "row"),
        P("sec", None, None, None),
        P(None, "rad", "row"),
        P(None, "rad", "row"),
        P("sec", ("row", "rad")),
        P("sec", ("row", "rad")),
        P(),
        P(),
    )
    out_specs = P(None, "sec", None, "rad", "row")

    return jax.shard_map(body, mesh=mesh, in_specs=in_specs, out_specs=out_specs, check_vma=False)
```

```python
import functools

import jax
import jax.numpy as jnp
from jax import lax
from jax.experimental import pallas as pl
from jax.experimental.pallas import tpu as pltpu
from jax.sharding import PartitionSpec as P


STEPS = 4
time_step = 0.08
INTERPRET = False
VMEM_LIMIT = 8 * 1024 * 1024
FAR_LIMIT = 60 * 1024 * 1024

NV = 5
ROWS = 8
FIELD_ROWS = 80
PLANES = 16
TILE_ROWS = 48


def vmem():
    return pl.BlockSpec(memory_space=pltpu.VMEM)


def smem():
    return pl.BlockSpec(memory_space=pltpu.SMEM)


def hbm():
    return pl.BlockSpec(memory_space=pltpu.HBM)


def call(kernel, outs, scalars, arrays, flops=0, scratch=(), far=()):
    moved = sum(a.size * 4 for a in arrays) + sum(4 * functools.reduce(lambda x, y: x * y, o) for o in outs)
    scratch = list(scratch)
    if far:
        scratch += [pltpu.VMEM(a.shape, jnp.float32) for a in far] + [pltpu.SemaphoreType.DMA((len(far),))]
    return pl.pallas_call(
        kernel,
        out_shape=[jax.ShapeDtypeStruct(o, jnp.float32) for o in outs],
        in_specs=[smem() for _ in scalars] + [vmem() for _ in arrays] + [hbm() for _ in far],
        out_specs=[vmem() for _ in outs],
        scratch_shapes=scratch,
        compiler_params=pltpu.CompilerParams(vmem_limit_bytes=FAR_LIMIT if far else VMEM_LIMIT),
        cost_estimate=pl.CostEstimate(flops=flops, bytes_accessed=moved, transcendentals=0),
        interpret=INTERPRET,
    )(*scalars, *arrays, *far)


def lanes_of(shape):
    return lax.broadcasted_iota(jnp.int32, shape, 1)


def rows_of(shape):
    return lax.broadcasted_iota(jnp.int32, shape, 0)


def roll(x, by, axis):
    size = x.shape[axis]
    if not isinstance(by, int):
        return pltpu.roll(x, lax.rem(by + 2 * size, size), axis)
    by %= size
    return x if by == 0 else pltpu.roll(x, by, axis)


def pressure(weight_ref, values):
    total = weight_ref[0] * values[0]
    for v in range(1, NV):
        total = total + weight_ref[v] * values[v]
    return total


def fetch(sources, targets, sems):
    copies = [pltpu.make_async_copy(a, b, sems.at[i]) for i, (a, b) in enumerate(zip(sources, targets))]
    for copy in copies:
        copy.start()
    for copy in copies:
        copy.wait()


def first_kernel(ids, weight, down_donors, up_donors, *refs):
    sources, (down, up, out_pressure, send, to_above, to_below), targets, sems = refs[:5], refs[5:11], refs[11:16], refs[16]
    fetch(sources, targets, sems)
    state, radial, circ, mu, outflow = targets
    lanes = lanes_of((8, 128))
    row, size = ids[1], send.shape[0]
    for v in range(NV):
        down[v] = state[v, PLANES - 1]
    up[...] = pressure(weight, [state[v, 0] for v in range(NV)])
    out_pressure[...] = pressure(weight, [outflow[v] for v in range(NV)])
    listed = jnp.zeros((8, 128), jnp.int32)
    for a in range(8):
        listed = jnp.where(lanes == a, down_donors[a], listed)
        listed = jnp.where(lanes == 8 + a, up_donors[a], listed)
    listed = listed.astype(jnp.float32)
    for j in range(size):
        send[j, 0:8, :] = listed

    def put(at, cell):
        to_above[pl.ds(at, 1), :] = cell[7:8]
        to_below[pl.ds(at, 1), :] = cell[0:1]

    def one(k, carry):
        last, first = carry
        for v in range(NV):
            cell = state[v, k]
            at = v * 16 + k
            put(at, cell)
            here = lanes == at
            last = jnp.where(here, roll(cell, at + 1, 1), last)
            first = jnp.where(here, roll(cell, at, 1), first)
        put(FIELD_ROWS + k, mu[k])
        put(FIELD_ROWS + 16 + k, radial[k])
        here = lanes == 80 + k
        last = jnp.where(here, roll(mu[k], 81 + k, 1), last)
        first = jnp.where(here, roll(mu[k], 80 + k, 1), first)
        last = jnp.where(lanes == 96 + k, roll(circ[k], 97 + k, 1), last)
        return last, first

    zero = jnp.zeros((8, 128), jnp.float32)
    last, first = lax.fori_loop(0, PLANES, one, (zero, zero))
    send[lax.rem(row + 1, size), 8:16, :] = last
    send[lax.rem(row + size - 1, size), 8:16, :] = first


def gather_kernel(ids, down, up, inflow, out_pressure, after, send):
    section = ids[0]
    size = send.shape[0]
    for v in range(NV):
        value = jnp.where(section == 0, inflow[v], down[v])
        for j in range(size):
            send[j, v * 8 : v * 8 + 8, :] = value
    value = jnp.where(section == ids[4] - 1, out_pressure[...], up[...])
    for j in range(size):
        send[j, 40:48, :] = value


def select_kernel(step, ids, wanted, got, *refs):
    send = refs[-1]
    size = send.shape[0]
    row = ids[1]

    def one(j, carry):
        for a in range(8):
            d = wanted[j, a] & 63
            r, b = d >> 3, d & 7
            for v in range(NV):
                send[j, v * 8 + a : v * 8 + a + 1, :] = got[r, pl.ds(v * 8 + b, 1), :]
            e = wanted[j, 8 + a] & 63
            send[j, 40 + a : 41 + a, :] = got[e >> 3, pl.ds(40 + (e & 7), 1), :]
        return carry

    lax.fori_loop(0, size, one, 0)
    if step:
        edges = refs[0]
        send[lax.rem(row + 1, size), 48:56, :] = edges[0]
        send[lax.rem(row + size - 1, size), 48:56, :] = edges[1]


def sides(step, ids, around):
    base = 48 if step else 8
    row, row_size = ids[1], ids[5]
    left = around[lax.rem(row + row_size - 1, row_size), base : base + ROWS, :]
    right = around[lax.rem(row + 1, row_size), base : base + ROWS, :]
    return left, right


def beyond(ref, at):
    return jnp.broadcast_to(ref[pl.ds(at, 1), :], (ROWS, 128))


def coef_kernel(ids, volume, axial, radial, circ, mu, around, low, high, coef):
    rad, rad_size = ids[2], ids[3]
    lanes = lanes_of((ROWS, 128))
    rows = rows_of((ROWS, 128))
    casing = jnp.logical_and(rad == rad_size - 1, rows == 7)
    left, right = sides(0, ids, around)

    def one(k, carry):
        m = mu[k]
        c = time_step / volume[k]
        half = 0.5 * c
        diffused = []

        def put(at, area, viscous):
            coef[at, k] = half * area
            b = c * area * viscous
            coef[at + 1, k] = b
            diffused.append(b)

        lower, upper = jnp.maximum(k - 1, 0), jnp.minimum(k + 1, PLANES - 1)
        put(0, axial[lower], 0.5 * (m + mu[lower]))
        put(2, axial[k], 0.5 * (m + mu[upper]))
        face = jnp.where(casing, 0.0, radial[k])
        face_below = jnp.where(rows == 0, beyond(low, FIELD_ROWS + 16 + k), roll(face, 1, 0))
        mu_below = jnp.where(rows == 0, beyond(low, FIELD_ROWS + k), roll(m, 1, 0))
        mu_above = jnp.where(rows == 7, beyond(high, FIELD_ROWS + k), roll(m, 7, 0))
        put(4, face_below, 0.5 * (m + mu_below))
        put(6, face, 0.5 * (m + mu_above))
        ring = circ[k]
        at = 80 + k
        mu_left = jnp.where(lanes == 0, roll(left, -at, 1), roll(m, 1, 1))
        mu_right = jnp.where(lanes == 127, roll(right, 127 - at, 1), roll(m, 127, 1))
        circ_left = jnp.where(lanes == 0, roll(left, -(at + 16), 1), roll(ring, 1, 1))
        put(8, circ_left, 0.5 * (mu_left + m))
        put(10, ring, 0.5 * (m + mu_right))
        total = diffused[0]
        for b in diffused[1:]:
            total = total + b
        coef[12, k] = 1.0 - total
        return carry

    lax.fori_loop(0, PLANES, one, 0)


def advance(k, before, here, after, coef, matrix, left, right, low, high):
    lanes = lanes_of((ROWS, 128))
    rows = rows_of((ROWS, 128))
    rest = coef[12, k]
    total = [rest * here[v] for v in range(NV)]
    for d in range(3):
        low_a, low_b = coef[4 * d, k], coef[4 * d + 1, k]
        high_a, high_b = coef[4 * d + 2, k], coef[4 * d + 3, k]
        own_a = high_a - low_a
        mixed = []
        for v in range(NV):
            cell = here[v]
            at = v * 16 + k
            if d == 0:
                lower, upper = before[v], after[v]
            elif d == 1:
                lower = jnp.where(rows == 0, beyond(low, at), roll(cell, 1, 0))
                upper = jnp.where(rows == 7, beyond(high, at), roll(cell, 7, 0))
            else:
                lower = jnp.where(lanes == 0, roll(left, -at, 1), roll(cell, 1, 1))
                upper = jnp.where(lanes == 127, roll(right, 127 - at, 1), roll(cell, 127, 1))
            mixed.append(high_a * upper - low_a * lower + own_a * cell)
            total[v] = total[v] + (high_b * upper + low_b * lower)
        for u in range(NV):
            for v in range(NV):
                at = 25 * d + 5 * u + v
                total[u] = total[u] - jnp.broadcast_to(matrix[at : at + 1, :], (ROWS, 128)) * mixed[v]
    return total


def ghosts_of(ids, wanted, weight, coupling, field, across, ghost):
    for a in range(8):
        d = wanted[ids[1], a] >> 6
        for v in range(NV):
            ghost[v, a : a + 1, :] = across[d, v * 8 + a : v * 8 + a + 1, :]
        e = wanted[ids[1], 8 + a] >> 6
        ghost[NV, a : a + 1, :] = across[e, 40 + a : 41 + a, :]
    outlet = [field[v, PLANES - 1] for v in range(NV)]
    jump = ghost[NV] - pressure(weight, outlet)
    return [ghost[v] for v in range(NV)], [outlet[v] + coupling[v] * jump for v in range(NV)]


def ends_of(step, ids, wanted, weight, coupling, field, coef, matrix, across, around, low, high, ghost):
    lanes = lanes_of((ROWS, 128))
    left, right = sides(step, ids, around)
    inlet_ghost, outlet_ghost = ghosts_of(ids, wanted, weight, coupling, field, across, ghost)
    plane = lambda k: [field[v, k] for v in range(NV)]
    new_inlet = advance(0, inlet_ghost, plane(0), plane(1), coef, matrix, left, right, low, high)
    last = PLANES - 1
    new_outlet = advance(last, plane(last - 1), plane(last), outlet_ghost, coef, matrix, left, right, low, high)
    return new_inlet, new_outlet


def ends_kernel(step, ids, wanted, weight, coupling, field, coef, matrix, across, around, low, high, ends, down, up, ghost):
    new_inlet, new_outlet = ends_of(step, ids, wanted, weight, coupling, field, coef, matrix, across, around, low, high, ghost)
    for v in range(NV):
        ends[0, v] = new_inlet[v]
        ends[1, v] = new_outlet[v]
        down[v] = new_outlet[v]
    up[...] = pressure(weight, new_inlet)


def bulk_kernel(step, ids, field, coef, matrix, around, low, high, ends, new, edges, to_above, to_below):
    lanes = lanes_of((ROWS, 128))
    left, right = sides(step, ids, around)

    def note(k, total, last, first):
        for v in range(NV):
            new[v, k] = total[v]
            at = v * 16 + k
            to_above[pl.ds(at, 1), :] = total[v][7:8]
            to_below[pl.ds(at, 1), :] = total[v][0:1]
            spot = lanes == at
            last = jnp.where(spot, roll(total[v], at + 1, 1), last)
            first = jnp.where(spot, roll(total[v], at, 1), first)
        return last, first

    def one(k, carry):
        before, here, last, first = carry
        after = [field[v, k + 1] for v in range(NV)]
        total = advance(k, before, here, after, coef, matrix, left, right, low, high)
        last, first = note(k, total, last, first)
        return here, after, last, first

    zero = jnp.zeros((ROWS, 128), jnp.float32)
    last, first = note(0, [ends[0, v] for v in range(NV)], zero, zero)
    last, first = note(PLANES - 1, [ends[1, v] for v in range(NV)], last, first)
    carry = ([field[v, 0] for v in range(NV)], [field[v, 1] for v in range(NV)], last, first)
    _, _, last, first = lax.fori_loop(1, PLANES - 1, one, carry)
    edges[0] = last
    edges[1] = first


def last_kernel(step, ids, wanted, weight, coupling, field, coef, matrix, across, around, low, high, new, ghost):
    lanes = lanes_of((ROWS, 128))
    left, right = sides(step, ids, around)
    new_inlet, new_outlet = ends_of(step, ids, wanted, weight, coupling, field, coef, matrix, across, around, low, high, ghost)
    for v in range(NV):
        new[v, 0] = new_inlet[v]
        new[v, PLANES - 1] = new_outlet[v]

    def one(k, carry):
        before, here = carry
        after = [field[v, k + 1] for v in range(NV)]
        total = advance(k, before, here, after, coef, matrix, left, right, low, high)
        for v in range(NV):
            new[v, k] = total[v]
        return here, after

    carry = ([field[v, 0] for v in range(NV)], [field[v, 1] for v in range(NV)])
    lax.fori_loop(1, PLANES - 1, one, carry)


def body(
    state,
    volume,
    face_axial,
    face_radial,
    face_circum,
    viscosity,
    flux_matrix,
    inflow_plane,
    outflow_plane,
    down_donors,
    up_donors,
    pressure_weight,
    boundary_coupling,
):
    sections, row_size, rad_size = lax.axis_size("sec"), lax.axis_size("row"), lax.axis_size("rad")
    ids = jnp.stack(
        [
            lax.axis_index("sec"),
            lax.axis_index("row"),
            lax.axis_index("rad"),
            jnp.int32(rad_size),
            jnp.int32(sections),
            jnp.int32(row_size),
        ]
    ).astype(jnp.int32)
    own = [state[:, 0], volume[0], face_axial[0], face_radial[0], face_circum[0], viscosity[0]]
    matrix = jnp.broadcast_to(jnp.pad(flux_matrix[0].reshape(75), (0, 5))[:, None], (80, 128))
    extended = (NV, PLANES, ROWS, 128)
    strips = (2, ROWS, 128)
    sent = (FIELD_ROWS + 32, 128)
    scalars = [pressure_weight, boundary_coupling]

    down, up, out_pressure, lists, to_above, to_below = call(
        first_kernel,
        [(NV, 8, 128), (8, 128), (8, 128), (row_size, 16, 128), sent, sent],
        [ids, pressure_weight, down_donors[0], up_donors[0]],
        [],
        far=[own[0], own[3], own[4], own[5], outflow_plane],
    )
    forward = [(i, i + 1) for i in range(sections - 1)]
    backward = [(i + 1, i) for i in range(sections - 1)]
    outward = [(i, i + 1) for i in range(rad_size - 1)]
    inward = [(i + 1, i) for i in range(rad_size - 1)]
    table = lax.all_to_all(lists, "row", 0, 0)
    wanted = table[:, 0, :16].astype(jnp.int32)
    field = own[0]
    coef = edges = None
    for step in range(STEPS):
        last_step = step == STEPS - 1
        down = lax.ppermute(down, "sec", forward)
        up = lax.ppermute(up, "sec", backward)
        (send,) = call(
            gather_kernel,
            [(rad_size, TILE_ROWS, 128)],
            [ids],
            [down, up, inflow_plane, out_pressure, edges if step else table],
        )
        got = lax.all_to_all(send, "rad", 0, 0)
        low = lax.ppermute(to_above, "rad", outward)
        high = lax.ppermute(to_below, "rad", inward)
        if step == 0:
            (coef,) = call(coef_kernel, [(13, PLANES, ROWS, 128)], [ids], own[1:] + [table, low, high])
        (send,) = call(
            functools.partial(select_kernel, step),
            [(row_size, TILE_ROWS + (ROWS if step else 0), 128)],
            [ids, wanted],
            [got, edges] if step else [got],
        )
        across = lax.all_to_all(send, "row", 0, 0)
        around = across if step else table
        ghost = [pltpu.VMEM((NV + 1, ROWS, 128), jnp.float32)]
        if last_step:
            (field,) = call(
                functools.partial(last_kernel, step),
                [(NV, PLANES, 8, 128)],
                [ids, wanted] + scalars,
                [field, coef, matrix, across, around, low, high],
                flops=PLANES * ROWS * 128 * 300,
                scratch=ghost,
            )
        else:
            ends, down, up = call(
                functools.partial(ends_kernel, step),
                [(2, NV, ROWS, 128), (NV, 8, 128), (8, 128)],
                [ids, wanted] + scalars,
                [field, coef, matrix, across, around, low, high],
                flops=2 * ROWS * 128 * 300,
                scratch=ghost,
            )
            field, edges, to_above, to_below = call(
                functools.partial(bulk_kernel, step),
                [extended, strips, (FIELD_ROWS, 128), (FIELD_ROWS, 128)],
                [ids],
                [field, coef, matrix, around, low, high, ends],
                flops=PLANES * ROWS * 128 * 300,
            )
    return field[:, None]


def solution(mesh):
    in_specs = (
        P(None, "sec", None, "rad", "row"),
        P("sec", None, "rad", "row"),
        P("sec", None, "rad", "row"),
        P("sec", None, "rad", "row"),
        P("sec", None, "rad", "row"),
        P("sec", None, "rad", "row"),
        P("sec", None, None, None),
        P(None, "rad", "row"),
        P(None, "rad", "row"),
        P("sec", ("row", "rad")),
        P("sec", ("row", "rad")),
        P(),
        P(),
    )
    out_specs = P(None, "sec", None, "rad", "row")

    return jax.shard_map(body, mesh=mesh, in_specs=in_specs, out_specs=out_specs, check_vma=False)
```

```python
import functools

import jax
import jax.numpy as jnp
from jax import lax
from jax.experimental import pallas as pl
from jax.experimental.pallas import tpu as pltpu
from jax.sharding import PartitionSpec as P


STEPS = 4
time_step = 0.08
INTERPRET = False
VMEM_LIMIT = 8 * 1024 * 1024
FAR_LIMIT = 60 * 1024 * 1024

NV = 5
ROWS = 8
FIELD_ROWS = 80
PLANES = 16
TILE_ROWS = 48


def vmem():
    return pl.BlockSpec(memory_space=pltpu.VMEM)


def smem():
    return pl.BlockSpec(memory_space=pltpu.SMEM)


def hbm():
    return pl.BlockSpec(memory_space=pltpu.HBM)


def call(kernel, outs, scalars, arrays, flops=0, scratch=(), far=()):
    moved = sum(a.size * 4 for a in arrays) + sum(4 * functools.reduce(lambda x, y: x * y, o) for o in outs)
    scratch = list(scratch)
    if far:
        scratch += [pltpu.VMEM(a.shape, jnp.float32) for a in far] + [pltpu.SemaphoreType.DMA((len(far),))]
    return pl.pallas_call(
        kernel,
        out_shape=[jax.ShapeDtypeStruct(o, jnp.float32) for o in outs],
        in_specs=[smem() for _ in scalars] + [vmem() for _ in arrays] + [hbm() for _ in far],
        out_specs=[vmem() for _ in outs],
        scratch_shapes=scratch,
        compiler_params=pltpu.CompilerParams(vmem_limit_bytes=FAR_LIMIT if far else VMEM_LIMIT),
        cost_estimate=pl.CostEstimate(flops=flops, bytes_accessed=moved, transcendentals=0),
        interpret=INTERPRET,
    )(*scalars, *arrays, *far)


def lanes_of(shape):
    return lax.broadcasted_iota(jnp.int32, shape, 1)


def rows_of(shape):
    return lax.broadcasted_iota(jnp.int32, shape, 0)


def roll(x, by, axis):
    size = x.shape[axis]
    if not isinstance(by, int):
        return pltpu.roll(x, lax.rem(by + 2 * size, size), axis)
    by %= size
    return x if by == 0 else pltpu.roll(x, by, axis)


def pressure(weight_ref, values):
    total = weight_ref[0] * values[0]
    for v in range(1, NV):
        total = total + weight_ref[v] * values[v]
    return total


def fetch(sources, targets, sems):
    copies = [pltpu.make_async_copy(a, b, sems.at[i]) for i, (a, b) in enumerate(zip(sources, targets))]
    for copy in copies:
        copy.start()
    for copy in copies:
        copy.wait()


def first_kernel(ids, weight, down_donors, up_donors, *refs):
    sources, (beside, out_pressure, send, first_swap, second_swap), targets, sems = refs[:5], refs[5:10], refs[10:15], refs[15]
    fetch(sources, targets, sems)
    state, radial, circ, mu, outflow = targets
    lanes = lanes_of((8, 128))
    row, size = ids[1], send.shape[0]
    for v in range(NV):
        beside[v] = state[v, PLANES - 1]
    beside[NV] = pressure(weight, [state[v, 0] for v in range(NV)])
    out_pressure[...] = pressure(weight, [outflow[v] for v in range(NV)])
    listed = jnp.zeros((8, 128), jnp.int32)
    for a in range(8):
        listed = jnp.where(lanes == a, down_donors[a], listed)
        listed = jnp.where(lanes == 8 + a, up_donors[a], listed)
    listed = listed.astype(jnp.float32)
    for j in range(size):
        send[j, 0:8, :] = listed

    even = lax.rem(ids[2], 2) == 0

    def put(at, cell):
        first_swap[pl.ds(at, 1), :] = jnp.where(even, cell[7:8], cell[0:1])
        second_swap[pl.ds(at, 1), :] = jnp.where(even, cell[0:1], cell[7:8])

    def one(k, carry):
        last, first = carry
        for v in range(NV):
            cell = state[v, k]
            at = v * 16 + k
            put(at, cell)
            here = lanes == at
            last = jnp.where(here, roll(cell, at + 1, 1), last)
            first = jnp.where(here, roll(cell, at, 1), first)
        put(FIELD_ROWS + k, mu[k])
        put(FIELD_ROWS + 16 + k, radial[k])
        here = lanes == 80 + k
        last = jnp.where(here, roll(mu[k], 81 + k, 1), last)
        first = jnp.where(here, roll(mu[k], 80 + k, 1), first)
        last = jnp.where(lanes == 96 + k, roll(circ[k], 97 + k, 1), last)
        return last, first

    zero = jnp.zeros((8, 128), jnp.float32)
    last, first = lax.fori_loop(0, PLANES, one, (zero, zero))
    send[lax.rem(row + 1, size), 8:16, :] = last
    send[lax.rem(row + size - 1, size), 8:16, :] = first


def gather_kernel(ids, one_way, other_way, inflow, out_pressure, after, send):
    section = ids[0]
    odd = lax.rem(section, 2) == 1
    size = send.shape[0]
    for v in range(NV):
        value = jnp.where(section == 0, inflow[v], jnp.where(odd, one_way[v], other_way[v]))
        for j in range(size):
            send[j, v * 8 : v * 8 + 8, :] = value
    value = jnp.where(section == ids[4] - 1, out_pressure[...], jnp.where(odd, other_way[NV], one_way[NV]))
    for j in range(size):
        send[j, 40:48, :] = value


def select_kernel(step, ids, wanted, got, *refs):
    send = refs[-1]
    size = send.shape[0]
    row = ids[1]

    def one(j, carry):
        for a in range(8):
            d = wanted[j, a] & 63
            r, b = d >> 3, d & 7
            for v in range(NV):
                send[j, v * 8 + a : v * 8 + a + 1, :] = got[r, pl.ds(v * 8 + b, 1), :]
            e = wanted[j, 8 + a] & 63
            send[j, 40 + a : 41 + a, :] = got[e >> 3, pl.ds(40 + (e & 7), 1), :]
        return carry

    lax.fori_loop(0, size, one, 0)
    if step:
        edges = refs[0]
        send[lax.rem(row + 1, size), 48:56, :] = edges[0]
        send[lax.rem(row + size - 1, size), 48:56, :] = edges[1]


def sides(step, ids, around):
    base = 48 if step else 8
    row, row_size = ids[1], ids[5]
    left = around[lax.rem(row + row_size - 1, row_size), base : base + ROWS, :]
    right = around[lax.rem(row + 1, row_size), base : base + ROWS, :]
    return left, right


def settle(ids, first_swap, second_swap, low, high):
    even = lax.rem(ids[2], 2) == 0
    low[...] = jnp.where(even, second_swap[...], first_swap[...])
    high[...] = jnp.where(even, first_swap[...], second_swap[...])


def beyond(ref, at):
    return jnp.broadcast_to(ref[pl.ds(at, 1), :], (ROWS, 128))


def coef_kernel(ids, volume, axial, radial, circ, mu, around, first_swap, second_swap, coef, low, high):
    settle(ids, first_swap, second_swap, low, high)
    rad, rad_size = ids[2], ids[3]
    lanes = lanes_of((ROWS, 128))
    rows = rows_of((ROWS, 128))
    casing = jnp.logical_and(rad == rad_size - 1, rows == 7)
    left, right = sides(0, ids, around)

    def one(k, carry):
        m = mu[k]
        c = time_step / volume[k]
        half = 0.5 * c
        diffused = []

        def put(at, area, viscous):
            coef[at, k] = half * area
            b = c * area * viscous
            coef[at + 1, k] = b
            diffused.append(b)

        lower, upper = jnp.maximum(k - 1, 0), jnp.minimum(k + 1, PLANES - 1)
        put(0, axial[lower], 0.5 * (m + mu[lower]))
        put(2, axial[k], 0.5 * (m + mu[upper]))
        face = jnp.where(casing, 0.0, radial[k])
        face_below = jnp.where(rows == 0, beyond(low, FIELD_ROWS + 16 + k), roll(face, 1, 0))
        mu_below = jnp.where(rows == 0, beyond(low, FIELD_ROWS + k), roll(m, 1, 0))
        mu_above = jnp.where(rows == 7, beyond(high, FIELD_ROWS + k), roll(m, 7, 0))
        put(4, face_below, 0.5 * (m + mu_below))
        put(6, face, 0.5 * (m + mu_above))
        ring = circ[k]
        at = 80 + k
        mu_left = jnp.where(lanes == 0, roll(left, -at, 1), roll(m, 1, 1))
        mu_right = jnp.where(lanes == 127, roll(right, 127 - at, 1), roll(m, 127, 1))
        circ_left = jnp.where(lanes == 0, roll(left, -(at + 16), 1), roll(ring, 1, 1))
        put(8, circ_left, 0.5 * (mu_left + m))
        put(10, ring, 0.5 * (m + mu_right))
        total = diffused[0]
        for b in diffused[1:]:
            total = total + b
        coef[12, k] = 1.0 - total
        return carry

    lax.fori_loop(0, PLANES, one, 0)


def advance(k, before, here, after, coef, matrix, left, right, low, high):
    lanes = lanes_of((ROWS, 128))
    rows = rows_of((ROWS, 128))
    rest = coef[12, k]
    total = [rest * here[v] for v in range(NV)]
    for d in range(3):
        low_a, low_b = coef[4 * d, k], coef[4 * d + 1, k]
        high_a, high_b = coef[4 * d + 2, k], coef[4 * d + 3, k]
        own_a = high_a - low_a
        mixed = []
        for v in range(NV):
            cell = here[v]
            at = v * 16 + k
            if d == 0:
                lower, upper = before[v], after[v]
            elif d == 1:
                lower = jnp.where(rows == 0, beyond(low, at), roll(cell, 1, 0))
                upper = jnp.where(rows == 7, beyond(high, at), roll(cell, 7, 0))
            else:
                lower = jnp.where(lanes == 0, roll(left, -at, 1), roll(cell, 1, 1))
                upper = jnp.where(lanes == 127, roll(right, 127 - at, 1), roll(cell, 127, 1))
            mixed.append(high_a * upper - low_a * lower + own_a * cell)
            total[v] = total[v] + (high_b * upper + low_b * lower)
        for u in range(NV):
            for v in range(NV):
                at = 25 * d + 5 * u + v
                total[u] = total[u] - jnp.broadcast_to(matrix[at : at + 1, :], (ROWS, 128)) * mixed[v]
    return total


def ghosts_of(ids, wanted, weight, coupling, field, across, ghost):
    for a in range(8):
        d = wanted[ids[1], a] >> 6
        for v in range(NV):
            ghost[v, a : a + 1, :] = across[d, v * 8 + a : v * 8 + a + 1, :]
        e = wanted[ids[1], 8 + a] >> 6
        ghost[NV, a : a + 1, :] = across[e, 40 + a : 41 + a, :]
    outlet = [field[v, PLANES - 1] for v in range(NV)]
    jump = ghost[NV] - pressure(weight, outlet)
    return [ghost[v] for v in range(NV)], [outlet[v] + coupling[v] * jump for v in range(NV)]


def ends_of(step, ids, wanted, weight, coupling, field, coef, matrix, across, around, low, high, ghost):
    lanes = lanes_of((ROWS, 128))
    left, right = sides(step, ids, around)
    inlet_ghost, outlet_ghost = ghosts_of(ids, wanted, weight, coupling, field, across, ghost)
    plane = lambda k: [field[v, k] for v in range(NV)]
    new_inlet = advance(0, inlet_ghost, plane(0), plane(1), coef, matrix, left, right, low, high)
    last = PLANES - 1
    new_outlet = advance(last, plane(last - 1), plane(last), outlet_ghost, coef, matrix, left, right, low, high)
    return new_inlet, new_outlet


def ends_kernel(step, ids, wanted, weight, coupling, field, coef, matrix, across, around, first_swap, second_swap, ends, beside, ghost, low, high):
    settle(ids, first_swap, second_swap, low, high)
    new_inlet, new_outlet = ends_of(step, ids, wanted, weight, coupling, field, coef, matrix, across, around, low, high, ghost)
    for v in range(NV):
        ends[0, v] = new_inlet[v]
        ends[1, v] = new_outlet[v]
        beside[v] = new_outlet[v]
    beside[NV] = pressure(weight, new_inlet)


def bulk_kernel(step, ids, field, coef, matrix, around, from_first, from_second, ends, new, edges, first_swap, second_swap, low, high):
    settle(ids, from_first, from_second, low, high)
    even = lax.rem(ids[2], 2) == 0
    lanes = lanes_of((ROWS, 128))
    left, right = sides(step, ids, around)

    def note(k, total, last, first):
        for v in range(NV):
            new[v, k] = total[v]
            at = v * 16 + k
            first_swap[pl.ds(at, 1), :] = jnp.where(even, total[v][7:8], total[v][0:1])
            second_swap[pl.ds(at, 1), :] = jnp.where(even, total[v][0:1], total[v][7:8])
            spot = lanes == at
            last = jnp.where(spot, roll(total[v], at + 1, 1), last)
            first = jnp.where(spot, roll(total[v], at, 1), first)
        return last, first

    def one(k, carry):
        before, here, last, first = carry
        after = [field[v, k + 1] for v in range(NV)]
        total = advance(k, before, here, after, coef, matrix, left, right, low, high)
        last, first = note(k, total, last, first)
        return here, after, last, first

    zero = jnp.zeros((ROWS, 128), jnp.float32)
    last, first = note(0, [ends[0, v] for v in range(NV)], zero, zero)
    last, first = note(PLANES - 1, [ends[1, v] for v in range(NV)], last, first)
    carry = ([field[v, 0] for v in range(NV)], [field[v, 1] for v in range(NV)], last, first)
    _, _, last, first = lax.fori_loop(1, PLANES - 1, one, carry)
    edges[0] = last
    edges[1] = first


def last_kernel(step, ids, wanted, weight, coupling, field, coef, matrix, across, around, first_swap, second_swap, new, ghost, low, high):
    settle(ids, first_swap, second_swap, low, high)
    lanes = lanes_of((ROWS, 128))
    left, right = sides(step, ids, around)
    new_inlet, new_outlet = ends_of(step, ids, wanted, weight, coupling, field, coef, matrix, across, around, low, high, ghost)
    for v in range(NV):
        new[v, 0] = new_inlet[v]
        new[v, PLANES - 1] = new_outlet[v]

    def one(k, carry):
        before, here = carry
        after = [field[v, k + 1] for v in range(NV)]
        total = advance(k, before, here, after, coef, matrix, left, right, low, high)
        for v in range(NV):
            new[v, k] = total[v]
        return here, after

    carry = ([field[v, 0] for v in range(NV)], [field[v, 1] for v in range(NV)])
    lax.fori_loop(1, PLANES - 1, one, carry)


def body(
    state,
    volume,
    face_axial,
    face_radial,
    face_circum,
    viscosity,
    flux_matrix,
    inflow_plane,
    outflow_plane,
    down_donors,
    up_donors,
    pressure_weight,
    boundary_coupling,
):
    sections, row_size, rad_size = lax.axis_size("sec"), lax.axis_size("row"), lax.axis_size("rad")
    ids = jnp.stack(
        [
            lax.axis_index("sec"),
            lax.axis_index("row"),
            lax.axis_index("rad"),
            jnp.int32(rad_size),
            jnp.int32(sections),
            jnp.int32(row_size),
        ]
    ).astype(jnp.int32)
    own = [state[:, 0], volume[0], face_axial[0], face_radial[0], face_circum[0], viscosity[0]]
    matrix = jnp.broadcast_to(jnp.pad(flux_matrix[0].reshape(75), (0, 5))[:, None], (80, 128))
    extended = (NV, PLANES, ROWS, 128)
    strips = (2, ROWS, 128)
    sent = (FIELD_ROWS + 32, 128)
    scalars = [pressure_weight, boundary_coupling]

    beside, out_pressure, lists, first_swap, second_swap = call(
        first_kernel,
        [(NV + 1, 8, 128), (8, 128), (row_size, 16, 128), sent, sent],
        [ids, pressure_weight, down_donors[0], up_donors[0]],
        [],
        far=[own[0], own[3], own[4], own[5], outflow_plane],
    )

    def swaps(size, begin):
        return [pair for i in range(begin, size - 1, 2) for pair in ((i, i + 1), (i + 1, i))]

    table = lax.all_to_all(lists, "row", 0, 0)
    wanted = table[:, 0, :16].astype(jnp.int32)
    field = own[0]
    coef = edges = None
    for step in range(STEPS):
        last_step = step == STEPS - 1
        one_way = lax.ppermute(beside, "sec", swaps(sections, 0))
        other_way = lax.ppermute(beside, "sec", swaps(sections, 1))
        (send,) = call(
            gather_kernel,
            [(rad_size, TILE_ROWS, 128)],
            [ids],
            [one_way, other_way, inflow_plane, out_pressure, edges if step else table],
        )
        got = lax.all_to_all(send, "rad", 0, 0)
        low = lax.ppermute(first_swap, "rad", swaps(rad_size, 0))
        high = lax.ppermute(second_swap, "rad", swaps(rad_size, 1))
        strip = [pltpu.VMEM(low.shape, jnp.float32)] * 2
        if step == 0:
            (coef,) = call(coef_kernel, [(13, PLANES, ROWS, 128)], [ids], own[1:] + [table, low, high], scratch=strip)
        (send,) = call(
            functools.partial(select_kernel, step),
            [(row_size, TILE_ROWS + (ROWS if step else 0), 128)],
            [ids, wanted],
            [got, edges] if step else [got],
        )
        across = lax.all_to_all(send, "row", 0, 0)
        around = across if step else table
        ghost = [pltpu.VMEM((NV + 1, ROWS, 128), jnp.float32)]
        if last_step:
            (field,) = call(
                functools.partial(last_kernel, step),
                [(NV, PLANES, 8, 128)],
                [ids, wanted] + scalars,
                [field, coef, matrix, across, around, low, high],
                flops=PLANES * ROWS * 128 * 300,
                scratch=ghost + strip,
            )
        else:
            ends, beside = call(
                functools.partial(ends_kernel, step),
                [(2, NV, ROWS, 128), (NV + 1, 8, 128)],
                [ids, wanted] + scalars,
                [field, coef, matrix, across, around, low, high],
                flops=2 * ROWS * 128 * 300,
                scratch=ghost + strip,
            )
            field, edges, first_swap, second_swap = call(
                functools.partial(bulk_kernel, step),
                [extended, strips, (FIELD_ROWS, 128), (FIELD_ROWS, 128)],
                [ids],
                [field, coef, matrix, around, low, high, ends],
                scratch=strip,
                flops=PLANES * ROWS * 128 * 300,
            )
    return field[:, None]


def solution(mesh):
    in_specs = (
        P(None, "sec", None, "rad", "row"),
        P("sec", None, "rad", "row"),
        P("sec", None, "rad", "row"),
        P("sec", None, "rad", "row"),
        P("sec", None, "rad", "row"),
        P("sec", None, "rad", "row"),
        P("sec", None, None, None),
        P(None, "rad", "row"),
        P(None, "rad", "row"),
        P("sec", ("row", "rad")),
        P("sec", ("row", "rad")),
        P(),
        P(),
    )
    out_specs = P(None, "sec", None, "rad", "row")

    return jax.shard_map(body, mesh=mesh, in_specs=in_specs, out_specs=out_specs, check_vma=False)
```

```python
import functools

import jax
import jax.numpy as jnp
from jax import lax
from jax.experimental import pallas as pl
from jax.experimental.pallas import tpu as pltpu
from jax.sharding import PartitionSpec as P


STEPS = 4
time_step = 0.08
INTERPRET = False
VMEM_LIMIT = 8 * 1024 * 1024
FAR_LIMIT = 60 * 1024 * 1024

NV = 5
ROWS = 8
FIELD_ROWS = 80
PLANES = 16
TILE_ROWS = 48


def vmem():
    return pl.BlockSpec(memory_space=pltpu.VMEM)


def smem():
    return pl.BlockSpec(memory_space=pltpu.SMEM)


def hbm():
    return pl.BlockSpec(memory_space=pltpu.HBM)


def call(kernel, outs, scalars, arrays, flops=0, scratch=(), far=()):
    moved = sum(a.size * 4 for a in arrays) + sum(4 * functools.reduce(lambda x, y: x * y, o) for o in outs)
    scratch = list(scratch)
    if far:
        scratch += [pltpu.VMEM(a.shape, jnp.float32) for a in far] + [pltpu.SemaphoreType.DMA((len(far),))]
    return pl.pallas_call(
        kernel,
        out_shape=[jax.ShapeDtypeStruct(o, jnp.float32) for o in outs],
        in_specs=[smem() for _ in scalars] + [vmem() for _ in arrays] + [hbm() for _ in far],
        out_specs=[vmem() for _ in outs],
        scratch_shapes=scratch,
        compiler_params=pltpu.CompilerParams(vmem_limit_bytes=FAR_LIMIT if far else VMEM_LIMIT),
        cost_estimate=pl.CostEstimate(flops=flops, bytes_accessed=moved, transcendentals=0),
        interpret=INTERPRET,
    )(*scalars, *arrays, *far)


def lanes_of(shape):
    return lax.broadcasted_iota(jnp.int32, shape, 1)


def rows_of(shape):
    return lax.broadcasted_iota(jnp.int32, shape, 0)


def roll(x, by, axis):
    size = x.shape[axis]
    if not isinstance(by, int):
        return pltpu.roll(x, lax.rem(by + 2 * size, size), axis)
    by %= size
    return x if by == 0 else pltpu.roll(x, by, axis)


def pressure(weight_ref, values):
    total = weight_ref[0] * values[0]
    for v in range(1, NV):
        total = total + weight_ref[v] * values[v]
    return total


def fetch(sources, targets, sems):
    copies = [pltpu.make_async_copy(a, b, sems.at[i]) for i, (a, b) in enumerate(zip(sources, targets))]
    for copy in copies:
        copy.start()
    for copy in copies:
        copy.wait()


def beside_kernel(weight, state_hbm, beside, inlet, sem):
    copies = [
        pltpu.make_async_copy(state_hbm.at[:, PLANES - 1], beside.at[pl.ds(0, NV)], sem.at[0]),
        pltpu.make_async_copy(state_hbm.at[:, 0], inlet, sem.at[1]),
    ]
    for copy in copies:
        copy.start()
    for copy in copies:
        copy.wait()
    beside[NV] = pressure(weight, [inlet[v] for v in range(NV)])


def first_kernel(ids, weight, down_donors, up_donors, *refs):
    sources, (out_pressure, send, first_swap, second_swap), targets, sems = refs[:5], refs[5:9], refs[9:14], refs[14]
    fetch(sources, targets, sems)
    state, radial, circ, mu, outflow = targets
    lanes = lanes_of((8, 128))
    row, size = ids[1], send.shape[0]
    out_pressure[...] = pressure(weight, [outflow[v] for v in range(NV)])
    listed = jnp.zeros((8, 128), jnp.int32)
    for a in range(8):
        listed = jnp.where(lanes == a, down_donors[a], listed)
        listed = jnp.where(lanes == 8 + a, up_donors[a], listed)
    listed = listed.astype(jnp.float32)
    for j in range(size):
        send[j, 0:8, :] = listed

    even = lax.rem(ids[2], 2) == 0

    def put(at, cell):
        first_swap[pl.ds(at, 1), :] = jnp.where(even, cell[7:8], cell[0:1])
        second_swap[pl.ds(at, 1), :] = jnp.where(even, cell[0:1], cell[7:8])

    def one(k, carry):
        last, first = carry
        for v in range(NV):
            cell = state[v, k]
            at = v * 16 + k
            put(at, cell)
            here = lanes == at
            last = jnp.where(here, roll(cell, at + 1, 1), last)
            first = jnp.where(here, roll(cell, at, 1), first)
        put(FIELD_ROWS + k, mu[k])
        put(FIELD_ROWS + 16 + k, radial[k])
        here = lanes == 80 + k
        last = jnp.where(here, roll(mu[k], 81 + k, 1), last)
        first = jnp.where(here, roll(mu[k], 80 + k, 1), first)
        last = jnp.where(lanes == 96 + k, roll(circ[k], 97 + k, 1), last)
        return last, first

    zero = jnp.zeros((8, 128), jnp.float32)
    last, first = lax.fori_loop(0, PLANES, one, (zero, zero))
    send[lax.rem(row + 1, size), 8:16, :] = last
    send[lax.rem(row + size - 1, size), 8:16, :] = first


def gather_kernel(ids, one_way, other_way, inflow, out_pressure, after, send):
    section = ids[0]
    odd = lax.rem(section, 2) == 1
    size = send.shape[0]
    for v in range(NV):
        value = jnp.where(section == 0, inflow[v], jnp.where(odd, one_way[v], other_way[v]))
        for j in range(size):
            send[j, v * 8 : v * 8 + 8, :] = value
    value = jnp.where(section == ids[4] - 1, out_pressure[...], jnp.where(odd, other_way[NV], one_way[NV]))
    for j in range(size):
        send[j, 40:48, :] = value


def select_kernel(step, ids, wanted, got, *refs):
    send = refs[-1]
    size = send.shape[0]
    row = ids[1]

    def one(j, carry):
        for a in range(8):
            d = wanted[j, a] & 63
            r, b = d >> 3, d & 7
            for v in range(NV):
                send[j, v * 8 + a : v * 8 + a + 1, :] = got[r, pl.ds(v * 8 + b, 1), :]
            e = wanted[j, 8 + a] & 63
            send[j, 40 + a : 41 + a, :] = got[e >> 3, pl.ds(40 + (e & 7), 1), :]
        return carry

    lax.fori_loop(0, size, one, 0)
    if step:
        edges = refs[0]
        send[lax.rem(row + 1, size), 48:56, :] = edges[0]
        send[lax.rem(row + size - 1, size), 48:56, :] = edges[1]


def sides(step, ids, around):
    base = 48 if step else 8
    row, row_size = ids[1], ids[5]
    left = around[lax.rem(row + row_size - 1, row_size), base : base + ROWS, :]
    right = around[lax.rem(row + 1, row_size), base : base + ROWS, :]
    return left, right


def settle(ids, first_swap, second_swap, low, high):
    even = lax.rem(ids[2], 2) == 0
    low[...] = jnp.where(even, second_swap[...], first_swap[...])
    high[...] = jnp.where(even, first_swap[...], second_swap[...])


def beyond(ref, at):
    return jnp.broadcast_to(ref[pl.ds(at, 1), :], (ROWS, 128))


def coef_kernel(ids, volume, axial, radial, circ, mu, around, first_swap, second_swap, coef, low, high):
    settle(ids, first_swap, second_swap, low, high)
    rad, rad_size = ids[2], ids[3]
    lanes = lanes_of((ROWS, 128))
    rows = rows_of((ROWS, 128))
    casing = jnp.logical_and(rad == rad_size - 1, rows == 7)
    left, right = sides(0, ids, around)

    def one(k, carry):
        m = mu[k]
        c = time_step / volume[k]
        half = 0.5 * c
        diffused = []

        def put(at, area, viscous):
            coef[at, k] = half * area
            b = c * area * viscous
            coef[at + 1, k] = b
            diffused.append(b)

        lower, upper = jnp.maximum(k - 1, 0), jnp.minimum(k + 1, PLANES - 1)
        put(0, axial[lower], 0.5 * (m + mu[lower]))
        put(2, axial[k], 0.5 * (m + mu[upper]))
        face = jnp.where(casing, 0.0, radial[k])
        face_below = jnp.where(rows == 0, beyond(low, FIELD_ROWS + 16 + k), roll(face, 1, 0))
        mu_below = jnp.where(rows == 0, beyond(low, FIELD_ROWS + k), roll(m, 1, 0))
        mu_above = jnp.where(rows == 7, beyond(high, FIELD_ROWS + k), roll(m, 7, 0))
        put(4, face_below, 0.5 * (m + mu_below))
        put(6, face, 0.5 * (m + mu_above))
        ring = circ[k]
        at = 80 + k
        mu_left = jnp.where(lanes == 0, roll(left, -at, 1), roll(m, 1, 1))
        mu_right = jnp.where(lanes == 127, roll(right, 127 - at, 1), roll(m, 127, 1))
        circ_left = jnp.where(lanes == 0, roll(left, -(at + 16), 1), roll(ring, 1, 1))
        put(8, circ_left, 0.5 * (mu_left + m))
        put(10, ring, 0.5 * (m + mu_right))
        total = diffused[0]
        for b in diffused[1:]:
            total = total + b
        coef[12, k] = 1.0 - total
        return carry

    lax.fori_loop(0, PLANES, one, 0)


def advance(k, before, here, after, coef, matrix, left, right, low, high):
    lanes = lanes_of((ROWS, 128))
    rows = rows_of((ROWS, 128))
    rest = coef[12, k]
    total = [rest * here[v] for v in range(NV)]
    for d in range(3):
        low_a, low_b = coef[4 * d, k], coef[4 * d + 1, k]
        high_a, high_b = coef[4 * d + 2, k], coef[4 * d + 3, k]
        own_a = high_a - low_a
        mixed = []
        for v in range(NV):
            cell = here[v]
            at = v * 16 + k
            if d == 0:
                lower, upper = before[v], after[v]
            elif d == 1:
                lower = jnp.where(rows == 0, beyond(low, at), roll(cell, 1, 0))
                upper = jnp.where(rows == 7, beyond(high, at), roll(cell, 7, 0))
            else:
                lower = jnp.where(lanes == 0, roll(left, -at, 1), roll(cell, 1, 1))
                upper = jnp.where(lanes == 127, roll(right, 127 - at, 1), roll(cell, 127, 1))
            mixed.append(high_a * upper - low_a * lower + own_a * cell)
            total[v] = total[v] + (high_b * upper + low_b * lower)
        for u in range(NV):
            for v in range(NV):
                at = 25 * d + 5 * u + v
                total[u] = total[u] - jnp.broadcast_to(matrix[at : at + 1, :], (ROWS, 128)) * mixed[v]
    return total


def ghosts_of(ids, wanted, weight, coupling, field, across, ghost):
    for a in range(8):
        d = wanted[ids[1], a] >> 6
        for v in range(NV):
            ghost[v, a : a + 1, :] = across[d, v * 8 + a : v * 8 + a + 1, :]
        e = wanted[ids[1], 8 + a] >> 6
        ghost[NV, a : a + 1, :] = across[e, 40 + a : 41 + a, :]
    outlet = [field[v, PLANES - 1] for v in range(NV)]
    jump = ghost[NV] - pressure(weight, outlet)
    return [ghost[v] for v in range(NV)], [outlet[v] + coupling[v] * jump for v in range(NV)]


def ends_of(step, ids, wanted, weight, coupling, field, coef, matrix, across, around, low, high, ghost):
    lanes = lanes_of((ROWS, 128))
    left, right = sides(step, ids, around)
    inlet_ghost, outlet_ghost = ghosts_of(ids, wanted, weight, coupling, field, across, ghost)
    plane = lambda k: [field[v, k] for v in range(NV)]
    new_inlet = advance(0, inlet_ghost, plane(0), plane(1), coef, matrix, left, right, low, high)
    last = PLANES - 1
    new_outlet = advance(last, plane(last - 1), plane(last), outlet_ghost, coef, matrix, left, right, low, high)
    return new_inlet, new_outlet


def ends_kernel(step, ids, wanted, weight, coupling, field, coef, matrix, across, around, first_swap, second_swap, ends, beside, ghost, low, high):
    settle(ids, first_swap, second_swap, low, high)
    new_inlet, new_outlet = ends_of(step, ids, wanted, weight, coupling, field, coef, matrix, across, around, low, high, ghost)
    for v in range(NV):
        ends[0, v] = new_inlet[v]
        ends[1, v] = new_outlet[v]
        beside[v] = new_outlet[v]
    beside[NV] = pressure(weight, new_inlet)


def bulk_kernel(step, ids, field, coef, matrix, around, from_first, from_second, ends, new, edges, first_swap, second_swap, low, high):
    settle(ids, from_first, from_second, low, high)
    even = lax.rem(ids[2], 2) == 0
    lanes = lanes_of((ROWS, 128))
    left, right = sides(step, ids, around)

    def note(k, total, last, first):
        for v in range(NV):
            new[v, k] = total[v]
            at = v * 16 + k
            first_swap[pl.ds(at, 1), :] = jnp.where(even, total[v][7:8], total[v][0:1])
            second_swap[pl.ds(at, 1), :] = jnp.where(even, total[v][0:1], total[v][7:8])
            spot = lanes == at
            last = jnp.where(spot, roll(total[v], at + 1, 1), last)
            first = jnp.where(spot, roll(total[v], at, 1), first)
        return last, first

    def one(k, carry):
        before, here, last, first = carry
        after = [field[v, k + 1] for v in range(NV)]
        total = advance(k, before, here, after, coef, matrix, left, right, low, high)
        last, first = note(k, total, last, first)
        return here, after, last, first

    zero = jnp.zeros((ROWS, 128), jnp.float32)
    last, first = note(0, [ends[0, v] for v in range(NV)], zero, zero)
    last, first = note(PLANES - 1, [ends[1, v] for v in range(NV)], last, first)
    carry = ([field[v, 0] for v in range(NV)], [field[v, 1] for v in range(NV)], last, first)
    _, _, last, first = lax.fori_loop(1, PLANES - 1, one, carry)
    edges[0] = last
    edges[1] = first


def last_kernel(step, ids, wanted, weight, coupling, field, coef, matrix, across, around, first_swap, second_swap, new, ghost, low, high):
    settle(ids, first_swap, second_swap, low, high)
    lanes = lanes_of((ROWS, 128))
    left, right = sides(step, ids, around)
    new_inlet, new_outlet = ends_of(step, ids, wanted, weight, coupling, field, coef, matrix, across, around, low, high, ghost)
    for v in range(NV):
        new[v, 0] = new_inlet[v]
        new[v, PLANES - 1] = new_outlet[v]

    def one(k, carry):
        before, here = carry
        after = [field[v, k + 1] for v in range(NV)]
        total = advance(k, before, here, after, coef, matrix, left, right, low, high)
        for v in range(NV):
            new[v, k] = total[v]
        return here, after

    carry = ([field[v, 0] for v in range(NV)], [field[v, 1] for v in range(NV)])
    lax.fori_loop(1, PLANES - 1, one, carry)


def body(
    state,
    volume,
    face_axial,
    face_radial,
    face_circum,
    viscosity,
    flux_matrix,
    inflow_plane,
    outflow_plane,
    down_donors,
    up_donors,
    pressure_weight,
    boundary_coupling,
):
    sections, row_size, rad_size = lax.axis_size("sec"), lax.axis_size("row"), lax.axis_size("rad")
    ids = jnp.stack(
        [
            lax.axis_index("sec"),
            lax.axis_index("row"),
            lax.axis_index("rad"),
            jnp.int32(rad_size),
            jnp.int32(sections),
            jnp.int32(row_size),
        ]
    ).astype(jnp.int32)
    own = [state[:, 0], volume[0], face_axial[0], face_radial[0], face_circum[0], viscosity[0]]
    matrix = jnp.broadcast_to(jnp.pad(flux_matrix[0].reshape(75), (0, 5))[:, None], (80, 128))
    extended = (NV, PLANES, ROWS, 128)
    strips = (2, ROWS, 128)
    sent = (FIELD_ROWS + 32, 128)
    scalars = [pressure_weight, boundary_coupling]

    beside = pl.pallas_call(
        beside_kernel,
        out_shape=jax.ShapeDtypeStruct((NV + 1, 8, 128), jnp.float32),
        in_specs=[smem(), hbm()],
        out_specs=vmem(),
        scratch_shapes=[pltpu.VMEM((NV, 8, 128), jnp.float32), pltpu.SemaphoreType.DMA((2,))],
        name="beside",
        compiler_params=pltpu.CompilerParams(vmem_limit_bytes=FAR_LIMIT),
        interpret=INTERPRET,
    )(pressure_weight, own[0])
    out_pressure, lists, first_swap, second_swap = call(
        first_kernel,
        [(8, 128), (row_size, 16, 128), sent, sent],
        [ids, pressure_weight, down_donors[0], up_donors[0]],
        [],
        far=[own[0], own[3], own[4], own[5], outflow_plane],
    )

    def swaps(size, begin):
        return [pair for i in range(begin, size - 1, 2) for pair in ((i, i + 1), (i + 1, i))]

    table = lax.all_to_all(lists, "row", 0, 0)
    wanted = table[:, 0, :16].astype(jnp.int32)
    field = own[0]
    coef = edges = None
    for step in range(STEPS):
        last_step = step == STEPS - 1
        one_way = lax.ppermute(beside, "sec", swaps(sections, 0))
        other_way = lax.ppermute(beside, "sec", swaps(sections, 1))
        (send,) = call(
            gather_kernel,
            [(rad_size, TILE_ROWS, 128)],
            [ids],
            [one_way, other_way, inflow_plane, out_pressure, edges if step else table],
        )
        got = lax.all_to_all(send, "rad", 0, 0)
        high = lax.ppermute(second_swap, "rad", swaps(rad_size, 1))
        low = lax.ppermute(first_swap, "rad", swaps(rad_size, 0))
        strip = [pltpu.VMEM(low.shape, jnp.float32)] * 2
        if step == 0:
            (coef,) = call(coef_kernel, [(13, PLANES, ROWS, 128)], [ids], own[1:] + [table, low, high], scratch=strip)
        (send,) = call(
            functools.partial(select_kernel, step),
            [(row_size, TILE_ROWS + (ROWS if step else 0), 128)],
            [ids, wanted],
            [got, edges] if step else [got],
        )
        across = lax.all_to_all(send, "row", 0, 0)
        around = across if step else table
        ghost = [pltpu.VMEM((NV + 1, ROWS, 128), jnp.float32)]
        if last_step:
            (field,) = call(
                functools.partial(last_kernel, step),
                [(NV, PLANES, 8, 128)],
                [ids, wanted] + scalars,
                [field, coef, matrix, across, around, low, high],
                flops=PLANES * ROWS * 128 * 300,
                scratch=ghost + strip,
            )
        else:
            ends, beside = call(
                functools.partial(ends_kernel, step),
                [(2, NV, ROWS, 128), (NV + 1, 8, 128)],
                [ids, wanted] + scalars,
                [field, coef, matrix, across, around, low, high],
                flops=2 * ROWS * 128 * 300,
                scratch=ghost + strip,
            )
            field, edges, first_swap, second_swap = call(
                functools.partial(bulk_kernel, step),
                [extended, strips, (FIELD_ROWS, 128), (FIELD_ROWS, 128)],
                [ids],
                [field, coef, matrix, around, low, high, ends],
                scratch=strip,
                flops=PLANES * ROWS * 128 * 300,
            )
    return field[:, None]


def solution(mesh):
    in_specs = (
        P(None, "sec", None, "rad", "row"),
        P("sec", None, "rad", "row"),
        P("sec", None, "rad", "row"),
        P("sec", None, "rad", "row"),
        P("sec", None, "rad", "row"),
        P("sec", None, "rad", "row"),
        P("sec", None, None, None),
        P(None, "rad", "row"),
        P(None, "rad", "row"),
        P("sec", ("row", "rad")),
        P("sec", ("row", "rad")),
        P(),
        P(),
    )
    out_specs = P(None, "sec", None, "rad", "row")

    return jax.shard_map(body, mesh=mesh, in_specs=in_specs, out_specs=out_specs, check_vma=False)
```

```python
import functools

import jax
import jax.numpy as jnp
from jax import lax
from jax.experimental import pallas as pl
from jax.experimental.pallas import tpu as pltpu
from jax.sharding import PartitionSpec as P


STEPS = 4
time_step = 0.08
INTERPRET = False
VMEM_LIMIT = 8 * 1024 * 1024
FAR_LIMIT = 60 * 1024 * 1024

NV = 5
ROWS = 8
FIELD_ROWS = 80
PLANES = 16
TILE_ROWS = 48


def vmem():
    return pl.BlockSpec(memory_space=pltpu.VMEM)


def smem():
    return pl.BlockSpec(memory_space=pltpu.SMEM)


def hbm():
    return pl.BlockSpec(memory_space=pltpu.HBM)


def call(kernel, outs, scalars, arrays, flops=0, scratch=(), far=()):
    moved = sum(a.size * 4 for a in arrays) + sum(4 * functools.reduce(lambda x, y: x * y, o) for o in outs)
    scratch = list(scratch)
    if far:
        scratch += [pltpu.VMEM(a.shape, jnp.float32) for a in far] + [pltpu.SemaphoreType.DMA((len(far),))]
    return pl.pallas_call(
        kernel,
        out_shape=[jax.ShapeDtypeStruct(o, jnp.float32) for o in outs],
        in_specs=[smem() for _ in scalars] + [vmem() for _ in arrays] + [hbm() for _ in far],
        out_specs=[vmem() for _ in outs],
        scratch_shapes=scratch,
        compiler_params=pltpu.CompilerParams(vmem_limit_bytes=FAR_LIMIT if far else VMEM_LIMIT),
        cost_estimate=pl.CostEstimate(flops=flops, bytes_accessed=moved, transcendentals=0),
        interpret=INTERPRET,
    )(*scalars, *arrays, *far)


def lanes_of(shape):
    return lax.broadcasted_iota(jnp.int32, shape, 1)


def rows_of(shape):
    return lax.broadcasted_iota(jnp.int32, shape, 0)


def roll(x, by, axis):
    size = x.shape[axis]
    if not isinstance(by, int):
        return pltpu.roll(x, lax.rem(by + 2 * size, size), axis)
    by %= size
    return x if by == 0 else pltpu.roll(x, by, axis)


def pressure(weight_ref, values):
    total = weight_ref[0] * values[0]
    for v in range(1, NV):
        total = total + weight_ref[v] * values[v]
    return total


def fetch(sources, targets, sems):
    copies = [pltpu.make_async_copy(a, b, sems.at[i]) for i, (a, b) in enumerate(zip(sources, targets))]
    for copy in copies:
        copy.start()
    for copy in copies:
        copy.wait()


def beside_kernel(weight, state_hbm, beside, inlet, sem):
    copies = [
        pltpu.make_async_copy(state_hbm.at[:, PLANES - 1], beside.at[pl.ds(0, NV)], sem.at[0]),
        pltpu.make_async_copy(state_hbm.at[:, 0], inlet, sem.at[1]),
    ]
    for copy in copies:
        copy.start()
    for copy in copies:
        copy.wait()
    beside[NV] = pressure(weight, [inlet[v] for v in range(NV)])


def first_kernel(ids, weight, down_donors, up_donors, *refs):
    sources, (out_pressure, send, first_swap, second_swap), targets, sems = refs[:5], refs[5:9], refs[9:14], refs[14]
    fetch(sources, targets, sems)
    state, radial, circ, mu, outflow = targets
    lanes = lanes_of((8, 128))
    row, size = ids[1], send.shape[0]
    out_pressure[...] = pressure(weight, [outflow[v] for v in range(NV)])
    listed = jnp.zeros((8, 128), jnp.int32)
    for a in range(8):
        listed = jnp.where(lanes == a, down_donors[a], listed)
        listed = jnp.where(lanes == 8 + a, up_donors[a], listed)
    listed = listed.astype(jnp.float32)
    for j in range(size):
        send[j, 0:8, :] = listed

    even = lax.rem(ids[2], 2) == 0

    def put(at, cell):
        first_swap[pl.ds(at, 1), :] = jnp.where(even, cell[7:8], cell[0:1])
        second_swap[pl.ds(at, 1), :] = jnp.where(even, cell[0:1], cell[7:8])

    def one(k, carry):
        last, first = carry
        for v in range(NV):
            cell = state[v, k]
            at = v * 16 + k
            put(at, cell)
            here = lanes == at
            last = jnp.where(here, roll(cell, at + 1, 1), last)
            first = jnp.where(here, roll(cell, at, 1), first)
        put(FIELD_ROWS + k, mu[k])
        put(FIELD_ROWS + 16 + k, radial[k])
        here = lanes == 80 + k
        last = jnp.where(here, roll(mu[k], 81 + k, 1), last)
        first = jnp.where(here, roll(mu[k], 80 + k, 1), first)
        last = jnp.where(lanes == 96 + k, roll(circ[k], 97 + k, 1), last)
        return last, first

    zero = jnp.zeros((8, 128), jnp.float32)
    last, first = lax.fori_loop(0, PLANES, one, (zero, zero))
    send[lax.rem(row + 1, size), 8:16, :] = last
    send[lax.rem(row + size - 1, size), 8:16, :] = first


def gather_kernel(ids, one_way, other_way, inflow, out_pressure, *refs):
    send = refs[-1]
    if len(refs) > 1:
        ends, rad = refs[0], ids[2]
        for target, row, inside in ((rad + 1, 7, rad < send.shape[0] - 1), (rad - 1, 0, rad > 0)):

            @pl.when(inside)
            def _():
                for n in range(2):
                    for v in range(NV):
                        at = TILE_ROWS + n * NV + v
                        spot = jnp.clip(target, 0, send.shape[0] - 1)
                        send[spot, at : at + 1, :] = ends[n, v, row : row + 1, :]

    section = ids[0]
    odd = lax.rem(section, 2) == 1
    size = send.shape[0]
    for v in range(NV):
        value = jnp.where(section == 0, inflow[v], jnp.where(odd, one_way[v], other_way[v]))
        for j in range(size):
            send[j, v * 8 : v * 8 + 8, :] = value
    value = jnp.where(section == ids[4] - 1, out_pressure[...], jnp.where(odd, other_way[NV], one_way[NV]))
    for j in range(size):
        send[j, 40:48, :] = value


def select_kernel(step, ids, wanted, got, *refs):
    send = refs[-1]
    size = send.shape[0]
    row = ids[1]

    def one(j, carry):
        for a in range(8):
            d = wanted[j, a] & 63
            r, b = d >> 3, d & 7
            for v in range(NV):
                send[j, v * 8 + a : v * 8 + a + 1, :] = got[r, pl.ds(v * 8 + b, 1), :]
            e = wanted[j, 8 + a] & 63
            send[j, 40 + a : 41 + a, :] = got[e >> 3, pl.ds(40 + (e & 7), 1), :]
        return carry

    lax.fori_loop(0, size, one, 0)
    if step:
        edges = refs[0]
        send[lax.rem(row + 1, size), 48:56, :] = edges[0]
        send[lax.rem(row + size - 1, size), 48:56, :] = edges[1]


def sides(step, ids, around):
    base = 48 if step else 8
    row, row_size = ids[1], ids[5]
    left = around[lax.rem(row + row_size - 1, row_size), base : base + ROWS, :]
    right = around[lax.rem(row + 1, row_size), base : base + ROWS, :]
    return left, right


def settle(ids, first_swap, second_swap, low, high):
    even = lax.rem(ids[2], 2) == 0
    low[...] = jnp.where(even, second_swap[...], first_swap[...])
    high[...] = jnp.where(even, first_swap[...], second_swap[...])


def beyond(ref, at):
    return jnp.broadcast_to(ref[pl.ds(at, 1), :], (ROWS, 128))


def coef_kernel(ids, volume, axial, radial, circ, mu, around, first_swap, second_swap, coef, low, high):
    settle(ids, first_swap, second_swap, low, high)
    rad, rad_size = ids[2], ids[3]
    lanes = lanes_of((ROWS, 128))
    rows = rows_of((ROWS, 128))
    casing = jnp.logical_and(rad == rad_size - 1, rows == 7)
    left, right = sides(0, ids, around)

    def one(k, carry):
        m = mu[k]
        c = time_step / volume[k]
        half = 0.5 * c
        diffused = []

        def put(at, area, viscous):
            coef[at, k] = half * area
            b = c * area * viscous
            coef[at + 1, k] = b
            diffused.append(b)

        lower, upper = jnp.maximum(k - 1, 0), jnp.minimum(k + 1, PLANES - 1)
        put(0, axial[lower], 0.5 * (m + mu[lower]))
        put(2, axial[k], 0.5 * (m + mu[upper]))
        face = jnp.where(casing, 0.0, radial[k])
        face_below = jnp.where(rows == 0, beyond(low, FIELD_ROWS + 16 + k), roll(face, 1, 0))
        mu_below = jnp.where(rows == 0, beyond(low, FIELD_ROWS + k), roll(m, 1, 0))
        mu_above = jnp.where(rows == 7, beyond(high, FIELD_ROWS + k), roll(m, 7, 0))
        put(4, face_below, 0.5 * (m + mu_below))
        put(6, face, 0.5 * (m + mu_above))
        ring = circ[k]
        at = 80 + k
        mu_left = jnp.where(lanes == 0, roll(left, -at, 1), roll(m, 1, 1))
        mu_right = jnp.where(lanes == 127, roll(right, 127 - at, 1), roll(m, 127, 1))
        circ_left = jnp.where(lanes == 0, roll(left, -(at + 16), 1), roll(ring, 1, 1))
        put(8, circ_left, 0.5 * (mu_left + m))
        put(10, ring, 0.5 * (m + mu_right))
        total = diffused[0]
        for b in diffused[1:]:
            total = total + b
        coef[12, k] = 1.0 - total
        return carry

    lax.fori_loop(0, PLANES, one, 0)


def advance(k, before, here, after, coef, matrix, left, right, low, high):
    lanes = lanes_of((ROWS, 128))
    rows = rows_of((ROWS, 128))
    rest = coef[12, k]
    total = [rest * here[v] for v in range(NV)]
    for d in range(3):
        low_a, low_b = coef[4 * d, k], coef[4 * d + 1, k]
        high_a, high_b = coef[4 * d + 2, k], coef[4 * d + 3, k]
        own_a = high_a - low_a
        mixed = []
        for v in range(NV):
            cell = here[v]
            at = v * 16 + k
            if d == 0:
                lower, upper = before[v], after[v]
            elif d == 1:
                lower = jnp.where(rows == 0, beyond(low, at), roll(cell, 1, 0))
                upper = jnp.where(rows == 7, beyond(high, at), roll(cell, 7, 0))
            else:
                lower = jnp.where(lanes == 0, roll(left, -at, 1), roll(cell, 1, 1))
                upper = jnp.where(lanes == 127, roll(right, 127 - at, 1), roll(cell, 127, 1))
            mixed.append(high_a * upper - low_a * lower + own_a * cell)
            total[v] = total[v] + (high_b * upper + low_b * lower)
        for u in range(NV):
            for v in range(NV):
                at = 25 * d + 5 * u + v
                total[u] = total[u] - jnp.broadcast_to(matrix[at : at + 1, :], (ROWS, 128)) * mixed[v]
    return total


def ghosts_of(ids, wanted, weight, coupling, field, across, ghost):
    for a in range(8):
        d = wanted[ids[1], a] >> 6
        for v in range(NV):
            ghost[v, a : a + 1, :] = across[d, v * 8 + a : v * 8 + a + 1, :]
        e = wanted[ids[1], 8 + a] >> 6
        ghost[NV, a : a + 1, :] = across[e, 40 + a : 41 + a, :]
    outlet = [field[v, PLANES - 1] for v in range(NV)]
    jump = ghost[NV] - pressure(weight, outlet)
    return [ghost[v] for v in range(NV)], [outlet[v] + coupling[v] * jump for v in range(NV)]


def ends_of(step, ids, wanted, weight, coupling, field, coef, matrix, across, around, low, high, ghost):
    lanes = lanes_of((ROWS, 128))
    left, right = sides(step, ids, around)
    inlet_ghost, outlet_ghost = ghosts_of(ids, wanted, weight, coupling, field, across, ghost)
    plane = lambda k: [field[v, k] for v in range(NV)]
    new_inlet = advance(0, inlet_ghost, plane(0), plane(1), coef, matrix, left, right, low, high)
    last = PLANES - 1
    new_outlet = advance(last, plane(last - 1), plane(last), outlet_ghost, coef, matrix, left, right, low, high)
    return new_inlet, new_outlet


def ends_kernel(step, ids, wanted, weight, coupling, field, coef, matrix, across, around, *refs):
    ends, beside, ghost, low, high = refs[-5:]
    if step == 0:
        settle(ids, refs[0], refs[1], low, high)
    else:
        got, rad = refs[0], ids[2]
        size = got.shape[0]
        below, above = jnp.maximum(rad - 1, 0), jnp.minimum(rad + 1, size - 1)
        for n, k in enumerate((0, PLANES - 1)):
            for v in range(NV):
                at, spot = TILE_ROWS + n * NV + v, v * 16 + k
                low[spot : spot + 1, :] = jnp.where(rad == 0, 0.0, got[below, at : at + 1, :])
                high[spot : spot + 1, :] = jnp.where(rad == size - 1, 0.0, got[above, at : at + 1, :])
    new_inlet, new_outlet = ends_of(step, ids, wanted, weight, coupling, field, coef, matrix, across, around, low, high, ghost)
    for v in range(NV):
        ends[0, v] = new_inlet[v]
        ends[1, v] = new_outlet[v]
        beside[v] = new_outlet[v]
    beside[NV] = pressure(weight, new_inlet)


def bulk_kernel(step, ids, field, coef, matrix, around, from_first, from_second, ends, new, *refs):
    low, high = refs[-2:]
    if len(refs) > 2:
        edges, first_swap, second_swap = refs[:3]
    settle(ids, from_first, from_second, low, high)
    even = lax.rem(ids[2], 2) == 0
    lanes = lanes_of((ROWS, 128))
    left, right = sides(step, ids, around)

    def note(k, total, last, first):
        for v in range(NV):
            new[v, k] = total[v]
            if len(refs) == 2:
                continue
            at = v * 16 + k
            first_swap[pl.ds(at, 1), :] = jnp.where(even, total[v][7:8], total[v][0:1])
            second_swap[pl.ds(at, 1), :] = jnp.where(even, total[v][0:1], total[v][7:8])
            spot = lanes == at
            last = jnp.where(spot, roll(total[v], at + 1, 1), last)
            first = jnp.where(spot, roll(total[v], at, 1), first)
        return last, first

    def one(k, carry):
        before, here, last, first = carry
        after = [field[v, k + 1] for v in range(NV)]
        total = advance(k, before, here, after, coef, matrix, left, right, low, high)
        last, first = note(k, total, last, first)
        return here, after, last, first

    zero = jnp.zeros((ROWS, 128), jnp.float32)
    last, first = note(0, [ends[0, v] for v in range(NV)], zero, zero)
    last, first = note(PLANES - 1, [ends[1, v] for v in range(NV)], last, first)
    carry = ([field[v, 0] for v in range(NV)], [field[v, 1] for v in range(NV)], last, first)
    _, _, last, first = lax.fori_loop(1, PLANES - 1, one, carry)
    if len(refs) > 2:
        edges[0] = last
        edges[1] = first


def body(
    state,
    volume,
    face_axial,
    face_radial,
    face_circum,
    viscosity,
    flux_matrix,
    inflow_plane,
    outflow_plane,
    down_donors,
    up_donors,
    pressure_weight,
    boundary_coupling,
):
    sections, row_size, rad_size = lax.axis_size("sec"), lax.axis_size("row"), lax.axis_size("rad")
    ids = jnp.stack(
        [
            lax.axis_index("sec"),
            lax.axis_index("row"),
            lax.axis_index("rad"),
            jnp.int32(rad_size),
            jnp.int32(sections),
            jnp.int32(row_size),
        ]
    ).astype(jnp.int32)
    own = [state[:, 0], volume[0], face_axial[0], face_radial[0], face_circum[0], viscosity[0]]
    matrix = jnp.broadcast_to(jnp.pad(flux_matrix[0].reshape(75), (0, 5))[:, None], (80, 128))
    extended = (NV, PLANES, ROWS, 128)
    strips = (2, ROWS, 128)
    sent = (FIELD_ROWS + 32, 128)
    scalars = [pressure_weight, boundary_coupling]

    beside = pl.pallas_call(
        beside_kernel,
        out_shape=jax.ShapeDtypeStruct((NV + 1, 8, 128), jnp.float32),
        in_specs=[smem(), hbm()],
        out_specs=vmem(),
        scratch_shapes=[pltpu.VMEM((NV, 8, 128), jnp.float32), pltpu.SemaphoreType.DMA((2,))],
        name="beside",
        compiler_params=pltpu.CompilerParams(vmem_limit_bytes=FAR_LIMIT),
        interpret=INTERPRET,
    )(pressure_weight, own[0])
    out_pressure, lists, first_swap, second_swap = call(
        first_kernel,
        [(8, 128), (row_size, 16, 128), sent, sent],
        [ids, pressure_weight, down_donors[0], up_donors[0]],
        [],
        far=[own[0], own[3], own[4], own[5], outflow_plane],
    )

    def swaps(size, begin):
        return [pair for i in range(begin, size - 1, 2) for pair in ((i, i + 1), (i + 1, i))]

    table = lax.all_to_all(lists, "row", 0, 0)
    wanted = table[:, 0, :16].astype(jnp.int32)
    field = own[0]
    coef = edges = None
    for step in range(STEPS):
        last_step = step == STEPS - 1
        one_way = lax.ppermute(beside, "sec", swaps(sections, 0))
        other_way = lax.ppermute(beside, "sec", swaps(sections, 1))
        (send,) = call(
            gather_kernel,
            [(rad_size, TILE_ROWS + (16 if step else 0), 128)],
            [ids],
            [one_way, other_way, inflow_plane, out_pressure] + ([ends] if step else []),
        )
        got = lax.all_to_all(send, "rad", 0, 0)
        high = lax.ppermute(second_swap, "rad", swaps(rad_size, 1))
        low = lax.ppermute(first_swap, "rad", swaps(rad_size, 0))
        strip = [pltpu.VMEM(low.shape, jnp.float32)] * 2
        if step == 0:
            (coef,) = call(coef_kernel, [(13, PLANES, ROWS, 128)], [ids], own[1:] + [table, low, high], scratch=strip)
        (send,) = call(
            functools.partial(select_kernel, step),
            [(row_size, TILE_ROWS + (ROWS if step else 0), 128)],
            [ids, wanted],
            [got, edges] if step else [got],
        )
        across = lax.all_to_all(send, "row", 0, 0)
        around = across if step else table
        ghost = [pltpu.VMEM((NV + 1, ROWS, 128), jnp.float32)]
        ends, beside = call(
            functools.partial(ends_kernel, step),
            [(2, NV, ROWS, 128), (NV + 1, 8, 128)],
            [ids, wanted] + scalars,
            [field, coef, matrix, across, around] + ([got] if step else [low, high]),
            flops=2 * ROWS * 128 * 300,
            scratch=ghost + strip,
        )
        result = call(
            functools.partial(bulk_kernel, step),
            [extended] + ([] if last_step else [strips, (FIELD_ROWS, 128), (FIELD_ROWS, 128)]),
            [ids],
            [field, coef, matrix, around, low, high, ends],
            flops=PLANES * ROWS * 128 * 300,
            scratch=strip,
        )
        field = result[0]
        if not last_step:
            edges, first_swap, second_swap = result[1:]
    return field[:, None]


def solution(mesh):
    in_specs = (
        P(None, "sec", None, "rad", "row"),
        P("sec", None, "rad", "row"),
        P("sec", None, "rad", "row"),
        P("sec", None, "rad", "row"),
        P("sec", None, "rad", "row"),
        P("sec", None, "rad", "row"),
        P("sec", None, None, None),
        P(None, "rad", "row"),
        P(None, "rad", "row"),
        P("sec", ("row", "rad")),
        P("sec", ("row", "rad")),
        P(),
        P(),
    )
    out_specs = P(None, "sec", None, "rad", "row")

    return jax.shard_map(body, mesh=mesh, in_specs=in_specs, out_specs=out_specs, check_vma=False)
```

```python
import functools

import jax
import jax.numpy as jnp
from jax import lax
from jax.experimental import pallas as pl
from jax.experimental.pallas import tpu as pltpu
from jax.sharding import PartitionSpec as P


STEPS = 4
time_step = 0.08
INTERPRET = False
VMEM_LIMIT = 8 * 1024 * 1024
FAR_LIMIT = 60 * 1024 * 1024

NV = 5
ROWS = 8
FIELD_ROWS = 80
PLANES = 16
TILE_ROWS = 48


def vmem():
    return pl.BlockSpec(memory_space=pltpu.VMEM)


def smem():
    return pl.BlockSpec(memory_space=pltpu.SMEM)


def hbm():
    return pl.BlockSpec(memory_space=pltpu.HBM)


def call(kernel, outs, scalars, arrays, flops=0, scratch=(), far=()):
    moved = sum(a.size * 4 for a in arrays) + sum(4 * functools.reduce(lambda x, y: x * y, o) for o in outs)
    scratch = list(scratch)
    if far:
        scratch += [pltpu.VMEM(a.shape, jnp.float32) for a in far] + [pltpu.SemaphoreType.DMA((len(far),))]
    return pl.pallas_call(
        kernel,
        out_shape=[jax.ShapeDtypeStruct(o, jnp.float32) for o in outs],
        in_specs=[smem() for _ in scalars] + [vmem() for _ in arrays] + [hbm() for _ in far],
        out_specs=[vmem() for _ in outs],
        scratch_shapes=scratch,
        compiler_params=pltpu.CompilerParams(vmem_limit_bytes=FAR_LIMIT if far else VMEM_LIMIT),
        cost_estimate=pl.CostEstimate(flops=flops, bytes_accessed=moved, transcendentals=0),
        interpret=INTERPRET,
    )(*scalars, *arrays, *far)


def lanes_of(shape):
    return lax.broadcasted_iota(jnp.int32, shape, 1)


def rows_of(shape):
    return lax.broadcasted_iota(jnp.int32, shape, 0)


def roll(x, by, axis):
    size = x.shape[axis]
    if not isinstance(by, int):
        return pltpu.roll(x, lax.rem(by + 2 * size, size), axis)
    by %= size
    return x if by == 0 else pltpu.roll(x, by, axis)


def pressure(weight_ref, values):
    total = weight_ref[0] * values[0]
    for v in range(1, NV):
        total = total + weight_ref[v] * values[v]
    return total


def fetch(sources, targets, sems):
    copies = [pltpu.make_async_copy(a, b, sems.at[i]) for i, (a, b) in enumerate(zip(sources, targets))]
    for copy in copies:
        copy.start()
    for copy in copies:
        copy.wait()


def beside_kernel(weight, state_hbm, beside, inlet, sem):
    copies = [
        pltpu.make_async_copy(state_hbm.at[:, PLANES - 1], beside.at[pl.ds(0, NV)], sem.at[0]),
        pltpu.make_async_copy(state_hbm.at[:, 0], inlet, sem.at[1]),
    ]
    for copy in copies:
        copy.start()
    for copy in copies:
        copy.wait()
    beside[NV] = pressure(weight, [inlet[v] for v in range(NV)])


def first_kernel(ids, weight, down_donors, up_donors, *refs):
    sources, (out_pressure, send, first_swap, second_swap), targets, sems = refs[:5], refs[5:9], refs[9:14], refs[14]
    fetch(sources, targets, sems)
    state, radial, circ, mu, outflow = targets
    lanes = lanes_of((8, 128))
    row, size = ids[1], send.shape[0]
    out_pressure[...] = pressure(weight, [outflow[v] for v in range(NV)])
    listed = jnp.zeros((8, 128), jnp.int32)
    for a in range(8):
        listed = jnp.where(lanes == a, down_donors[a], listed)
        listed = jnp.where(lanes == 8 + a, up_donors[a], listed)
    listed = listed.astype(jnp.float32)
    for j in range(size):
        send[j, 0:8, :] = listed

    even = lax.rem(ids[2], 2) == 0

    def put(at, cell):
        first_swap[pl.ds(at, 1), :] = jnp.where(even, cell[7:8], cell[0:1])
        second_swap[pl.ds(at, 1), :] = jnp.where(even, cell[0:1], cell[7:8])

    def one(k, carry):
        last, first = carry
        for v in range(NV):
            cell = state[v, k]
            at = v * 16 + k
            put(at, cell)
            here = lanes == at
            last = jnp.where(here, roll(cell, at + 1, 1), last)
            first = jnp.where(here, roll(cell, at, 1), first)
        put(FIELD_ROWS + k, mu[k])
        put(FIELD_ROWS + 16 + k, radial[k])
        here = lanes == 80 + k
        last = jnp.where(here, roll(mu[k], 81 + k, 1), last)
        first = jnp.where(here, roll(mu[k], 80 + k, 1), first)
        last = jnp.where(lanes == 96 + k, roll(circ[k], 97 + k, 1), last)
        return last, first

    zero = jnp.zeros((8, 128), jnp.float32)
    last, first = lax.fori_loop(0, PLANES, one, (zero, zero), unroll=2)
    send[lax.rem(row + 1, size), 8:16, :] = last
    send[lax.rem(row + size - 1, size), 8:16, :] = first


def gather_kernel(ids, one_way, other_way, inflow, out_pressure, *refs):
    send = refs[-1]
    if len(refs) > 1:
        ends, rad = refs[0], ids[2]
        for target, row, inside in ((rad + 1, 7, rad < send.shape[0] - 1), (rad - 1, 0, rad > 0)):

            @pl.when(inside)
            def _():
                for n in range(2):
                    for v in range(NV):
                        at = TILE_ROWS + n * NV + v
                        spot = jnp.clip(target, 0, send.shape[0] - 1)
                        send[spot, at : at + 1, :] = ends[n, v, row : row + 1, :]

    section = ids[0]
    odd = lax.rem(section, 2) == 1
    size = send.shape[0]
    for v in range(NV):
        value = jnp.where(section == 0, inflow[v], jnp.where(odd, one_way[v], other_way[v]))
        for j in range(size):
            send[j, v * 8 : v * 8 + 8, :] = value
    value = jnp.where(section == ids[4] - 1, out_pressure[...], jnp.where(odd, other_way[NV], one_way[NV]))
    for j in range(size):
        send[j, 40:48, :] = value


def select_kernel(step, ids, wanted, got, *refs):
    send = refs[-1]
    size = send.shape[0]
    row = ids[1]

    def one(j, carry):
        for a in range(8):
            d = wanted[j, a] & 63
            r, b = d >> 3, d & 7
            for v in range(NV):
                send[j, v * 8 + a : v * 8 + a + 1, :] = got[r, pl.ds(v * 8 + b, 1), :]
            e = wanted[j, 8 + a] & 63
            send[j, 40 + a : 41 + a, :] = got[e >> 3, pl.ds(40 + (e & 7), 1), :]
        return carry

    lax.fori_loop(0, size, one, 0)
    if step:
        edges = refs[0]
        send[lax.rem(row + 1, size), 48:56, :] = edges[0]
        send[lax.rem(row + size - 1, size), 48:56, :] = edges[1]


def sides(step, ids, around):
    base = 48 if step else 8
    row, row_size = ids[1], ids[5]
    left = around[lax.rem(row + row_size - 1, row_size), base : base + ROWS, :]
    right = around[lax.rem(row + 1, row_size), base : base + ROWS, :]
    return left, right


def settle(ids, first_swap, second_swap, low, high):
    even = lax.rem(ids[2], 2) == 0
    low[...] = jnp.where(even, second_swap[...], first_swap[...])
    high[...] = jnp.where(even, first_swap[...], second_swap[...])


def beyond(ref, at):
    return jnp.broadcast_to(ref[pl.ds(at, 1), :], (ROWS, 128))


def coef_kernel(ids, volume, axial, radial, circ, mu, around, first_swap, second_swap, coef, low, high):
    settle(ids, first_swap, second_swap, low, high)
    rad, rad_size = ids[2], ids[3]
    lanes = lanes_of((ROWS, 128))
    rows = rows_of((ROWS, 128))
    casing = jnp.logical_and(rad == rad_size - 1, rows == 7)
    left, right = sides(0, ids, around)

    def one(k, carry):
        m = mu[k]
        c = time_step / volume[k]
        half = 0.5 * c
        diffused = []

        def put(at, area, viscous):
            coef[at, k] = half * area
            b = c * area * viscous
            coef[at + 1, k] = b
            diffused.append(b)

        lower, upper = jnp.maximum(k - 1, 0), jnp.minimum(k + 1, PLANES - 1)
        put(0, axial[lower], 0.5 * (m + mu[lower]))
        put(2, axial[k], 0.5 * (m + mu[upper]))
        face = jnp.where(casing, 0.0, radial[k])
        face_below = jnp.where(rows == 0, beyond(low, FIELD_ROWS + 16 + k), roll(face, 1, 0))
        mu_below = jnp.where(rows == 0, beyond(low, FIELD_ROWS + k), roll(m, 1, 0))
        mu_above = jnp.where(rows == 7, beyond(high, FIELD_ROWS + k), roll(m, 7, 0))
        put(4, face_below, 0.5 * (m + mu_below))
        put(6, face, 0.5 * (m + mu_above))
        ring = circ[k]
        at = 80 + k
        mu_left = jnp.where(lanes == 0, roll(left, -at, 1), roll(m, 1, 1))
        mu_right = jnp.where(lanes == 127, roll(right, 127 - at, 1), roll(m, 127, 1))
        circ_left = jnp.where(lanes == 0, roll(left, -(at + 16), 1), roll(ring, 1, 1))
        put(8, circ_left, 0.5 * (mu_left + m))
        put(10, ring, 0.5 * (m + mu_right))
        total = diffused[0]
        for b in diffused[1:]:
            total = total + b
        coef[12, k] = 1.0 - total
        return carry

    lax.fori_loop(0, PLANES, one, 0, unroll=2)


def advance(k, before, here, after, coef, matrix, left, right, low, high):
    lanes = lanes_of((ROWS, 128))
    rows = rows_of((ROWS, 128))
    rest = coef[12, k]
    total = [rest * here[v] for v in range(NV)]
    for d in range(3):
        low_a, low_b = coef[4 * d, k], coef[4 * d + 1, k]
        high_a, high_b = coef[4 * d + 2, k], coef[4 * d + 3, k]
        own_a = high_a - low_a
        mixed = []
        for v in range(NV):
            cell = here[v]
            at = v * 16 + k
            if d == 0:
                lower, upper = before[v], after[v]
            elif d == 1:
                lower = jnp.where(rows == 0, beyond(low, at), roll(cell, 1, 0))
                upper = jnp.where(rows == 7, beyond(high, at), roll(cell, 7, 0))
            else:
                lower = jnp.where(lanes == 0, roll(left, -at, 1), roll(cell, 1, 1))
                upper = jnp.where(lanes == 127, roll(right, 127 - at, 1), roll(cell, 127, 1))
            mixed.append(high_a * upper - low_a * lower + own_a * cell)
            total[v] = total[v] + (high_b * upper + low_b * lower)
        for u in range(NV):
            for v in range(NV):
                at = 25 * d + 5 * u + v
                total[u] = total[u] - jnp.broadcast_to(matrix[at : at + 1, :], (ROWS, 128)) * mixed[v]
    return total


def ghosts_of(ids, wanted, weight, coupling, field, across, ghost):
    for a in range(8):
        d = wanted[ids[1], a] >> 6
        for v in range(NV):
            ghost[v, a : a + 1, :] = across[d, v * 8 + a : v * 8 + a + 1, :]
        e = wanted[ids[1], 8 + a] >> 6
        ghost[NV, a : a + 1, :] = across[e, 40 + a : 41 + a, :]
    outlet = [field[v, PLANES - 1] for v in range(NV)]
    jump = ghost[NV] - pressure(weight, outlet)
    return [ghost[v] for v in range(NV)], [outlet[v] + coupling[v] * jump for v in range(NV)]


def ends_of(step, ids, wanted, weight, coupling, field, coef, matrix, across, around, low, high, ghost):
    lanes = lanes_of((ROWS, 128))
    left, right = sides(step, ids, around)
    inlet_ghost, outlet_ghost = ghosts_of(ids, wanted, weight, coupling, field, across, ghost)
    plane = lambda k: [field[v, k] for v in range(NV)]
    new_inlet = advance(0, inlet_ghost, plane(0), plane(1), coef, matrix, left, right, low, high)
    last = PLANES - 1
    new_outlet = advance(last, plane(last - 1), plane(last), outlet_ghost, coef, matrix, left, right, low, high)
    return new_inlet, new_outlet


def ends_kernel(step, ids, wanted, weight, coupling, field, coef, matrix, across, around, *refs):
    ends, beside, ghost, low, high = refs[-5:]
    if step == 0:
        settle(ids, refs[0], refs[1], low, high)
    else:
        got, rad = refs[0], ids[2]
        size = got.shape[0]
        below, above = jnp.maximum(rad - 1, 0), jnp.minimum(rad + 1, size - 1)
        for n, k in enumerate((0, PLANES - 1)):
            for v in range(NV):
                at, spot = TILE_ROWS + n * NV + v, v * 16 + k
                low[spot : spot + 1, :] = jnp.where(rad == 0, 0.0, got[below, at : at + 1, :])
                high[spot : spot + 1, :] = jnp.where(rad == size - 1, 0.0, got[above, at : at + 1, :])
    new_inlet, new_outlet = ends_of(step, ids, wanted, weight, coupling, field, coef, matrix, across, around, low, high, ghost)
    for v in range(NV):
        ends[0, v] = new_inlet[v]
        ends[1, v] = new_outlet[v]
        beside[v] = new_outlet[v]
    beside[NV] = pressure(weight, new_inlet)


def bulk_kernel(step, ids, field, coef, matrix, around, from_first, from_second, ends, new, *refs):
    low, high = refs[-2:]
    if len(refs) > 2:
        edges, first_swap, second_swap = refs[:3]
    settle(ids, from_first, from_second, low, high)
    even = lax.rem(ids[2], 2) == 0
    lanes = lanes_of((ROWS, 128))
    left, right = sides(step, ids, around)

    def note(k, total, last, first):
        for v in range(NV):
            new[v, k] = total[v]
            if len(refs) == 2:
                continue
            at = v * 16 + k
            first_swap[pl.ds(at, 1), :] = jnp.where(even, total[v][7:8], total[v][0:1])
            second_swap[pl.ds(at, 1), :] = jnp.where(even, total[v][0:1], total[v][7:8])
            spot = lanes == at
            last = jnp.where(spot, roll(total[v], at + 1, 1), last)
            first = jnp.where(spot, roll(total[v], at, 1), first)
        return last, first

    def one(k, carry):
        before, here, last, first = carry
        after = [field[v, k + 1] for v in range(NV)]
        total = advance(k, before, here, after, coef, matrix, left, right, low, high)
        last, first = note(k, total, last, first)
        return here, after, last, first

    zero = jnp.zeros((ROWS, 128), jnp.float32)
    last, first = note(0, [ends[0, v] for v in range(NV)], zero, zero)
    last, first = note(PLANES - 1, [ends[1, v] for v in range(NV)], last, first)
    carry = ([field[v, 0] for v in range(NV)], [field[v, 1] for v in range(NV)], last, first)
    _, _, last, first = lax.fori_loop(1, PLANES - 1, one, carry, unroll=2)
    if len(refs) > 2:
        edges[0] = last
        edges[1] = first


def body(
    state,
    volume,
    face_axial,
    face_radial,
    face_circum,
    viscosity,
    flux_matrix,
    inflow_plane,
    outflow_plane,
    down_donors,
    up_donors,
    pressure_weight,
    boundary_coupling,
):
    sections, row_size, rad_size = lax.axis_size("sec"), lax.axis_size("row"), lax.axis_size("rad")
    ids = jnp.stack(
        [
            lax.axis_index("sec"),
            lax.axis_index("row"),
            lax.axis_index("rad"),
            jnp.int32(rad_size),
            jnp.int32(sections),
            jnp.int32(row_size),
        ]
    ).astype(jnp.int32)
    own = [state[:, 0], volume[0], face_axial[0], face_radial[0], face_circum[0], viscosity[0]]
    matrix = jnp.broadcast_to(jnp.pad(flux_matrix[0].reshape(75), (0, 5))[:, None], (80, 128))
    extended = (NV, PLANES, ROWS, 128)
    strips = (2, ROWS, 128)
    sent = (FIELD_ROWS + 32, 128)
    scalars = [pressure_weight, boundary_coupling]

    beside = pl.pallas_call(
        beside_kernel,
        out_shape=jax.ShapeDtypeStruct((NV + 1, 8, 128), jnp.float32),
        in_specs=[smem(), hbm()],
        out_specs=vmem(),
        scratch_shapes=[pltpu.VMEM((NV, 8, 128), jnp.float32), pltpu.SemaphoreType.DMA((2,))],
        name="beside",
        compiler_params=pltpu.CompilerParams(vmem_limit_bytes=FAR_LIMIT),
        interpret=INTERPRET,
    )(pressure_weight, own[0])
    out_pressure, lists, first_swap, second_swap = call(
        first_kernel,
        [(8, 128), (row_size, 16, 128), sent, sent],
        [ids, pressure_weight, down_donors[0], up_donors[0]],
        [],
        far=[own[0], own[3], own[4], own[5], outflow_plane],
    )

    def swaps(size, begin):
        return [pair for i in range(begin, size - 1, 2) for pair in ((i, i + 1), (i + 1, i))]

    table = lax.all_to_all(lists, "row", 0, 0)
    wanted = table[:, 0, :16].astype(jnp.int32)
    field = own[0]
    coef = edges = None
    for step in range(STEPS):
        last_step = step == STEPS - 1
        one_way = lax.ppermute(beside, "sec", swaps(sections, 0))
        other_way = lax.ppermute(beside, "sec", swaps(sections, 1))
        (send,) = call(
            gather_kernel,
            [(rad_size, TILE_ROWS + (16 if step else 0), 128)],
            [ids],
            [one_way, other_way, inflow_plane, out_pressure] + ([ends] if step else []),
        )
        got = lax.all_to_all(send, "rad", 0, 0)
        high = lax.ppermute(second_swap, "rad", swaps(rad_size, 1))
        low = lax.ppermute(first_swap, "rad", swaps(rad_size, 0))
        strip = [pltpu.VMEM(low.shape, jnp.float32)] * 2
        if step == 0:
            (coef,) = call(coef_kernel, [(13, PLANES, ROWS, 128)], [ids], own[1:] + [table, low, high], scratch=strip)
        (send,) = call(
            functools.partial(select_kernel, step),
            [(row_size, TILE_ROWS + (ROWS if step else 0), 128)],
            [ids, wanted],
            [got, edges] if step else [got],
        )
        across = lax.all_to_all(send, "row", 0, 0)
        around = across if step else table
        ghost = [pltpu.VMEM((NV + 1, ROWS, 128), jnp.float32)]
        ends, beside = call(
            functools.partial(ends_kernel, step),
            [(2, NV, ROWS, 128), (NV + 1, 8, 128)],
            [ids, wanted] + scalars,
            [field, coef, matrix, across, around] + ([got] if step else [low, high]),
            flops=2 * ROWS * 128 * 300,
            scratch=ghost + strip,
        )
        result = call(
            functools.partial(bulk_kernel, step),
            [extended] + ([] if last_step else [strips, (FIELD_ROWS, 128), (FIELD_ROWS, 128)]),
            [ids],
            [field, coef, matrix, around, low, high, ends],
            flops=PLANES * ROWS * 128 * 300,
            scratch=strip,
        )
        field = result[0]
        if not last_step:
            edges, first_swap, second_swap = result[1:]
    return field[:, None]


def solution(mesh):
    in_specs = (
        P(None, "sec", None, "rad", "row"),
        P("sec", None, "rad", "row"),
        P("sec", None, "rad", "row"),
        P("sec", None, "rad", "row"),
        P("sec", None, "rad", "row"),
        P("sec", None, "rad", "row"),
        P("sec", None, None, None),
        P(None, "rad", "row"),
        P(None, "rad", "row"),
        P("sec", ("row", "rad")),
        P("sec", ("row", "rad")),
        P(),
        P(),
    )
    out_specs = P(None, "sec", None, "rad", "row")

    return jax.shard_map(body, mesh=mesh, in_specs=in_specs, out_specs=out_specs, check_vma=False)
```

```python
import functools

import jax
import jax.numpy as jnp
from jax import lax
from jax.experimental import pallas as pl
from jax.experimental.pallas import tpu as pltpu
from jax.sharding import PartitionSpec as P


STEPS = 4
time_step = 0.08
INTERPRET = False
VMEM_LIMIT = 8 * 1024 * 1024
FAR_LIMIT = 60 * 1024 * 1024

NV = 5
ROWS = 8
FIELD_ROWS = 80
PLANES = 16
TILE_ROWS = 48


def vmem():
    return pl.BlockSpec(memory_space=pltpu.VMEM)


def smem():
    return pl.BlockSpec(memory_space=pltpu.SMEM)


def hbm():
    return pl.BlockSpec(memory_space=pltpu.HBM)


def call(kernel, outs, scalars, arrays, flops=0, scratch=(), far=()):
    moved = sum(a.size * 4 for a in arrays) + sum(4 * functools.reduce(lambda x, y: x * y, o) for o in outs)
    scratch = list(scratch)
    if far:
        scratch += [pltpu.VMEM(a.shape, jnp.float32) for a in far] + [pltpu.SemaphoreType.DMA((len(far),))]
    return pl.pallas_call(
        kernel,
        out_shape=[jax.ShapeDtypeStruct(o, jnp.float32) for o in outs],
        in_specs=[smem() for _ in scalars] + [vmem() for _ in arrays] + [hbm() for _ in far],
        out_specs=[vmem() for _ in outs],
        scratch_shapes=scratch,
        compiler_params=pltpu.CompilerParams(vmem_limit_bytes=FAR_LIMIT if far else VMEM_LIMIT),
        cost_estimate=pl.CostEstimate(flops=flops, bytes_accessed=moved, transcendentals=0),
        interpret=INTERPRET,
    )(*scalars, *arrays, *far)


def lanes_of(shape):
    return lax.broadcasted_iota(jnp.int32, shape, 1)


def rows_of(shape):
    return lax.broadcasted_iota(jnp.int32, shape, 0)


def roll(x, by, axis):
    size = x.shape[axis]
    if not isinstance(by, int):
        return pltpu.roll(x, lax.rem(by + 2 * size, size), axis)
    by %= size
    return x if by == 0 else pltpu.roll(x, by, axis)


def pressure(weight_ref, values):
    total = weight_ref[0] * values[0]
    for v in range(1, NV):
        total = total + weight_ref[v] * values[v]
    return total


def fetch(sources, targets, sems):
    copies = [pltpu.make_async_copy(a, b, sems.at[i]) for i, (a, b) in enumerate(zip(sources, targets))]
    for copy in copies:
        copy.start()
    for copy in copies:
        copy.wait()


def first_kernel(ids, weight, down_donors, up_donors, *refs):
    sources, (beside, out_pressure, send, first_swap, second_swap), targets, sems = refs[:5], refs[5:10], refs[10:15], refs[15]
    fetch(sources, targets, sems)
    state, radial, circ, mu, outflow = targets
    lanes = lanes_of((8, 128))
    row, size = ids[1], send.shape[0]
    for v in range(NV):
        beside[v] = state[v, PLANES - 1]
    beside[NV] = pressure(weight, [state[v, 0] for v in range(NV)])
    out_pressure[...] = pressure(weight, [outflow[v] for v in range(NV)])
    listed = jnp.zeros((8, 128), jnp.int32)
    for a in range(8):
        listed = jnp.where(lanes == a, down_donors[a], listed)
        listed = jnp.where(lanes == 8 + a, up_donors[a], listed)
    listed = listed.astype(jnp.float32)
    for j in range(size):
        send[j, 0:8, :] = listed

    even = lax.rem(ids[2], 2) == 0

    def put(at, cell):
        first_swap[pl.ds(at, 1), :] = jnp.where(even, cell[7:8], cell[0:1])
        second_swap[pl.ds(at, 1), :] = jnp.where(even, cell[0:1], cell[7:8])

    def one(k, carry):
        last, first = carry
        for v in range(NV):
            cell = state[v, k]
            at = v * 16 + k
            put(at, cell)
            here = lanes == at
            last = jnp.where(here, roll(cell, at + 1, 1), last)
            first = jnp.where(here, roll(cell, at, 1), first)
        put(FIELD_ROWS + k, mu[k])
        put(FIELD_ROWS + 16 + k, radial[k])
        here = lanes == 80 + k
        last = jnp.where(here, roll(mu[k], 81 + k, 1), last)
        first = jnp.where(here, roll(mu[k], 80 + k, 1), first)
        last = jnp.where(lanes == 96 + k, roll(circ[k], 97 + k, 1), last)
        return last, first

    zero = jnp.zeros((8, 128), jnp.float32)
    last, first = lax.fori_loop(0, PLANES, one, (zero, zero), unroll=4)
    send[lax.rem(row + 1, size), 8:16, :] = last
    send[lax.rem(row + size - 1, size), 8:16, :] = first


def gather_kernel(ids, one_way, other_way, inflow, out_pressure, after, send):
    section = ids[0]
    odd = lax.rem(section, 2) == 1
    size = send.shape[0]
    for v in range(NV):
        value = jnp.where(section == 0, inflow[v], jnp.where(odd, one_way[v], other_way[v]))
        for j in range(size):
            send[j, v * 8 : v * 8 + 8, :] = value
    value = jnp.where(section == ids[4] - 1, out_pressure[...], jnp.where(odd, other_way[NV], one_way[NV]))
    for j in range(size):
        send[j, 40:48, :] = value


def select_kernel(step, ids, wanted, got, *refs):
    send = refs[-1]
    size = send.shape[0]
    row = ids[1]

    def one(j, carry):
        for a in range(8):
            d = wanted[j, a] & 63
            r, b = d >> 3, d & 7
            for v in range(NV):
                send[j, v * 8 + a : v * 8 + a + 1, :] = got[r, pl.ds(v * 8 + b, 1), :]
            e = wanted[j, 8 + a] & 63
            send[j, 40 + a : 41 + a, :] = got[e >> 3, pl.ds(40 + (e & 7), 1), :]
        return carry

    lax.fori_loop(0, size, one, 0, unroll=2)
    if step:
        edges = refs[0]
        send[lax.rem(row + 1, size), 48:56, :] = edges[0]
        send[lax.rem(row + size - 1, size), 48:56, :] = edges[1]


def sides(step, ids, around):
    base = 48 if step else 8
    row, row_size = ids[1], ids[5]
    left = around[lax.rem(row + row_size - 1, row_size), base : base + ROWS, :]
    right = around[lax.rem(row + 1, row_size), base : base + ROWS, :]
    return left, right


def settle(ids, first_swap, second_swap, low, high):
    even = lax.rem(ids[2], 2) == 0
    low[...] = jnp.where(even, second_swap[...], first_swap[...])
    high[...] = jnp.where(even, first_swap[...], second_swap[...])


def beyond(ref, at):
    return jnp.broadcast_to(ref[pl.ds(at, 1), :], (ROWS, 128))


def coef_kernel(ids, volume, axial, radial, circ, mu, around, first_swap, second_swap, coef, low, high):
    settle(ids, first_swap, second_swap, low, high)
    rad, rad_size = ids[2], ids[3]
    lanes = lanes_of((ROWS, 128))
    rows = rows_of((ROWS, 128))
    casing = jnp.logical_and(rad == rad_size - 1, rows == 7)
    left, right = sides(0, ids, around)

    def one(k, carry):
        m = mu[k]
        c = time_step / volume[k]
        half = 0.5 * c
        diffused = []

        def put(at, area, viscous):
            coef[at, k] = half * area
            b = c * area * viscous
            coef[at + 1, k] = b
            diffused.append(b)

        lower, upper = jnp.maximum(k - 1, 0), jnp.minimum(k + 1, PLANES - 1)
        put(0, axial[lower], 0.5 * (m + mu[lower]))
        put(2, axial[k], 0.5 * (m + mu[upper]))
        face = jnp.where(casing, 0.0, radial[k])
        face_below = jnp.where(rows == 0, beyond(low, FIELD_ROWS + 16 + k), roll(face, 1, 0))
        mu_below = jnp.where(rows == 0, beyond(low, FIELD_ROWS + k), roll(m, 1, 0))
        mu_above = jnp.where(rows == 7, beyond(high, FIELD_ROWS + k), roll(m, 7, 0))
        put(4, face_below, 0.5 * (m + mu_below))
        put(6, face, 0.5 * (m + mu_above))
        ring = circ[k]
        at = 80 + k
        mu_left = jnp.where(lanes == 0, roll(left, -at, 1), roll(m, 1, 1))
        mu_right = jnp.where(lanes == 127, roll(right, 127 - at, 1), roll(m, 127, 1))
        circ_left = jnp.where(lanes == 0, roll(left, -(at + 16), 1), roll(ring, 1, 1))
        put(8, circ_left, 0.5 * (mu_left + m))
        put(10, ring, 0.5 * (m + mu_right))
        total = diffused[0]
        for b in diffused[1:]:
            total = total + b
        coef[12, k] = 1.0 - total
        return carry

    lax.fori_loop(0, PLANES, one, 0, unroll=4)


def advance(k, before, here, after, coef, matrix, left, right, low, high):
    lanes = lanes_of((ROWS, 128))
    rows = rows_of((ROWS, 128))
    rest = coef[12, k]
    total = [rest * here[v] for v in range(NV)]
    for d in range(3):
        low_a, low_b = coef[4 * d, k], coef[4 * d + 1, k]
        high_a, high_b = coef[4 * d + 2, k], coef[4 * d + 3, k]
        own_a = high_a - low_a
        mixed = []
        for v in range(NV):
            cell = here[v]
            at = v * 16 + k
            if d == 0:
                lower, upper = before[v], after[v]
            elif d == 1:
                lower = jnp.where(rows == 0, beyond(low, at), roll(cell, 1, 0))
                upper = jnp.where(rows == 7, beyond(high, at), roll(cell, 7, 0))
            else:
                lower = jnp.where(lanes == 0, roll(left, -at, 1), roll(cell, 1, 1))
                upper = jnp.where(lanes == 127, roll(right, 127 - at, 1), roll(cell, 127, 1))
            mixed.append(high_a * upper - low_a * lower + own_a * cell)
            total[v] = total[v] + (high_b * upper + low_b * lower)
        for u in range(NV):
            for v in range(NV):
                at = 25 * d + 5 * u + v
                total[u] = total[u] - jnp.broadcast_to(matrix[at : at + 1, :], (ROWS, 128)) * mixed[v]
    return total


def ghosts_of(ids, wanted, weight, coupling, field, across, ghost):
    for a in range(8):
        d = wanted[ids[1], a] >> 6
        for v in range(NV):
            ghost[v, a : a + 1, :] = across[d, v * 8 + a : v * 8 + a + 1, :]
        e = wanted[ids[1], 8 + a] >> 6
        ghost[NV, a : a + 1, :] = across[e, 40 + a : 41 + a, :]
    outlet = [field[v, PLANES - 1] for v in range(NV)]
    jump = ghost[NV] - pressure(weight, outlet)
    return [ghost[v] for v in range(NV)], [outlet[v] + coupling[v] * jump for v in range(NV)]


def ends_of(step, ids, wanted, weight, coupling, field, coef, matrix, across, around, low, high, ghost):
    lanes = lanes_of((ROWS, 128))
    left, right = sides(step, ids, around)
    inlet_ghost, outlet_ghost = ghosts_of(ids, wanted, weight, coupling, field, across, ghost)
    plane = lambda k: [field[v, k] for v in range(NV)]
    new_inlet = advance(0, inlet_ghost, plane(0), plane(1), coef, matrix, left, right, low, high)
    last = PLANES - 1
    new_outlet = advance(last, plane(last - 1), plane(last), outlet_ghost, coef, matrix, left, right, low, high)
    return new_inlet, new_outlet


def ends_kernel(step, ids, wanted, weight, coupling, field, coef, matrix, across, around, first_swap, second_swap, ends, beside, ghost, low, high):
    settle(ids, first_swap, second_swap, low, high)
    new_inlet, new_outlet = ends_of(step, ids, wanted, weight, coupling, field, coef, matrix, across, around, low, high, ghost)
    for v in range(NV):
        ends[0, v] = new_inlet[v]
        ends[1, v] = new_outlet[v]
        beside[v] = new_outlet[v]
    beside[NV] = pressure(weight, new_inlet)


def bulk_kernel(step, ids, field, coef, matrix, around, from_first, from_second, ends, new, edges, first_swap, second_swap, low, high):
    settle(ids, from_first, from_second, low, high)
    even = lax.rem(ids[2], 2) == 0
    lanes = lanes_of((ROWS, 128))
    left, right = sides(step, ids, around)

    def note(k, total, last, first):
        for v in range(NV):
            new[v, k] = total[v]
            at = v * 16 + k
            first_swap[pl.ds(at, 1), :] = jnp.where(even, total[v][7:8], total[v][0:1])
            second_swap[pl.ds(at, 1), :] = jnp.where(even, total[v][0:1], total[v][7:8])
            spot = lanes == at
            last = jnp.where(spot, roll(total[v], at + 1, 1), last)
            first = jnp.where(spot, roll(total[v], at, 1), first)
        return last, first

    def one(k, carry):
        before, here, last, first = carry
        after = [field[v, k + 1] for v in range(NV)]
        total = advance(k, before, here, after, coef, matrix, left, right, low, high)
        last, first = note(k, total, last, first)
        return here, after, last, first

    zero = jnp.zeros((ROWS, 128), jnp.float32)
    last, first = note(0, [ends[0, v] for v in range(NV)], zero, zero)
    last, first = note(PLANES - 1, [ends[1, v] for v in range(NV)], last, first)
    carry = ([field[v, 0] for v in range(NV)], [field[v, 1] for v in range(NV)], last, first)
    _, _, last, first = lax.fori_loop(1, PLANES - 1, one, carry, unroll=7)
    edges[0] = last
    edges[1] = first


def last_kernel(step, ids, wanted, weight, coupling, field, coef, matrix, across, around, first_swap, second_swap, new, ghost, low, high):
    settle(ids, first_swap, second_swap, low, high)
    lanes = lanes_of((ROWS, 128))
    left, right = sides(step, ids, around)
    new_inlet, new_outlet = ends_of(step, ids, wanted, weight, coupling, field, coef, matrix, across, around, low, high, ghost)
    for v in range(NV):
        new[v, 0] = new_inlet[v]
        new[v, PLANES - 1] = new_outlet[v]

    def one(k, carry):
        before, here = carry
        after = [field[v, k + 1] for v in range(NV)]
        total = advance(k, before, here, after, coef, matrix, left, right, low, high)
        for v in range(NV):
            new[v, k] = total[v]
        return here, after

    carry = ([field[v, 0] for v in range(NV)], [field[v, 1] for v in range(NV)])
    lax.fori_loop(1, PLANES - 1, one, carry, unroll=7)


def body(
    state,
    volume,
    face_axial,
    face_radial,
    face_circum,
    viscosity,
    flux_matrix,
    inflow_plane,
    outflow_plane,
    down_donors,
    up_donors,
    pressure_weight,
    boundary_coupling,
):
    sections, row_size, rad_size = lax.axis_size("sec"), lax.axis_size("row"), lax.axis_size("rad")
    ids = jnp.stack(
        [
            lax.axis_index("sec"),
            lax.axis_index("row"),
            lax.axis_index("rad"),
            jnp.int32(rad_size),
            jnp.int32(sections),
            jnp.int32(row_size),
        ]
    ).astype(jnp.int32)
    own = [state[:, 0], volume[0], face_axial[0], face_radial[0], face_circum[0], viscosity[0]]
    matrix = jnp.broadcast_to(jnp.pad(flux_matrix[0].reshape(75), (0, 5))[:, None], (80, 128))
    extended = (NV, PLANES, ROWS, 128)
    strips = (2, ROWS, 128)
    sent = (FIELD_ROWS + 32, 128)
    scalars = [pressure_weight, boundary_coupling]

    beside, out_pressure, lists, first_swap, second_swap = call(
        first_kernel,
        [(NV + 1, 8, 128), (8, 128), (row_size, 16, 128), sent, sent],
        [ids, pressure_weight, down_donors[0], up_donors[0]],
        [],
        far=[own[0], own[3], own[4], own[5], outflow_plane],
    )

    def swaps(size, begin):
        return [pair for i in range(begin, size - 1, 2) for pair in ((i, i + 1), (i + 1, i))]

    table = lax.all_to_all(lists, "row", 0, 0)
    wanted = table[:, 0, :16].astype(jnp.int32)
    field = own[0]
    coef = edges = None
    for step in range(STEPS):
        last_step = step == STEPS - 1
        one_way = lax.ppermute(beside, "sec", swaps(sections, 0))
        other_way = lax.ppermute(beside, "sec", swaps(sections, 1))
        (send,) = call(
            gather_kernel,
            [(rad_size, TILE_ROWS, 128)],
            [ids],
            [one_way, other_way, inflow_plane, out_pressure, edges if step else beside],
        )
        got = lax.all_to_all(send, "rad", 0, 0)
        high = lax.ppermute(second_swap, "rad", swaps(rad_size, 1))
        low = lax.ppermute(first_swap, "rad", swaps(rad_size, 0))
        strip = [pltpu.VMEM(low.shape, jnp.float32)] * 2
        if step == 0:
            (coef,) = call(coef_kernel, [(13, PLANES, ROWS, 128)], [ids], own[1:] + [table, low, high], scratch=strip)
        (send,) = call(
            functools.partial(select_kernel, step),
            [(row_size, TILE_ROWS + (ROWS if step else 0), 128)],
            [ids, wanted],
            [got, edges] if step else [got],
        )
        across = lax.all_to_all(send, "row", 0, 0)
        around = across if step else table
        ghost = [pltpu.VMEM((NV + 1, ROWS, 128), jnp.float32)]
        if last_step:
            (field,) = call(
                functools.partial(last_kernel, step),
                [(NV, PLANES, 8, 128)],
                [ids, wanted] + scalars,
                [field, coef, matrix, across, around, low, high],
                flops=PLANES * ROWS * 128 * 300,
                scratch=ghost + strip,
            )
        else:
            ends, beside = call(
                functools.partial(ends_kernel, step),
                [(2, NV, ROWS, 128), (NV + 1, 8, 128)],
                [ids, wanted] + scalars,
                [field, coef, matrix, across, around, low, high],
                flops=2 * ROWS * 128 * 300,
                scratch=ghost + strip,
            )
            field, edges, first_swap, second_swap = call(
                functools.partial(bulk_kernel, step),
                [extended, strips, (FIELD_ROWS, 128), (FIELD_ROWS, 128)],
                [ids],
                [field, coef, matrix, around, low, high, ends],
                scratch=strip,
                flops=PLANES * ROWS * 128 * 300,
            )
    return field[:, None]


def solution(mesh):
    in_specs = (
        P(None, "sec", None, "rad", "row"),
        P("sec", None, "rad", "row"),
        P("sec", None, "rad", "row"),
        P("sec", None, "rad", "row"),
        P("sec", None, "rad", "row"),
        P("sec", None, "rad", "row"),
        P("sec", None, None, None),
        P(None, "rad", "row"),
        P(None, "rad", "row"),
        P("sec", ("row", "rad")),
        P("sec", ("row", "rad")),
        P(),
        P(),
    )
    out_specs = P(None, "sec", None, "rad", "row")

    return jax.shard_map(body, mesh=mesh, in_specs=in_specs, out_specs=out_specs, check_vma=False)
```
